32 devices in a mesh: gz: 4 (over x, core), gy: 8 (over z, y).
Axes of the slice: x: 2, y: 2, z: 4, core: 2. Of those that a mesh axis runs over, the one named last changes fastest.
Arguments:
- distance: float32 [256, 128, 1024], P('gz', 'gy'), may hold values from 0 to 2
- parent: int32 [256, 128, 1024], P('gz', 'gy'), may hold values from 0 to 4095, as said below
- removed: int32 [4096], replicated, may hold values from 0 to 1
- occupied: int32 [256, 128, 1024], P('gz', 'gy'), may hold values 0 or 1
Outputs:
- lowered: float32 [256, 128, 1024], P('gz', 'gy')
- cleared_share: float32 [], replicated
The draws below stay inside these ranges and needn't reach their ends.
Inputs may be any that keep to these rules, and one draw needn't show every extreme that they name: `parent`: an obstacle id.
All inputs are finite; a program needn't handle non-finite values. No bound on the sum of `occupied` on one device may be relied on, other than what follows from the above.
Results may differ from the reference program's by a relative error of at most 0.0003.
Values sent between devices are 32-bit elements; how exact they have to be, the bound alone decides.
No kernel may reach another device: no remote copies, remote signals or barrier semaphores. Data moves between devices by JAX's collectives and lax.ppermute only.
A program may use at most 64 MiB of HBM per device.

```python
import jax
import jax.numpy as jnp
from jax import lax

OBJS = 4096
NZ = 256
NY = 128
NX = 1024


def draw_parent(key, part):
    zcoord = lax.broadcasted_iota(jnp.int32, (NZ, NY, NX), 0)
    ycoord = lax.broadcasted_iota(jnp.int32, (NZ, NY, NX), 1)
    half = OBJS // 2
    base = (zcoord * NY + ycoord * NZ) * half // (2 * NZ * NY)
    return (base + jax.random.randint(key, (NZ, NY, NX), 0, half, dtype=jnp.int32)).astype(jnp.int32)


def draw_removed(key, part):
    ident = lax.iota(jnp.int32, OBJS)
    level = 30 * ident // OBJS
    rolled = jax.random.randint(key, (OBJS,), 0, 1000, dtype=jnp.int32)
    return (rolled < 30 + level * level).astype(jnp.int32)


def place_ends(array, rng, smallest, top_value):
    longest = array.shape.index(max(array.shape))
    spots = []
    for shift in (0, 1):
        where = [jax.random.randint(jax.random.fold_in(rng, axis), (), 0, length) for axis, length in enumerate(array.shape)]
        where[longest] = (where[longest] + shift) % array.shape[longest]
        spots.append(tuple(where))
    return array.at[spots[0]].set(smallest).at[spots[1]].set(top_value)


def level_of(stream_key, shape, split, smallest, high):
    factor_of, own = 1.0, jax.random.fold_in(stream_key, 6)
    for axis_at, shards_of in split:
        heights = jnp.exp(jax.random.uniform(jax.random.fold_in(own, axis_at), (shards_of,), jnp.float32, smallest / len(split), high / len(split)))
        factor_of = factor_of * jnp.repeat(heights, shape[axis_at] // shards_of).reshape([-1 if axis == axis_at else 1 for axis in range(len(shape))])
    return factor_of


def setup_inputs(seed: int = 0) -> dict:
    keys = jax.random.split(jax.random.key(seed), 5)
    return {
        "distance": jnp.clip(2.0 * jax.random.uniform(keys[0], (NZ, NY, NX), jnp.float32) ** level_of(keys[0], (NZ, NY, NX), ((0, 4), (1, 8)), -0.2, 0.2), 0.0, 2.0),
        "parent": draw_parent(jax.random.fold_in(keys[4], 71), 0),
        "removed": draw_removed(jax.random.fold_in(keys[4], 71), 0),
        "occupied": place_ends((jax.random.randint(keys[3], (NZ, NY, NX), 0, 16) < 1).astype(jnp.int32), jax.random.fold_in(keys[3], 1), 0, 1),
    }


FAR = 1.0e6
VOXEL = 0.1
TRUNC = 2.0


def sweep(field):
    far_plane = jnp.full((1,) + field.shape[1:], FAR, field.dtype)
    zpad = jnp.concatenate([far_plane, field, far_plane], 0)
    nearest = jnp.minimum(zpad[2:], zpad[:-2])
    ypad = jnp.concatenate([field[:, -1:], field, field[:, :1]], 1)
    nearest = jnp.minimum(nearest, jnp.minimum(ypad[:, 2:], ypad[:, :-2]))
    far_col = jnp.full(field.shape[:2] + (1,), FAR, field.dtype)
    right = jnp.concatenate([field[:, :, 1:], far_col], 2)
    left = jnp.concatenate([far_col, field[:, :, :-1]], 2)
    nearest = jnp.minimum(nearest, jnp.minimum(left, right))
    return jnp.minimum(field, nearest + VOXEL)


def reference(distance, parent, removed, occupied):
    flagged = jnp.take(removed, parent.astype(jnp.int32), axis=0)
    cleared = ((flagged == 1) & (occupied == 0)).astype(jnp.int32)
    raised = jnp.where(occupied == 1, jnp.zeros_like(distance), jnp.where(cleared == 1, jnp.full_like(distance, TRUNC), distance))
    lowered = sweep(sweep(raised))
    count = jnp.sum(cleared)
    total = distance.shape[0] * distance.shape[1] * distance.shape[2]
    share = count.astype(jnp.float32) * jnp.float32(100.0 / total)
    return lowered, share
```

```python
import functools

import jax
import jax.numpy as jnp
from jax import lax
from jax.experimental import pallas as pl
from jax.experimental.pallas import tpu as pltpu
from jax.sharding import PartitionSpec as P

FAR = 1000000.0
VOXEL = 0.1
TRUNC = 2.0
LANES = 128
SUBLANES = 8
CHUNK = 8

ANY = pl.BlockSpec(memory_space=pl.ANY)
VMEM = pl.BlockSpec(memory_space=pltpu.VMEM)
SMEM = pl.BlockSpec(memory_space=pltpu.SMEM)


def packed_table(flags_ref):
    groups = flags_ref.shape[0]
    bits = (flags_ref[...] == 1).astype(jnp.int32)
    bits = bits << lax.broadcasted_iota(jnp.int32, bits.shape, 0)
    words = jnp.sum(bits, axis=0, keepdims=True)
    return jnp.broadcast_to(words, (SUBLANES, LANES))


def raise_tile(words, dist, par, occ):
    word = jnp.take_along_axis(words, par & (LANES - 1), axis=1)
    cleared = (word >> (par >> 7)) & (occ ^ 1)
    raised = jnp.where(occ == 1, 0.0, jnp.where(cleared == 1, TRUNC, dist))
    return raised, cleared


def faces_kernel(dist, par, flags, occ, ylo, yhi, zlo, zhi, ybuf, zbuf, ysem, zsem):
    depth, rows, cols = dist.shape
    copies = []
    for side, row in enumerate((0, rows - 1)):
        for which, src in enumerate((dist, par, occ)):
            buf = (ybuf[0], ybuf[1], ybuf[2])[which]
            cp = pltpu.make_async_copy(src.at[:, row, :], buf.at[side], ysem.at[side, which])
            cp.start()
            copies.append(cp)
    zcopies = []
    for side, first in enumerate((0, depth - 2)):
        for which, src in enumerate((dist, par, occ)):
            buf = (zbuf[0], zbuf[1], zbuf[2])[which]
            cp = pltpu.make_async_copy(src.at[pl.ds(first, 2)], buf.at[side], zsem.at[side, which])
            cp.start()
            zcopies.append(cp)
    words = packed_table(flags)
    for side, out in enumerate((ylo, yhi)):
        for cp in copies[3 * side : 3 * side + 3]:
            cp.wait()

        def body(step, _, side=side, out=out):
            at = pl.ds(pl.multiple_of(step * SUBLANES, SUBLANES), SUBLANES)
            for lane in range(0, cols, LANES):
                x = pl.ds(lane, LANES)
                tile, _ = raise_tile(
                    words, ybuf[0][side, at, x], ybuf[1][side, at, x], ybuf[2][side, at, x]
                )
                out[at, x] = tile
            return 0

        lax.fori_loop(0, depth // SUBLANES, body, 0)
    for side, out in enumerate((zlo, zhi)):
        for cp in zcopies[3 * side : 3 * side + 3]:
            cp.wait()
        for plane in range(2):
            for y in range(0, rows, SUBLANES):
                for lane in range(0, cols, LANES):
                    at = (side, plane, pl.ds(y, SUBLANES), pl.ds(lane, LANES))
                    tile, _ = raise_tile(words, zbuf[0][at], zbuf[1][at], zbuf[2][at])
                    out[at[1:]] = tile


def faces(dist, par, flags, occ):
    depth, rows, cols = dist.shape
    yface = jax.ShapeDtypeStruct((depth, cols), jnp.float32)
    zface = jax.ShapeDtypeStruct((2, rows, cols), jnp.float32)
    types = (jnp.float32, jnp.int32, jnp.int32)
    return pl.pallas_call(
        faces_kernel,
        name="faces",
        out_shape=(yface, yface, zface, zface),
        in_specs=[ANY, ANY, VMEM, ANY],
        out_specs=(VMEM,) * 4,
        scratch_shapes=[
            [pltpu.VMEM((2, depth, cols), t) for t in types],
            [pltpu.VMEM((2, 2, rows, cols), t) for t in types],
            pltpu.SemaphoreType.DMA((2, 3)),
            pltpu.SemaphoreType.DMA((2, 3)),
        ],
        cost_estimate=pl.CostEstimate(flops=0, bytes_accessed=4 * 2**20, transcendentals=0),
    )(dist, par, flags, occ)


def raise_kernel(dist, par, flags, occ, field, count, words, total):
    step = pl.program_id(0)
    depth, rows, cols = dist.shape

    @pl.when(step == 0)
    def _():
        words[...] = packed_table(flags)
        total[...] = jnp.zeros_like(total)

    table = words[...]

    def body(z, acc):
        for y in range(0, rows, SUBLANES):
            for lane in range(0, cols, LANES):
                at = (z, pl.ds(y, SUBLANES), pl.ds(lane, LANES))
                tile, cleared = raise_tile(table, dist[at], par[at], occ[at])
                field[(step * depth + z, *at[1:])] = tile
                acc = acc + cleared
        return acc

    total[...] = lax.fori_loop(0, depth, body, total[...])

    @pl.when(step == pl.num_programs(0) - 1)
    def _():
        count[0, 0] = jnp.sum(total[...])


def raise_all(dist, par, flags, occ):
    depth, rows, cols = dist.shape
    block = pl.BlockSpec((CHUNK, rows, cols), lambda i: (i, 0, 0))
    return pl.pallas_call(
        raise_kernel,
        name="raise_all",
        out_shape=(
            jax.ShapeDtypeStruct(dist.shape, jnp.float32),
            jax.ShapeDtypeStruct((1, 1), jnp.int32),
        ),
        grid=(depth // CHUNK,),
        in_specs=[block, block, VMEM, block],
        out_specs=(VMEM, SMEM),
        scratch_shapes=[
            pltpu.VMEM((SUBLANES, LANES), jnp.int32),
            pltpu.VMEM((SUBLANES, LANES), jnp.int32),
        ],
        cost_estimate=pl.CostEstimate(flops=0, bytes_accessed=16 * 2**20, transcendentals=0),
    )(dist, par, flags, occ)


def swept_plane(below, center, above):
    rows, cols = center.shape
    y = lax.broadcasted_iota(jnp.int32, center.shape, 0)
    x = lax.broadcasted_iota(jnp.int32, center.shape, 1)
    nearest = jnp.minimum(below, above)
    nearest = jnp.minimum(nearest, jnp.where(y == 0, FAR, pltpu.roll(center, 1, 0)))
    nearest = jnp.minimum(nearest, jnp.where(y == rows - 1, FAR, pltpu.roll(center, rows - 1, 0)))
    nearest = jnp.minimum(nearest, jnp.where(x == 0, FAR, pltpu.roll(center, 1, 1)))
    nearest = jnp.minimum(nearest, jnp.where(x == cols - 1, FAR, pltpu.roll(center, cols - 1, 1)))
    return jnp.minimum(center, nearest + VOXEL)


def sweep_kernel(ends, field, zlow, zhigh, out, tlo, thi, edges, once):
    step = pl.program_id(0)
    last = pl.num_programs(0) - 1
    depth, rows, cols = field.shape
    chunk = out.shape[0]
    no_low, no_high = ends[0] == 1, ends[1] == 1

    def low(plane):
        return jnp.where(no_low, FAR, zlow[plane])

    def high(plane):
        return jnp.where(no_high, FAR, zhigh[plane])

    def keep(z, plane):
        once[z + 1] = plane

    def keep_face(z, plane):
        keep(z, plane)
        tlo[pl.ds(z, 1), :] = plane[:1]
        thi[pl.ds(z, 1), :] = plane[rows - 1 :]

    @pl.when(step == 0)
    def _():
        keep(-1, jnp.where(no_low, FAR, swept_plane(low(0), low(1), field[0])))
        keep_face(0, swept_plane(low(1), field[0], field[1]))

    def finish(z):
        plane = swept_plane(once[z], once[z + 1], once[z + 2])
        out[z - step * chunk] = plane
        for at, row in enumerate((0, 1, rows - 2, rows - 1)):
            edges[at, pl.ds(z, 1), :] = plane[row : row + 1]

    def body(z, _):
        keep_face(z + 1, swept_plane(field[z], field[z + 1], field[z + 2]))
        finish(z)
        return 0

    first = step * chunk

    @pl.when(step < last)
    def _():
        lax.fori_loop(first, first + chunk, body, 0)

    @pl.when(step == last)
    def _():
        lax.fori_loop(first, first + chunk - 2, body, 0)
        end = depth - 1
        keep_face(end, swept_plane(field[end - 1], field[end], high(0)))
        finish(end - 1)
        keep(depth, jnp.where(no_high, FAR, swept_plane(field[end], high(0), high(1))))
        finish(end)


def sweep_both(ends, field, zlow, zhigh):
    depth, rows, cols = field.shape
    face = jax.ShapeDtypeStruct((depth, cols), jnp.float32)
    return pl.pallas_call(
        sweep_kernel,
        name="sweep_both",
        out_shape=(
            jax.ShapeDtypeStruct(field.shape, jnp.float32),
            face,
            face,
            jax.ShapeDtypeStruct((4, depth, cols), jnp.float32),
        ),
        grid=(depth // CHUNK,),
        in_specs=[SMEM, VMEM, VMEM, VMEM],
        out_specs=(pl.BlockSpec((CHUNK, rows, cols), lambda i: (i, 0, 0)), VMEM, VMEM, VMEM),
        scratch_shapes=[pltpu.VMEM((depth + 2, rows, cols), jnp.float32)],
        cost_estimate=pl.CostEstimate(flops=0, bytes_accessed=16 * 2**20, transcendentals=0),
    )(ends, field, zlow, zhigh)


def patch_kernel(rows, hops, edges, low, high, _, out, buf, sem):
    copies = []
    for side, (row, offer) in enumerate(zip(rows, (low, high))):
        at = row if row < 2 else row - out.shape[1] + 4
        reach = offer[...]
        for _ in range(hops):
            reach = reach + VOXEL
        buf[side] = jnp.minimum(edges[at], reach)
        cp = pltpu.make_async_copy(buf.at[side], out.at[:, row, :], sem.at[side])
        cp.start()
        copies.append(cp)
    for cp in copies:
        cp.wait()


def patch(out, edges, low, high, inset, hops):
    depth, count, cols = out.shape
    return pl.pallas_call(
        functools.partial(patch_kernel, (inset, count - 1 - inset), hops),
        name=f"patch{inset}",
        out_shape=jax.ShapeDtypeStruct(out.shape, out.dtype),
        in_specs=[VMEM, VMEM, VMEM, ANY],
        out_specs=ANY,
        input_output_aliases={3: 0},
        scratch_shapes=[pltpu.VMEM((2, depth, cols), jnp.float32), pltpu.SemaphoreType.DMA((2,))],
        cost_estimate=pl.CostEstimate(flops=0, bytes_accessed=2 * 2**20, transcendentals=0),
    )(edges, low, high, out)


def shifted(value, axis, by, periodic):
    count = lax.axis_size(axis)
    pairs = [(i, (i + by) % count) for i in range(count) if periodic or 0 <= i + by < count]
    return lax.ppermute(value, axis, pairs)


def summed(value, axes):
    for axis in axes:
        count = lax.axis_size(axis)
        if count & (count - 1):
            value = lax.psum(value, axis)
            continue
        step = count // 2
        while step:
            value = value + lax.ppermute(value, axis, [(i, i ^ step) for i in range(count)])
            step //= 2
    return value


def on_device(distance, parent, removed, occupied):
    flags = removed.reshape(-1, LANES)
    slab = lax.axis_index("gz")
    ends = jnp.stack([slab == 0, slab == lax.axis_size("gz") - 1]).astype(jnp.int32)

    ylo, yhi, zlo, zhi = faces(distance, parent, flags, occupied)
    low = shifted(yhi, "gy", 1, True)
    high = shifted(ylo, "gy", -1, True)
    zlow = shifted(zhi, "gz", 1, False)
    zhigh = shifted(zlo, "gz", -1, False)
    field, cleared = raise_all(distance, parent, flags, occupied)
    lowered, tlo, thi, edges = sweep_both(ends, field, zlow, zhigh)
    tlow = shifted(thi, "gy", 1, True)
    thigh = shifted(tlo, "gy", -1, True)
    lowered = patch(lowered, edges, low, high, 1, 2)
    lowered = patch(lowered, edges, tlow, thigh, 0, 1)

    count = summed(cleared, ("gz", "gy"))[0, 0]
    total = distance.size * lax.axis_size("gz") * lax.axis_size("gy")
    share = count.astype(jnp.float32) * jnp.float32(100.0 / total)
    return (lowered, share)


def solution(mesh):
    placed = (P("gz", "gy", None), P("gz", "gy", None), P(), P("gz", "gy", None))
    return jax.shard_map(
        on_device, mesh=mesh, in_specs=placed, out_specs=(P("gz", "gy", None), P()), check_vma=False
    )
```

```python
import functools

import jax
import jax.numpy as jnp
from jax import lax
from jax.experimental import pallas as pl
from jax.experimental.pallas import tpu as pltpu
from jax.sharding import PartitionSpec as P


FAR = 1000000.0
VOXEL = 0.1
TRUNC = 2.0
LANES = 128
SUBLANES = 8
CHUNK = 8
MIB = 2**20

HBM = pl.BlockSpec(memory_space=pltpu.HBM)
VMEM = pl.BlockSpec(memory_space=pltpu.VMEM)

COUNT_BITS = 12


def params(mib):
    return pltpu.CompilerParams(vmem_limit_bytes=mib * MIB)


def cost(mib):
    return pl.CostEstimate(flops=0, bytes_accessed=mib * MIB, transcendentals=0)


def packed_table(flags_ref):
    bits = (flags_ref[...] == 1).astype(jnp.int32)
    bits = bits << lax.broadcasted_iota(jnp.int32, bits.shape, 0)
    words = jnp.sum(bits, axis=0, keepdims=True)
    return jnp.broadcast_to(words, (SUBLANES, LANES))


def raise_tile(words, dist, par, occ):
    lane = par & (LANES - 1)
    word = jnp.take_along_axis(words, lane, axis=1, mode="promise_in_bounds")
    cleared = (word >> (par >> 7)) & (occ ^ 1)
    raised = jnp.where(occ == 1, 0.0, jnp.where(cleared == 1, TRUNC, dist))
    return raised, cleared


def swept_tiles(centers, others):
    lane = lax.broadcasted_iota(jnp.int32, (SUBLANES, LANES), 1)
    last = len(centers) - 1
    after = [pltpu.roll(c, 1, 1) for c in centers]
    before = [pltpu.roll(c, LANES - 1, 1) for c in centers]
    swept = []
    for i, center in enumerate(centers):
        left = jnp.where(lane == 0, after[i - 1] if i else FAR, after[i])
        right = jnp.where(lane == LANES - 1, before[i + 1] if i < last else FAR, before[i])
        nearest = jnp.minimum(left, right)
        for other in others[i]:
            nearest = jnp.minimum(nearest, other)
        swept.append(jnp.minimum(center, nearest + VOXEL))
    return swept


def padded_rows(rows, cols):
    return cols // LANES * (rows + SUBLANES) + SUBLANES


def row_of(column, row, rows):
    return column * (rows + SUBLANES) + SUBLANES + row


def fill_pads(ref, at, rows, cols):
    for column in range(cols // LANES + 1):
        first = row_of(column, -SUBLANES, rows)
        ref[(*at, pl.ds(first, SUBLANES), slice(None))] = jnp.full((SUBLANES, LANES), FAR)


def swept_plane(read, rows, cols, y):
    columns = range(cols // LANES)
    firsts = [row_of(c, y, rows) for c in columns]
    centers = [read(0, f) for f in firsts]
    others = [[t for t in (read(-1, f), read(1, f), read(0, f - 1), read(0, f + 1)) if t is not None] for f in firsts]
    return swept_tiles(centers, others)


def faces_kernel(dist, par, flags_at, occ, low, high, flags, buf, near, fsem, ysem):
    depth, rows, cols = dist.shape
    columns = range(cols // LANES)
    table_in = pltpu.make_async_copy(flags_at, flags, fsem)
    table_in.start()
    copies = {}
    for side in range(2):
        for away in range(2):
            row = (away, rows - 1 - away)[side]
            for which, src in enumerate((dist, par, occ)):
                cp = pltpu.make_async_copy(
                    src.at[:, row, :], buf[which].at[side, away], ysem.at[side, away, which]
                )
                cp.start()
                copies[side, away, which] = cp
    fill_pads(near, (), depth, cols)
    table_in.wait()
    words = packed_table(flags)
    for side, out in enumerate((low, high)):
        for key, cp in copies.items():
            if key[0] == side:
                cp.wait()

        def lift(step, _, side=side, out=out):
            z = pl.multiple_of(step * SUBLANES, SUBLANES)
            at = pl.ds(z, SUBLANES)
            for column in columns:
                x = pl.ds(column * LANES, LANES)
                tile, _ = raise_tile(words, *(buf[w][side, 0, at, x] for w in range(3)))
                out[0, at, x] = tile
                near[pl.ds(row_of(column, z, depth), SUBLANES), :] = tile
                tile, _ = raise_tile(words, *(buf[w][side, 1, at, x] for w in range(3)))
                out[1, at, x] = tile
            return 0

        lax.fori_loop(0, depth // SUBLANES, lift, 0)

        for z in range(0, depth, SUBLANES):
            at = pl.ds(z, SUBLANES)
            xs = [pl.ds(c * LANES, LANES) for c in columns]

            def read(first):
                return near[pl.ds(first, SUBLANES), :]

            firsts = [row_of(c, z, depth) for c in columns]
            others = [(read(f - 1), read(f + 1), out[1, at, x]) for f, x in zip(firsts, xs)]
            for x, tile in zip(xs, swept_tiles([read(f) for f in firsts], others)):
                out[1, at, x] = tile


def faces(dist, par, flags, occ):
    depth, _, cols = dist.shape
    face = jax.ShapeDtypeStruct((2, depth, cols), jnp.float32)
    return pl.pallas_call(
        faces_kernel,
        name="faces",
        out_shape=(face, face),
        in_specs=[HBM] * 4,
        out_specs=(VMEM,) * 2,
        scratch_shapes=[
            pltpu.VMEM(flags.shape, jnp.int32),
            [pltpu.VMEM((2, 2, depth, cols), t) for t in (jnp.float32, jnp.int32, jnp.int32)],
            pltpu.VMEM((padded_rows(depth, cols), LANES), jnp.float32),
            pltpu.SemaphoreType.DMA,
            pltpu.SemaphoreType.DMA((2, 2, 3)),
        ],
        compiler_params=params(16),
        cost_estimate=cost(4),
    )(dist, par, flags, occ)


def raise_kernel(dist, par, flags, occ, field, first, second, words, total, ends):
    step = pl.program_id(0)
    last = pl.num_programs(0) - 1
    chunk, rows, cols = dist.shape
    depth = field.shape[0]
    columns = range(cols // LANES)

    @pl.when(step == 0)
    def _():
        words[...] = packed_table(flags)
        total[...] = jnp.zeros_like(total)

    table = words[...]

    def body(pair, acc):
        for z in (pair * 2, pair * 2 + 1):
            fill_pads(field, (step * chunk + z,), rows, cols)
            for y in range(0, rows, SUBLANES):
                for column in columns:
                    at = (z, pl.ds(y, SUBLANES), pl.ds(column * LANES, LANES))
                    tile, cleared = raise_tile(table, dist[at], par[at], occ[at])
                    field[step * chunk + z, pl.ds(row_of(column, y, rows), SUBLANES), :] = tile
                    acc = acc + cleared
        return acc

    total[...] = lax.fori_loop(0, chunk // 2, body, total[...])

    def keep_end(side, z, inward):
        def read(dz, at):
            if dz and dz != inward:
                return None
            return field[z + dz, pl.ds(at, SUBLANES), :]

        for y in range(0, rows, SUBLANES):
            swept = swept_plane(read, rows, cols, y)
            for column in columns:
                x = pl.ds(column * LANES, LANES)
                ends[side, pl.ds(y, SUBLANES), x] = read(0, row_of(column, y, rows))
                ends[side, pl.ds(rows + y, SUBLANES), x] = swept[column]

    @pl.when(step == 0)
    def _():
        keep_end(0, 0, 1)

    @pl.when(step == last)
    def _():
        keep_end(1, depth - 1, -1)
        count = jnp.sum(total[...])
        row = lax.broadcasted_iota(jnp.int32, (SUBLANES, cols), 0)
        low = (count & (2**COUNT_BITS - 1)).astype(jnp.float32)
        high = (count >> COUNT_BITS).astype(jnp.float32)
        counts = jnp.where(row == 2, low, jnp.where(row == 3, high, 0.0))
        odd = lax.axis_index("gz") & 1
        for out, side in ((first, 1 - odd), (second, odd)):
            out[pl.ds(0, 2 * rows), :] = ends[side]
            out[pl.ds(2 * rows, SUBLANES), :] = counts


def raise_all(dist, par, flags, occ):
    depth, rows, cols = dist.shape
    block = pl.BlockSpec((CHUNK, rows, cols), lambda i: (i, 0, 0))
    message = jax.ShapeDtypeStruct((2 * rows + SUBLANES, cols), jnp.float32)
    return pl.pallas_call(
        raise_kernel,
        name="raise_all",
        out_shape=(
            jax.ShapeDtypeStruct((depth, padded_rows(rows, cols), LANES), jnp.float32),
            message,
            message,
        ),
        grid=(depth // CHUNK,),
        in_specs=[block, block, VMEM, block],
        out_specs=(VMEM, VMEM, VMEM),
        scratch_shapes=[
            pltpu.VMEM((SUBLANES, LANES), jnp.int32),
            pltpu.VMEM((SUBLANES, LANES), jnp.int32),
            pltpu.VMEM((2, 2 * rows, cols), jnp.float32),
        ],
        compiler_params=params(24),
        cost_estimate=cost(12),
    )(dist, par, flags, occ)


def sweep_kernel(start, depth, field, *refs):
    out, edges, once, slab = refs[-4:]
    step = pl.program_id(0)
    total = field.shape[0]
    chunk, rows, cols = out.shape
    columns = range(cols // LANES)
    base = start + step * chunk

    def sweep_once(z, below=True, above=True):
        def read(dz, at):
            if (dz < 0 and not below) or (dz > 0 and not above):
                return None
            return field[z + dz, pl.ds(at, SUBLANES), :]

        fill_pads(once, (z - start + 1,), rows, cols)
        for y in range(0, rows, SUBLANES):
            for column, tile in enumerate(swept_plane(read, rows, cols, y)):
                once[z - start + 1, pl.ds(row_of(column, y, rows), SUBLANES), :] = tile

    def sweep_twice(z):
        def read(dz, at):
            return once[z - start + 1 + dz, pl.ds(at, SUBLANES), :]

        for y in range(0, rows, SUBLANES):
            for column, tile in enumerate(swept_plane(read, rows, cols, y)):
                out[z - base, pl.ds(y, SUBLANES), pl.ds(column * LANES, LANES)] = tile
                at = (z - base) * (rows * len(columns)) + column * rows + y
                slab[pl.ds(pl.multiple_of(at, SUBLANES), SUBLANES), :] = tile

    def body(z, _):
        sweep_once(z + 1)
        sweep_twice(z)
        return 0

    @pl.when(step == 0)
    def _():
        if start:
            sweep_once(start - 1)
        else:
            once[0] = jnp.full(once.shape[1:], FAR)
        sweep_once(start, below=start > 0)

    at_end = start + depth == total
    finish = step == pl.num_programs(0) - 1

    if at_end:

        @pl.when(finish)
        def _():
            lax.fori_loop(base, base + chunk - 2, body, 0)
            sweep_once(total - 1, above=False)
            sweep_twice(total - 2)
            once[depth + 1] = jnp.full(once.shape[1:], FAR)
            sweep_twice(total - 1)

        @pl.when(jnp.logical_not(finish))
        def _():
            lax.fori_loop(base, base + chunk, body, 0)

    else:
        lax.fori_loop(base, base + chunk, body, 0)

    at = pl.ds(pl.multiple_of(step * chunk, SUBLANES), SUBLANES)
    for edge, row in enumerate((0, 1, rows - 2, rows - 1)):
        for column in columns:
            lines = pl.ds(column * rows + row, SUBLANES, stride=rows * len(columns))
            edges[edge, at, pl.ds(column * LANES, LANES)] = slab[lines, :]


def sweep_part(field, out, start, depth, rows, cols):
    total = field.shape[0]
    first = start // CHUNK
    return pl.pallas_call(
        functools.partial(sweep_kernel, start, depth),
        out_shape=(
            jax.ShapeDtypeStruct((total, rows, cols), jnp.float32),
            jax.ShapeDtypeStruct((4, depth, cols), jnp.float32),
        ),
        grid=(depth // CHUNK,),
        in_specs=[VMEM] + ([HBM] if start else []),
        out_specs=(pl.BlockSpec((CHUNK, rows, cols), lambda i: (i + first, 0, 0)), VMEM),
        scratch_shapes=[
            pltpu.VMEM((depth + 2, padded_rows(rows, cols), LANES), jnp.float32),
            pltpu.VMEM((CHUNK * rows * cols // LANES, LANES), jnp.float32),
        ],
        input_output_aliases={1: 0} if start else {},
        compiler_params=params(16),
        cost_estimate=cost(12),
    )(field, *([out] if start else []))


def patch_z_kernel(slabs, first, second, _, out, zedges, clow, chigh, planes, sem):
    depth, rows, cols = out.shape
    slab = lax.axis_index("gz")
    odd = slab & 1
    loads = []
    for side in range(2):
        z = (0, depth - 2)[side]
        cp = pltpu.make_async_copy(out.at[pl.ds(z, 2)], planes.at[side], sem.at[side])
        cp.start()
        loads.append(cp)
    stores = []
    for side in range(2):
        missing = slab == (0, slabs - 1)[side]
        got = jnp.where(odd != side, first[pl.ds(0, 2 * rows)], second[pl.ds(0, 2 * rows)])
        got = jnp.where(missing, FAR, got)
        raised, swept = got[:rows], got[rows:]
        near, far = (0, 1) if side == 0 else (1, 0)
        loads[side].wait()
        a = jnp.minimum(planes[side, near], swept + VOXEL)
        b = jnp.minimum(planes[side, far], raised + VOXEL + VOXEL)
        planes[side, near] = a
        planes[side, far] = b
        for edge, row in enumerate((0, 1, rows - 2, rows - 1)):
            zedges[edge, pl.ds(2 * side + near, 1), :] = a[row : row + 1]
            zedges[edge, pl.ds(2 * side + far, 1), :] = b[row : row + 1]
        clow[pl.ds(side, 1), :] = raised[:1]
        chigh[pl.ds(side, 1), :] = raised[rows - 1 :]
        z = (0, depth - 2)[side]
        cp = pltpu.make_async_copy(planes.at[side], out.at[pl.ds(z, 2)], sem.at[side])
        cp.start()
        stores.append(cp)
    for edge in range(4):
        zedges[edge, pl.ds(4, 4), :] = jnp.zeros((4, cols), jnp.float32)
    clow[pl.ds(2, 6), :] = jnp.zeros((6, cols), jnp.float32)
    chigh[pl.ds(2, 6), :] = jnp.zeros((6, cols), jnp.float32)
    for cp in stores:
        cp.wait()


def patch_z(first, second, out):
    _, rows, cols = out.shape
    corner = jax.ShapeDtypeStruct((SUBLANES, cols), jnp.float32)
    return pl.pallas_call(
        functools.partial(patch_z_kernel, lax.axis_size("gz")),
        name="patch_z",
        out_shape=(
            jax.ShapeDtypeStruct(out.shape, out.dtype),
            jax.ShapeDtypeStruct((4, SUBLANES, cols), jnp.float32),
            corner,
            corner,
        ),
        in_specs=[VMEM, VMEM, HBM],
        out_specs=(HBM, VMEM, VMEM, VMEM),
        input_output_aliases={2: 0},
        scratch_shapes=[
            pltpu.VMEM((2, 2, rows, cols), jnp.float32),
            pltpu.SemaphoreType.DMA((2,)),
        ],
        compiler_params=params(4),
        cost_estimate=cost(1),
    )(first, second, out)


def patch_y_kernel(scale, edge0, edge1, zedges, low, high, clow, chigh, counts, _, out, share, buf, sem):
    depth, rows, _ = out.shape
    half = edge0.shape[1]
    copies = []
    for side, (face, corner) in enumerate(((low, clow), (high, chigh))):
        for away in range(2):
            edge = (away, 3 - away)[side]
            row = (away, rows - 1 - away)[side]
            at = 2 * side + away
            reach = face[1 - away] + VOXEL
            if away:
                reach = reach + VOXEL
            buf[at, pl.ds(0, half), :] = jnp.minimum(edge0[edge], reach[:half])
            buf[at, pl.ds(half, depth - half), :] = jnp.minimum(edge1[edge], reach[half:])
            for end in range(2):
                for dz in range(2):
                    z = (0, depth - 2)[end] + dz
                    line = jnp.minimum(
                        zedges[edge, pl.ds(2 * end + dz, 1), :], buf[at, pl.ds(z, 1), :]
                    )
                    if not away and dz == end:
                        line = jnp.minimum(line, corner[pl.ds(end, 1), :] + VOXEL + VOXEL)
                    buf[at, pl.ds(z, 1), :] = line
            cp = pltpu.make_async_copy(buf.at[at], out.at[:, row, :], sem.at[at])
            cp.start()
            copies.append(cp)
    both = (counts[...] + clow[:, pl.ds(0, LANES)]).astype(jnp.int32)
    row = lax.broadcasted_iota(jnp.int32, both.shape, 0)
    both = jnp.where(row == 2, both, jnp.where(row == 3, both << COUNT_BITS, 0))
    count = jnp.sum(both, axis=0, keepdims=True)
    share[...] = count[:, :1].astype(jnp.float32) * jnp.float32(scale)
    for cp in copies:
        cp.wait()


def patch_y(scale, edge0, edge1, zedges, low, high, clow, chigh, counts, out):
    depth, _, cols = out.shape
    return pl.pallas_call(
        functools.partial(patch_y_kernel, scale),
        name="patch_y",
        out_shape=(
            jax.ShapeDtypeStruct(out.shape, out.dtype),
            jax.ShapeDtypeStruct((1, 1), jnp.float32),
        ),
        in_specs=[VMEM] * 8 + [HBM],
        out_specs=(HBM, VMEM),
        input_output_aliases={8: 0},
        scratch_shapes=[pltpu.VMEM((4, depth, cols), jnp.float32), pltpu.SemaphoreType.DMA((4,))],
        compiler_params=params(8),
        cost_estimate=cost(2),
    )(edge0, edge1, zedges, low, high, clow, chigh, counts, out)


def swapped(value, axis, partner):
    count = lax.axis_size(axis)
    return lax.ppermute(value, axis, [(i, partner(i) % count) for i in range(count)])


def shifted(value, axis, by):
    return swapped(value, axis, lambda i: i + by)


def on_device(distance, parent, removed, occupied):
    depth, rows, cols = distance.shape
    half = depth
    slabs, columns = lax.axis_size("gz"), lax.axis_size("gy")
    flags = removed.reshape(-1, LANES)
    distance, parent, occupied = (
        pltpu.with_memory_space_constraint(a, pltpu.HBM) for a in (distance, parent, occupied)
    )

    ylow, yhigh = faces(
        distance, parent, pltpu.with_memory_space_constraint(flags, pltpu.HBM), occupied
    )
    low = shifted(yhigh, "gy", 1)
    high = shifted(ylow, "gy", -1)

    field, first, second = raise_all(distance, parent, flags, occupied)
    got_first = swapped(first, "gz", lambda i: i ^ 1)
    lowered, edge0 = sweep_part(field, None, 0, half, rows, cols)
    got_first, edge0 = lax.optimization_barrier((got_first, edge0))
    second = second.at[2 * rows :].add(got_first[2 * rows :])
    got_second = swapped(second, "gz", lambda i: i - 1 + 2 * (i % 2))
    edge0, edge1 = edge0[:, :32], edge0[:, 32:]
    got_second, edge1 = lax.optimization_barrier((got_second, edge1))
    counts = (second[2 * rows :] + got_second[2 * rows :])[:, :LANES]
    lowered, zedges, clow, chigh = patch_z(got_first, got_second, lowered)
    step = columns // 2
    while step > 1:
        counts = counts + swapped(counts, "gy", lambda i: i ^ step)
        step //= 2
    clow = clow.at[:, :LANES].add(counts)
    chigh = chigh.at[:, :LANES].add(counts)
    from_low = shifted(chigh, "gy", 1)
    from_high = shifted(clow, "gy", -1)
    total = distance.size * slabs * columns
    lowered, share = patch_y(
        100.0 / total, edge0, edge1, zedges, low, high, from_low, from_high, counts, lowered
    )
    return (lowered, share[0, 0])


def solution(mesh):
    slabs, columns = mesh.shape["gz"], mesh.shape["gy"]
    if slabs != 4 or columns & (columns - 1):
        raise ValueError("unsupported mesh")
    placed = (P("gz", "gy", None), P("gz", "gy", None), P(), P("gz", "gy", None))
    return jax.shard_map(
        on_device, mesh=mesh, in_specs=placed, out_specs=(P("gz", "gy", None), P()), check_vma=False
    )
```

```python
import functools

import jax
import jax.numpy as jnp
from jax import lax
from jax.experimental import pallas as pl
from jax.experimental.pallas import tpu as pltpu
from jax.sharding import PartitionSpec as P


FAR = 1000000.0
VOXEL = 0.1
TRUNC = 2.0
LANES = 128
SUBLANES = 8
CHUNK = 8
RAISE_UNROLL = 4
SWEEP_UNROLL = 4
MIB = 2**20

HBM = pl.BlockSpec(memory_space=pltpu.HBM)
VMEM = pl.BlockSpec(memory_space=pltpu.VMEM)

COUNT_BITS = 12


def params(mib):
    return pltpu.CompilerParams(vmem_limit_bytes=mib * MIB)


def cost(mib):
    return pl.CostEstimate(flops=0, bytes_accessed=mib * MIB, transcendentals=0)


def packed_table(flags_ref):
    bits = (flags_ref[...] == 1).astype(jnp.int32)
    bits = bits << lax.broadcasted_iota(jnp.int32, bits.shape, 0)
    words = jnp.sum(bits, axis=0, keepdims=True)
    return jnp.broadcast_to(words, (SUBLANES, LANES))


PICK = lax.GatherDimensionNumbers(
    offset_dims=(),
    collapsed_slice_dims=(1,),
    start_index_map=(1,),
    operand_batching_dims=(0,),
    start_indices_batching_dims=(0,),
)


def raise_tile(words, dist, par, occ):
    lane = par & (LANES - 1)
    word = lax.gather(words, lane[..., None], PICK, (1, 1), mode="promise_in_bounds")
    cleared = (word >> (par >> 7)) & (occ ^ 1)
    raised = jnp.where(occ == 1, 0.0, jnp.where(cleared == 1, TRUNC, dist))
    return raised, cleared


def swept_tiles(centers, others):
    lane = lax.broadcasted_iota(jnp.int32, (SUBLANES, LANES), 1)
    last = len(centers) - 1
    after = [pltpu.roll(c, 1, 1) for c in centers]
    before = [pltpu.roll(c, LANES - 1, 1) for c in centers]
    swept = []
    for i, center in enumerate(centers):
        left = jnp.where(lane == 0, after[i - 1] if i else FAR, after[i])
        right = jnp.where(lane == LANES - 1, before[i + 1] if i < last else FAR, before[i])
        nearest = jnp.minimum(left, right)
        for other in others[i]:
            nearest = jnp.minimum(nearest, other)
        swept.append(jnp.minimum(center, nearest + VOXEL))
    return swept


def padded_rows(rows, cols):
    return cols // LANES * (rows + SUBLANES) + SUBLANES


def row_of(column, row, rows):
    return column * (rows + SUBLANES) + SUBLANES + row


def fill_pads(ref, at, rows, cols):
    for column in range(cols // LANES + 1):
        first = row_of(column, -SUBLANES, rows)
        ref[(*at, pl.ds(first, SUBLANES), slice(None))] = jnp.full((SUBLANES, LANES), FAR)


def swept_plane(read, rows, cols, y, beside=(-1, 1)):
    firsts = [row_of(c, y, rows) for c in range(cols // LANES)]
    centers = [read(0, f) for f in firsts]
    others = [[read(dz, f) for dz in beside] + [read(0, f - 1), read(0, f + 1)] for f in firsts]
    return swept_tiles(centers, others)


def faces_kernel(rows, cols, field, low, high):
    planes, height, _ = field.shape
    lines = field.reshape(planes * height, LANES)
    columns = range(cols // LANES)

    def body(group, _):
        z = pl.multiple_of(group * SUBLANES, SUBLANES)
        at = pl.ds(z, SUBLANES)
        for out, row, inward in ((low, 0, 1), (high, rows - 1, rows - 2)):

            def read(column, y, dz=0):
                first = (z + 1 + dz) * height + row_of(column, y, rows)
                return lines[pl.ds(first, SUBLANES, stride=height), :]

            ends = [read(c, row) for c in columns]
            others = [(read(c, row, -1), read(c, row, 1), read(c, inward)) for c in columns]
            for column, tile in enumerate(swept_tiles(ends, others)):
                x = pl.ds(column * LANES, LANES)
                out[0, at, x] = ends[column]
                out[1, at, x] = tile
        return 0

    lax.fori_loop(0, (planes - 2) // SUBLANES, body, 0)


def faces(field, rows, cols):
    face = jax.ShapeDtypeStruct((2, field.shape[0] - 2, cols), jnp.float32)
    return pl.pallas_call(
        functools.partial(faces_kernel, rows, cols),
        name="faces",
        out_shape=(face, face),
        in_specs=[VMEM],
        out_specs=(VMEM, VMEM),
        compiler_params=params(8),
        cost_estimate=cost(2),
    )(field)


def raise_kernel(dist, par, flags, occ, field, first, second, words, total, ends):
    step = pl.program_id(0)
    last = pl.num_programs(0) - 1
    chunk, rows, cols = dist.shape
    depth = field.shape[0] - 2
    columns = range(cols // LANES)

    @pl.when(step == 0)
    def _():
        words[...] = packed_table(flags)
        total[...] = jnp.zeros_like(total)
        for z in (0, depth + 1):
            field[z] = jnp.full(field.shape[1:], FAR)

    table = words[...]

    def body(group, acc):
        for part in range(RAISE_UNROLL):
            z = group * RAISE_UNROLL + part
            fill_pads(field, (step * chunk + z + 1,), rows, cols)
            for y in range(0, rows, SUBLANES):
                for column in columns:
                    at = (z, pl.ds(y, SUBLANES), pl.ds(column * LANES, LANES))
                    tile, cleared = raise_tile(table, dist[at], par[at], occ[at])
                    to = pl.ds(row_of(column, y, rows), SUBLANES)
                    field[step * chunk + z + 1, to, :] = tile
                    acc[part] = acc[part] + cleared
        return acc

    zeros = jnp.zeros((SUBLANES, LANES), jnp.int32)
    parts = lax.fori_loop(0, chunk // RAISE_UNROLL, body, [zeros] * RAISE_UNROLL)
    total[...] += sum(parts[1:], parts[0])

    def keep_end(side, z):
        def read(dz, at):
            return field[z + 1 + dz, pl.ds(at, SUBLANES), :]

        for y in range(0, rows, SUBLANES):
            swept = swept_plane(read, rows, cols, y, (1, -1)[side : side + 1])
            for column in columns:
                x = pl.ds(column * LANES, LANES)
                ends[side, pl.ds(y, SUBLANES), x] = read(0, row_of(column, y, rows))
                ends[side, pl.ds(rows + y, SUBLANES), x] = swept[column]

    @pl.when(step == 0)
    def _():
        keep_end(0, 0)

    @pl.when(step == last)
    def _():
        keep_end(1, depth - 1)
        count = jnp.sum(total[...])
        row = lax.broadcasted_iota(jnp.int32, (SUBLANES, cols), 0)
        low = (count & (2**COUNT_BITS - 1)).astype(jnp.float32)
        high = (count >> COUNT_BITS).astype(jnp.float32)
        counts = jnp.where(row == 2, low, jnp.where(row == 3, high, 0.0))
        odd = lax.axis_index("gz") & 1
        for out, side in ((first, 1 - odd), (second, odd)):
            out[pl.ds(0, 2 * rows), :] = ends[side]
            out[pl.ds(2 * rows, SUBLANES), :] = counts


def raise_all(dist, par, flags, occ):
    depth, rows, cols = dist.shape
    block = pl.BlockSpec((CHUNK, rows, cols), lambda i: (i, 0, 0))
    message = jax.ShapeDtypeStruct((2 * rows + SUBLANES, cols), jnp.float32)
    return pl.pallas_call(
        raise_kernel,
        name="raise_all",
        out_shape=(
            jax.ShapeDtypeStruct((depth + 2, padded_rows(rows, cols), LANES), jnp.float32),
            message,
            message,
        ),
        grid=(depth // CHUNK,),
        in_specs=[block, block, pl.BlockSpec(flags.shape, lambda i: (0, 0)), block],
        out_specs=(VMEM, VMEM, VMEM),
        scratch_shapes=[
            pltpu.VMEM((SUBLANES, LANES), jnp.int32),
            pltpu.VMEM((SUBLANES, LANES), jnp.int32),
            pltpu.VMEM((2, 2 * rows, cols), jnp.float32),
        ],
        compiler_params=params(24),
        cost_estimate=cost(12),
    )(dist, par, flags, occ)


def sweep_once_kernel(start, count, rows, cols, field, once):
    depth = field.shape[0] - 2

    def sweep(z):
        def read(dz, at):
            return field[z + 1 + dz, pl.ds(at, SUBLANES), :]

        fill_pads(once, (z - start + 1,), rows, cols)
        for y in range(0, rows, SUBLANES):
            for column, tile in enumerate(swept_plane(read, rows, cols, y)):
                once[z - start + 1, pl.ds(row_of(column, y, rows), SUBLANES), :] = tile

    def body(group, _):
        for part in range(SWEEP_UNROLL):
            sweep(start + group * SWEEP_UNROLL + part)
        return 0

    for z in (start - 1, start + count):
        if 0 <= z < depth:
            sweep(z)
        else:
            once[z - start + 1] = jnp.full(once.shape[1:], FAR)
    lax.fori_loop(0, count // SWEEP_UNROLL, body, 0)


def sweep_once(field, start, count, rows, cols):
    return pl.pallas_call(
        functools.partial(sweep_once_kernel, start, count, rows, cols),
        out_shape=jax.ShapeDtypeStruct((count + 2, *field.shape[1:]), jnp.float32),
        in_specs=[VMEM],
        out_specs=VMEM,
        compiler_params=params(8),
        cost_estimate=cost(8),
    )(field)


def sweep_again_kernel(start, once, *refs):
    out, slab, stage, sem = refs[-4:]
    _, chunk, rows, cols = stage.shape
    columns = range(cols // LANES)
    count = once.shape[0] - 2
    copies = []
    for step in range(count // chunk):
        slot = step % 2
        if step >= 2:
            copies[step - 2].wait()

        def body(group, _, step=step, slot=slot):
            for part in range(SWEEP_UNROLL):
                z = group * SWEEP_UNROLL + part
                plane = step * chunk + z

                def read(dz, at):
                    return once[plane + 1 + dz, pl.ds(at, SUBLANES), :]

                for y in range(0, rows, SUBLANES):
                    for column, tile in enumerate(swept_plane(read, rows, cols, y)):
                        stage[slot, z, pl.ds(y, SUBLANES), pl.ds(column * LANES, LANES)] = tile
                        at = plane * (rows * len(columns)) + column * rows + y
                        slab[pl.ds(pl.multiple_of(at, SUBLANES), SUBLANES), :] = tile
            return 0

        lax.fori_loop(0, chunk // SWEEP_UNROLL, body, 0)
        to = out.at[pl.ds(start + step * chunk, chunk)]
        cp = pltpu.make_async_copy(stage.at[slot], to, sem.at[slot])
        cp.start()
        copies.append(cp)
    for cp in copies[-2:]:
        cp.wait()


def sweep_again(once, out, start, depth, rows, cols):
    count = once.shape[0] - 2
    given = [] if out is None else [out]
    return pl.pallas_call(
        functools.partial(sweep_again_kernel, start),
        out_shape=(
            jax.ShapeDtypeStruct((depth, rows, cols), jnp.float32),
            jax.ShapeDtypeStruct((count * rows * cols // LANES, LANES), jnp.float32),
        ),
        in_specs=[VMEM] + [HBM] * len(given),
        out_specs=(HBM, VMEM),
        input_output_aliases={1: 0} if given else {},
        scratch_shapes=[
            pltpu.VMEM((2, CHUNK, rows, cols), jnp.float32),
            pltpu.SemaphoreType.DMA((2,)),
        ],
        compiler_params=params(8),
        cost_estimate=cost(8),
    )(once, *given)


def corners_kernel(first, second, counts, more, low, high, total):
    rows = (first.shape[0] - SUBLANES) // 2
    odd = lax.axis_index("gz") & 1
    total[...] = counts[...] + more[...]
    low[...] = total[...]
    high[...] = total[...]
    for side in range(2):
        for out, row in ((low, 0), (high, rows - 1)):
            line = jnp.where(odd != side, first[pl.ds(row, 1), :], second[pl.ds(row, 1), :])
            out[pl.ds(side, 1), :] = line


def corners(first, second, counts, more):
    shape = jax.ShapeDtypeStruct(counts.shape, jnp.float32)
    return pl.pallas_call(
        corners_kernel,
        name="corners",
        out_shape=(shape,) * 3,
        in_specs=[VMEM] * 4,
        out_specs=(VMEM,) * 3,
        compiler_params=params(2),
        cost_estimate=cost(1),
    )(first, second, counts, more)


def patch_z_kernel(slabs, first, second, slab_low, slab_high, _, out, edges, planes, sem):
    depth, rows, cols = out.shape
    columns = range(cols // LANES)
    slab = lax.axis_index("gz")
    odd = slab & 1
    size = rows * len(columns)
    stores = []
    for side, own in enumerate((slab_low, slab_high)):
        missing = slab == (0, slabs - 1)[side]
        base = (0, own.shape[0] - 2 * size)[side]
        for away in range(2):
            plane = (away, 1 - away)[side]
            offered = (rows, 0)[away]
            for y in range(0, rows, SUBLANES):
                for column in columns:
                    x = pl.ds(column * LANES, LANES)
                    at = (pl.ds(offered + y, SUBLANES), x)
                    got = jnp.where(odd != side, first[at], second[at])
                    got = jnp.where(missing, FAR, got) + VOXEL
                    if away:
                        got = got + VOXEL
                    tile = own[pl.ds(base + plane * size + column * rows + y, SUBLANES), :]
                    planes[side, plane, pl.ds(y, SUBLANES), x] = jnp.minimum(tile, got)
        to = out.at[pl.ds((0, depth - 2)[side], 2)]
        cp = pltpu.make_async_copy(planes.at[side], to, sem.at[side])
        cp.start()
        stores.append(cp)
    for edge, row in enumerate((0, 1, rows - 2, rows - 1)):
        z = 0
        for own in (slab_low, slab_high):
            for base in range(0, own.shape[0], SUBLANES * size):
                for column in columns:
                    tile = own[pl.ds(base + column * rows + row, SUBLANES, stride=size), :]
                    edges[edge, pl.ds(z, SUBLANES), pl.ds(column * LANES, LANES)] = tile
                z += SUBLANES
        for side in range(2):
            for plane in range(2):
                at = pl.ds((0, depth - 2)[side] + plane, 1)
                edges[edge, at, :] = planes[side, plane, pl.ds(row, 1), :]
    for cp in stores:
        cp.wait()


def patch_z(first, second, slab_low, slab_high, out):
    depth, rows, cols = out.shape
    return pl.pallas_call(
        functools.partial(patch_z_kernel, lax.axis_size("gz")),
        name="patch_z",
        out_shape=(
            jax.ShapeDtypeStruct(out.shape, out.dtype),
            jax.ShapeDtypeStruct((4, depth, cols), jnp.float32),
        ),
        in_specs=[VMEM] * 4 + [HBM],
        out_specs=(HBM, VMEM),
        input_output_aliases={4: 0},
        scratch_shapes=[
            pltpu.VMEM((2, 2, rows, cols), jnp.float32),
            pltpu.SemaphoreType.DMA((2,)),
        ],
        compiler_params=params(4),
        cost_estimate=cost(1),
    )(first, second, slab_low, slab_high, out)


def patch_y_kernel(scale, slabs, edges, low, high, clow, chigh, counts, _, out, share, buf, sem):
    depth, rows, _ = out.shape
    slab = lax.axis_index("gz")
    copies = []
    for side, (face, corner) in enumerate(((low, clow), (high, chigh))):
        for away in range(2):
            edge = (away, 3 - away)[side]
            row = (away, rows - 1 - away)[side]
            at = 2 * side + away
            reach = face[1 - away] + VOXEL
            if away:
                reach = reach + VOXEL
            buf[at] = jnp.minimum(edges[edge], reach)
            if not away:
                for end, z in enumerate((0, depth - 1)):
                    missing = slab == (0, slabs - 1)[end]
                    offer = jnp.where(missing, FAR, corner[pl.ds(end, 1), :])
                    line = jnp.minimum(buf[at, pl.ds(z, 1), :], offer + VOXEL + VOXEL)
                    buf[at, pl.ds(z, 1), :] = line
            cp = pltpu.make_async_copy(buf.at[at], out.at[:, row, :], sem.at[at])
            cp.start()
            copies.append(cp)
    x = pl.ds(0, LANES)
    both = (counts[:, x] + clow[:, x]).astype(jnp.int32)
    row = lax.broadcasted_iota(jnp.int32, both.shape, 0)
    both = jnp.where(row == 2, both, jnp.where(row == 3, both << COUNT_BITS, 0))
    count = jnp.sum(both, axis=0, keepdims=True)
    share[...] = count[:, :1].astype(jnp.float32) * jnp.float32(scale)
    for cp in copies:
        cp.wait()


def patch_y(scale, edges, low, high, clow, chigh, counts, out):
    depth, _, cols = out.shape
    return pl.pallas_call(
        functools.partial(patch_y_kernel, scale, lax.axis_size("gz")),
        name="patch_y",
        out_shape=(
            jax.ShapeDtypeStruct(out.shape, out.dtype),
            jax.ShapeDtypeStruct((1, 1), jnp.float32),
        ),
        in_specs=[VMEM] * 6 + [HBM],
        out_specs=(HBM, VMEM),
        input_output_aliases={6: 0},
        scratch_shapes=[pltpu.VMEM((4, depth, cols), jnp.float32), pltpu.SemaphoreType.DMA((4,))],
        compiler_params=params(8),
        cost_estimate=cost(2),
    )(edges, low, high, clow, chigh, counts, out)


def swapped(value, axis, partner):
    count = lax.axis_size(axis)
    return lax.ppermute(value, axis, [(i, partner(i) % count) for i in range(count)])


def shifted(value, axis, by):
    return swapped(value, axis, lambda i: i + by)


def on_device(distance, parent, removed, occupied):
    depth, rows, cols = distance.shape
    half = depth // 2
    slabs, columns = lax.axis_size("gz"), lax.axis_size("gy")
    tied = lax.optimization_barrier
    distance, parent, flags, occupied = (
        pltpu.with_memory_space_constraint(a, pltpu.HBM)
        for a in (distance, parent, removed.reshape(-1, LANES), occupied)
    )

    field, first, second = raise_all(distance, parent, flags, occupied)
    got_first = swapped(first, "gz", lambda i: i ^ 1)
    ylow, yhigh = faces(field, rows, cols)
    low = shifted(yhigh, "gy", 1)
    high = shifted(ylow, "gy", -1)
    once0 = sweep_once(field, 0, half, rows, cols)
    got_first, once0 = tied((got_first, once0))
    second = second.at[2 * rows :].add(got_first[2 * rows :])
    got_second = swapped(second, "gz", lambda i: i - 1 + 2 * (i % 2))
    once1 = sweep_once(field, half, half, rows, cols)
    got_second, once1 = tied((got_second, once1))
    counts = second[2 * rows :] + got_second[2 * rows :]
    more = jnp.zeros_like(counts)

    lowered, half0 = sweep_again(once0, None, 0, depth, rows, cols)
    lowered, half1 = sweep_again(once1, lowered, half, depth, rows, cols)
    step = columns // 2
    turn = 0
    while step > 1:
        if turn:
            counts = counts + more
        more = swapped(counts, "gy", lambda i: i ^ step)
        if turn == 0:
            more, half0 = tied((more, half0))
        elif turn == 1:
            more, half1 = tied((more, half1))
        step //= 2
        turn += 1
    clow, chigh, counts = corners(got_first, got_second, counts, more)
    from_low = shifted(chigh, "gy", 1)
    from_high = shifted(clow, "gy", -1)
    lowered, edges = patch_z(got_first, got_second, half0, half1, lowered)
    total = distance.size * slabs * columns
    lowered, share = patch_y(100.0 / total, edges, low, high, from_low, from_high, counts, lowered)
    return (lowered, share[0, 0])


def solution(mesh):
    slabs, columns = mesh.shape["gz"], mesh.shape["gy"]
    if slabs != 4 or columns < 8 or columns & (columns - 1):
        raise ValueError("unsupported mesh")
    placed = (P("gz", "gy", None), P("gz", "gy", None), P(), P("gz", "gy", None))
    return jax.shard_map(
        on_device, mesh=mesh, in_specs=placed, out_specs=(P("gz", "gy", None), P()), check_vma=False
    )
```

```python
import functools

import jax
import jax.numpy as jnp
from jax import lax
from jax.experimental import pallas as pl
from jax.experimental.pallas import tpu as pltpu
from jax.sharding import PartitionSpec as P


FAR = 1000000.0
VOXEL = 0.1
TRUNC = 2.0
LANES = 128
SUBLANES = 8
CHUNK = 8
RAISE_UNROLL = 4
SWEEP_UNROLL = 4
STORES = 4
MIB = 2**20

HBM = pl.BlockSpec(memory_space=pltpu.HBM)
VMEM = pl.BlockSpec(memory_space=pltpu.VMEM)

COUNT_BITS = 12


def params(mib):
    return pltpu.CompilerParams(vmem_limit_bytes=mib * MIB)


def cost(mib):
    return pl.CostEstimate(flops=0, bytes_accessed=mib * MIB, transcendentals=0)


def packed_table(flags_ref):
    bits = (flags_ref[...] == 1).astype(jnp.int32)
    bits = bits << lax.broadcasted_iota(jnp.int32, bits.shape, 0)
    words = jnp.sum(bits, axis=0, keepdims=True)
    return jnp.broadcast_to(words, (SUBLANES, LANES))


PICK = lax.GatherDimensionNumbers(
    offset_dims=(),
    collapsed_slice_dims=(1,),
    start_index_map=(1,),
    operand_batching_dims=(0,),
    start_indices_batching_dims=(0,),
)


def raise_tile(words, dist, par, occ):
    lane = par & (LANES - 1)
    word = lax.gather(words, lane[..., None], PICK, (1, 1), mode="promise_in_bounds")
    cleared = (word >> (par >> 7)) & (occ ^ 1)
    raised = jnp.where(occ == 1, 0.0, jnp.where(cleared == 1, TRUNC, dist))
    return raised, cleared


def swept_tiles(centers, others):
    lane = lax.broadcasted_iota(jnp.int32, (SUBLANES, LANES), 1)
    last = len(centers) - 1
    after = [pltpu.roll(c, 1, 1) for c in centers]
    before = [pltpu.roll(c, LANES - 1, 1) for c in centers]
    swept = []
    for i, center in enumerate(centers):
        left = jnp.where(lane == 0, after[i - 1] if i else FAR, after[i])
        right = jnp.where(lane == LANES - 1, before[i + 1] if i < last else FAR, before[i])
        nearest = jnp.minimum(left, right)
        for other in others[i]:
            nearest = jnp.minimum(nearest, other)
        swept.append(jnp.minimum(center, nearest + VOXEL))
    return swept


def padded_rows(rows, cols):
    return cols // LANES * (rows + SUBLANES) + SUBLANES


def row_of(column, row, rows):
    return column * (rows + SUBLANES) + SUBLANES + row


def fill_pads(ref, at, rows, cols):
    for column in range(cols // LANES + 1):
        first = row_of(column, -SUBLANES, rows)
        ref[(*at, pl.ds(first, SUBLANES), slice(None))] = jnp.full((SUBLANES, LANES), FAR)


def swept_plane(read, rows, cols, y, beside=(-1, 1)):
    firsts = [row_of(c, y, rows) for c in range(cols // LANES)]
    centers = [read(0, f) for f in firsts]
    others = [[read(dz, f) for dz in beside] + [read(0, f - 1), read(0, f + 1)] for f in firsts]
    return swept_tiles(centers, others)


def faces_kernel(rows, cols, field, low, high):
    planes, height, _ = field.shape
    lines = field.reshape(planes * height, LANES)
    columns = range(cols // LANES)

    def body(group, _):
        z = pl.multiple_of(group * SUBLANES, SUBLANES)
        at = pl.ds(z, SUBLANES)
        for out, row, inward in ((low, 0, 1), (high, rows - 1, rows - 2)):

            def read(column, y, dz=0):
                first = (z + 1 + dz) * height + row_of(column, y, rows)
                return lines[pl.ds(first, SUBLANES, stride=height), :]

            ends = [read(c, row) for c in columns]
            others = [(read(c, row, -1), read(c, row, 1), read(c, inward)) for c in columns]
            for column, tile in enumerate(swept_tiles(ends, others)):
                x = pl.ds(column * LANES, LANES)
                out[0, at, x] = ends[column]
                out[1, at, x] = tile
        return 0

    lax.fori_loop(0, (planes - 2) // SUBLANES, body, 0)


def faces(field, rows, cols):
    face = jax.ShapeDtypeStruct((2, field.shape[0] - 2, cols), jnp.float32)
    return pl.pallas_call(
        functools.partial(faces_kernel, rows, cols),
        name="faces",
        out_shape=(face, face),
        in_specs=[VMEM],
        out_specs=(VMEM, VMEM),
        compiler_params=params(8),
        cost_estimate=cost(2),
    )(field)


def raise_kernel(dist, par, flags_at, occ, field, first, second, flags, buf, ends, fsem, sem):
    depth, rows, cols = dist.shape
    columns = range(cols // LANES)
    chunks = depth // CHUNK

    def reads(chunk):
        at = pl.ds(chunk * CHUNK, CHUNK)
        return [
            pltpu.make_async_copy(src.at[at], dst.at[at], sem.at[which, chunk])
            for which, (src, dst) in enumerate(zip((dist, par, occ), buf))
        ]

    table_in = pltpu.make_async_copy(flags_at, flags, fsem)
    table_in.start()
    for chunk in range(chunks):
        for cp in reads(chunk):
            cp.start()
    for z in (0, depth + 1):
        field[z] = jnp.full(field.shape[1:], FAR)
    table_in.wait()
    table = packed_table(flags)

    def body(chunk, acc):
        for cp in reads(chunk):
            cp.wait()

        def planes(group, acc):
            for part in range(RAISE_UNROLL):
                z = chunk * CHUNK + group * RAISE_UNROLL + part
                fill_pads(field, (z + 1,), rows, cols)
                for y in range(0, rows, SUBLANES):
                    for column in columns:
                        at = (z, pl.ds(y, SUBLANES), pl.ds(column * LANES, LANES))
                        tile, cleared = raise_tile(table, *(b[at] for b in buf))
                        to = pl.ds(row_of(column, y, rows), SUBLANES)
                        field[z + 1, to, :] = tile
                        acc[part] = acc[part] + cleared
            return acc

        return lax.fori_loop(0, CHUNK // RAISE_UNROLL, planes, acc)

    zeros = jnp.zeros((SUBLANES, LANES), jnp.int32)
    parts = lax.fori_loop(0, chunks, body, [zeros] * RAISE_UNROLL)
    total = sum(parts[1:], parts[0])

    def keep_end(side, z):
        def read(dz, at):
            return field[z + 1 + dz, pl.ds(at, SUBLANES), :]

        for y in range(0, rows, SUBLANES):
            swept = swept_plane(read, rows, cols, y, (1, -1)[side : side + 1])
            for column in columns:
                x = pl.ds(column * LANES, LANES)
                ends[side, pl.ds(y, SUBLANES), x] = read(0, row_of(column, y, rows))
                ends[side, pl.ds(rows + y, SUBLANES), x] = swept[column]

    keep_end(0, 0)
    keep_end(1, depth - 1)
    count = jnp.sum(total)
    row = lax.broadcasted_iota(jnp.int32, (SUBLANES, cols), 0)
    low = (count & (2**COUNT_BITS - 1)).astype(jnp.float32)
    high = (count >> COUNT_BITS).astype(jnp.float32)
    counts = jnp.where(row == 2, low, jnp.where(row == 3, high, 0.0))
    odd = lax.axis_index("gz") & 1
    for out, side in ((first, odd), (second, 1 - odd)):
        out[pl.ds(0, 2 * rows), :] = ends[side]
        out[pl.ds(2 * rows, SUBLANES), :] = counts


def raise_all(dist, par, flags, occ):
    depth, rows, cols = dist.shape
    message = jax.ShapeDtypeStruct((2 * rows + SUBLANES, cols), jnp.float32)
    return pl.pallas_call(
        raise_kernel,
        name="raise_all",
        out_shape=(
            jax.ShapeDtypeStruct((depth + 2, padded_rows(rows, cols), LANES), jnp.float32),
            message,
            message,
        ),
        in_specs=[HBM] * 4,
        out_specs=(VMEM,) * 3,
        scratch_shapes=[
            pltpu.VMEM(flags.shape, jnp.int32),
            [pltpu.VMEM(a.shape, a.dtype) for a in (dist, par, occ)],
            pltpu.VMEM((2, 2 * rows, cols), jnp.float32),
            pltpu.SemaphoreType.DMA,
            pltpu.SemaphoreType.DMA((3, depth // CHUNK)),
        ],
        compiler_params=params(20),
        cost_estimate=cost(12),
    )(dist, par, flags, occ)


def sweep_once_kernel(start, count, rows, cols, field, once):
    depth = field.shape[0] - 2

    def sweep(z):
        def read(dz, at):
            return field[z + 1 + dz, pl.ds(at, SUBLANES), :]

        fill_pads(once, (z - start + 1,), rows, cols)
        for y in range(0, rows, SUBLANES):
            for column, tile in enumerate(swept_plane(read, rows, cols, y)):
                once[z - start + 1, pl.ds(row_of(column, y, rows), SUBLANES), :] = tile

    def body(group, _):
        for part in range(SWEEP_UNROLL):
            sweep(start + group * SWEEP_UNROLL + part)
        return 0

    for z in (start - 1, start + count):
        if 0 <= z < depth:
            sweep(z)
        else:
            once[z - start + 1] = jnp.full(once.shape[1:], FAR)
    lax.fori_loop(0, count // SWEEP_UNROLL, body, 0)


def sweep_once(field, start, count, rows, cols):
    return pl.pallas_call(
        functools.partial(sweep_once_kernel, start, count, rows, cols),
        out_shape=jax.ShapeDtypeStruct((count + 2, *field.shape[1:]), jnp.float32),
        in_specs=[VMEM],
        out_specs=VMEM,
        compiler_params=params(8),
        cost_estimate=cost(8),
    )(field)


def sweep_again_kernel(start, once, *refs):
    out, slab, stage, sem = refs[-4:]
    chunk, rows, cols = stage.shape[1:]
    columns = range(cols // LANES)
    count = once.shape[0] - 2
    slots = stage.shape[0]
    copies = []
    for step in range(count // chunk):
        slot = step % slots
        if step >= slots:
            copies[step - slots].wait()

        def body(group, _, step=step, slot=slot):
            for part in range(SWEEP_UNROLL):
                z = group * SWEEP_UNROLL + part
                plane = step * chunk + z

                def read(dz, at):
                    return once[plane + 1 + dz, pl.ds(at, SUBLANES), :]

                for y in range(0, rows, SUBLANES):
                    for column, tile in enumerate(swept_plane(read, rows, cols, y)):
                        stage[slot, z, pl.ds(y, SUBLANES), pl.ds(column * LANES, LANES)] = tile
                        at = plane * (rows * len(columns)) + column * rows + y
                        slab[pl.ds(pl.multiple_of(at, SUBLANES), SUBLANES), :] = tile
            return 0

        lax.fori_loop(0, chunk // SWEEP_UNROLL, body, 0)
        to = out.at[pl.ds(start + step * chunk, chunk)]
        cp = pltpu.make_async_copy(stage.at[slot], to, sem.at[slot])
        cp.start()
        copies.append(cp)
    for cp in copies[-slots:]:
        cp.wait()


def sweep_again(once, out, start, depth, rows, cols):
    count = once.shape[0] - 2
    given = [] if out is None else [out]
    return pl.pallas_call(
        functools.partial(sweep_again_kernel, start),
        out_shape=(
            jax.ShapeDtypeStruct((depth, rows, cols), jnp.float32),
            jax.ShapeDtypeStruct((count * rows * cols // LANES, LANES), jnp.float32),
        ),
        in_specs=[VMEM] + [HBM] * len(given),
        out_specs=(HBM, VMEM),
        input_output_aliases={1: 0} if given else {},
        scratch_shapes=[
            pltpu.VMEM((STORES, CHUNK, rows, cols), jnp.float32),
            pltpu.SemaphoreType.DMA((STORES,)),
        ],
        compiler_params=params(8),
        cost_estimate=cost(8),
    )(once, *given)


def corners_kernel(first, second, counts, more, low, high, total):
    rows = (first.shape[0] - SUBLANES) // 2
    odd = lax.axis_index("gz") & 1
    total[...] = counts[...] + more[...]
    low[...] = total[...]
    high[...] = total[...]
    for side in range(2):
        for out, row in ((low, 0), (high, rows - 1)):
            line = jnp.where(odd == side, first[pl.ds(row, 1), :], second[pl.ds(row, 1), :])
            out[pl.ds(side, 1), :] = line


def corners(first, second, counts, more):
    shape = jax.ShapeDtypeStruct(counts.shape, jnp.float32)
    return pl.pallas_call(
        corners_kernel,
        name="corners",
        out_shape=(shape,) * 3,
        in_specs=[VMEM] * 4,
        out_specs=(VMEM,) * 3,
        compiler_params=params(2),
        cost_estimate=cost(1),
    )(first, second, counts, more)


def patch_z_kernel(slabs, first, second, slab_low, slab_high, _, out, edges, planes, sem):
    depth, rows, cols = out.shape
    columns = range(cols // LANES)
    slab = lax.axis_index("gz")
    odd = slab & 1
    size = rows * len(columns)
    stores = []
    for side, own in enumerate((slab_low, slab_high)):
        missing = slab == (0, slabs - 1)[side]
        base = (0, own.shape[0] - 2 * size)[side]
        for away in range(2):
            plane = (away, 1 - away)[side]
            offered = (rows, 0)[away]
            for y in range(0, rows, SUBLANES):
                for column in columns:
                    x = pl.ds(column * LANES, LANES)
                    at = (pl.ds(offered + y, SUBLANES), x)
                    got = jnp.where(odd == side, first[at], second[at])
                    got = jnp.where(missing, FAR, got) + VOXEL
                    if away:
                        got = got + VOXEL
                    tile = own[pl.ds(base + plane * size + column * rows + y, SUBLANES), :]
                    planes[side, plane, pl.ds(y, SUBLANES), x] = jnp.minimum(tile, got)
        to = out.at[pl.ds((0, depth - 2)[side], 2)]
        cp = pltpu.make_async_copy(planes.at[side], to, sem.at[side])
        cp.start()
        stores.append(cp)
    for edge, row in enumerate((0, 1, rows - 2, rows - 1)):
        z = 0
        for own in (slab_low, slab_high):
            for base in range(0, own.shape[0], SUBLANES * size):
                for column in columns:
                    tile = own[pl.ds(base + column * rows + row, SUBLANES, stride=size), :]
                    edges[edge, pl.ds(z, SUBLANES), pl.ds(column * LANES, LANES)] = tile
                z += SUBLANES
        for side in range(2):
            for plane in range(2):
                at = pl.ds((0, depth - 2)[side] + plane, 1)
                edges[edge, at, :] = planes[side, plane, pl.ds(row, 1), :]
    for cp in stores:
        cp.wait()


def patch_z(first, second, slab_low, slab_high, out):
    depth, rows, cols = out.shape
    return pl.pallas_call(
        functools.partial(patch_z_kernel, lax.axis_size("gz")),
        name="patch_z",
        out_shape=(
            jax.ShapeDtypeStruct(out.shape, out.dtype),
            jax.ShapeDtypeStruct((4, depth, cols), jnp.float32),
        ),
        in_specs=[VMEM] * 4 + [HBM],
        out_specs=(HBM, VMEM),
        input_output_aliases={4: 0},
        scratch_shapes=[
            pltpu.VMEM((2, 2, rows, cols), jnp.float32),
            pltpu.SemaphoreType.DMA((2,)),
        ],
        compiler_params=params(4),
        cost_estimate=cost(1),
    )(first, second, slab_low, slab_high, out)


def patch_y_kernel(scale, slabs, edges, low, high, clow, chigh, counts, _, out, share, buf, sem):
    depth, rows, _ = out.shape
    slab = lax.axis_index("gz")
    copies = []
    for side, (face, corner) in enumerate(((low, clow), (high, chigh))):
        for away in range(2):
            edge = (away, 3 - away)[side]
            row = (away, rows - 1 - away)[side]
            at = 2 * side + away
            reach = face[1 - away] + VOXEL
            if away:
                reach = reach + VOXEL
            buf[at] = jnp.minimum(edges[edge], reach)
            if not away:
                for end, z in enumerate((0, depth - 1)):
                    missing = slab == (0, slabs - 1)[end]
                    offer = jnp.where(missing, FAR, corner[pl.ds(end, 1), :])
                    line = jnp.minimum(buf[at, pl.ds(z, 1), :], offer + VOXEL + VOXEL)
                    buf[at, pl.ds(z, 1), :] = line
            cp = pltpu.make_async_copy(buf.at[at], out.at[:, row, :], sem.at[at])
            cp.start()
            copies.append(cp)
    x = pl.ds(0, LANES)
    both = (counts[:, x] + clow[:, x]).astype(jnp.int32)
    row = lax.broadcasted_iota(jnp.int32, both.shape, 0)
    both = jnp.where(row == 2, both, jnp.where(row == 3, both << COUNT_BITS, 0))
    count = jnp.sum(both, axis=0, keepdims=True)
    share[...] = count[:, :1].astype(jnp.float32) * jnp.float32(scale)
    for cp in copies:
        cp.wait()


def patch_y(scale, edges, low, high, clow, chigh, counts, out):
    depth, _, cols = out.shape
    return pl.pallas_call(
        functools.partial(patch_y_kernel, scale, lax.axis_size("gz")),
        name="patch_y",
        out_shape=(
            jax.ShapeDtypeStruct(out.shape, out.dtype),
            jax.ShapeDtypeStruct((1, 1), jnp.float32),
        ),
        in_specs=[VMEM] * 6 + [HBM],
        out_specs=(HBM, VMEM),
        input_output_aliases={6: 0},
        scratch_shapes=[pltpu.VMEM((4, depth, cols), jnp.float32), pltpu.SemaphoreType.DMA((4,))],
        compiler_params=params(8),
        cost_estimate=cost(2),
    )(edges, low, high, clow, chigh, counts, out)


def swapped(value, axis, partner):
    count = lax.axis_size(axis)
    return lax.ppermute(value, axis, [(i, partner(i) % count) for i in range(count)])


def shifted(value, axis, by):
    return swapped(value, axis, lambda i: i + by)


def on_device(distance, parent, removed, occupied):
    depth, rows, cols = distance.shape
    half = depth // 2
    slabs, columns = lax.axis_size("gz"), lax.axis_size("gy")
    tied = lax.optimization_barrier
    distance, parent, flags, occupied = (
        pltpu.with_memory_space_constraint(a, pltpu.HBM)
        for a in (distance, parent, removed.reshape(-1, LANES), occupied)
    )

    field, first, second = raise_all(distance, parent, flags, occupied)
    got_first = swapped(first, "gz", lambda i: i - 1 + 2 * (i % 2))
    ylow, yhigh = faces(field, rows, cols)
    low = shifted(yhigh, "gy", 1)
    high = shifted(ylow, "gy", -1)
    once0 = sweep_once(field, 0, half, rows, cols)
    got_first, once0 = tied((got_first, once0))
    second = second.at[2 * rows :].add(got_first[2 * rows :])
    got_second = swapped(second, "gz", lambda i: i ^ 1)
    once1 = sweep_once(field, half, half, rows, cols)
    got_second, once1 = tied((got_second, once1))
    counts = second[2 * rows :] + got_second[2 * rows :]
    more = jnp.zeros_like(counts)

    lowered, half0 = sweep_again(once0, None, 0, depth, rows, cols)
    lowered, half1 = sweep_again(once1, lowered, half, depth, rows, cols)
    step = columns // 2
    turn = 0
    while step > 1:
        if turn:
            counts = counts + more
        more = swapped(counts, "gy", lambda i: i ^ step)
        if turn == 0:
            more, half0 = tied((more, half0))
        elif turn == 1:
            more, half1 = tied((more, half1))
        step //= 2
        turn += 1
    clow, chigh, counts = corners(got_first, got_second, counts, more)
    from_low = shifted(chigh, "gy", 1)
    from_high = shifted(clow, "gy", -1)
    lowered, edges = patch_z(got_first, got_second, half0, half1, lowered)
    total = distance.size * slabs * columns
    lowered, share = patch_y(100.0 / total, edges, low, high, from_low, from_high, counts, lowered)
    return (lowered, share[0, 0])


def solution(mesh):
    slabs, columns = mesh.shape["gz"], mesh.shape["gy"]
    if slabs != 4 or columns < 8 or columns & (columns - 1):
        raise ValueError("unsupported mesh")
    placed = (P("gz", "gy", None), P("gz", "gy", None), P(), P("gz", "gy", None))
    return jax.shard_map(
        on_device, mesh=mesh, in_specs=placed, out_specs=(P("gz", "gy", None), P()), check_vma=False
    )
```

```python
import functools

import jax
import jax.numpy as jnp
from jax import lax
from jax.experimental import pallas as pl
from jax.experimental.pallas import tpu as pltpu
from jax.sharding import PartitionSpec as P


FAR = 1000000.0
VOXEL = 0.1
TRUNC = 2.0
LANES = 128
SUBLANES = 8
CHUNK = 8
READ = 8
AHEAD = 3
RAISE_UNROLL = 8
SWEEP_UNROLL = 4
STORES = 4
MIB = 2**20

HBM = pl.BlockSpec(memory_space=pltpu.HBM)
VMEM = pl.BlockSpec(memory_space=pltpu.VMEM)

COUNT_BITS = 12


def params(mib):
    return pltpu.CompilerParams(vmem_limit_bytes=mib * MIB)


def cost(mib):
    return pl.CostEstimate(flops=0, bytes_accessed=mib * MIB, transcendentals=0)


def packed_table(flags_ref):
    bits = (flags_ref[...] == 1).astype(jnp.int32)
    bits = bits << lax.broadcasted_iota(jnp.int32, bits.shape, 0)
    words = jnp.sum(bits, axis=0, keepdims=True)
    return jnp.broadcast_to(words, (SUBLANES, LANES))


PICK = lax.GatherDimensionNumbers(
    offset_dims=(),
    collapsed_slice_dims=(1,),
    start_index_map=(1,),
    operand_batching_dims=(0,),
    start_indices_batching_dims=(0,),
)


def raise_tile(words, dist, par, occ):
    lane = par & (LANES - 1)
    word = lax.gather(words, lane[..., None], PICK, (1, 1), mode="promise_in_bounds")
    cleared = (word >> (par >> 7)) & (occ ^ 1)
    raised = jnp.where(occ == 1, 0.0, jnp.where(cleared == 1, TRUNC, dist))
    return raised, cleared


def swept_tiles(centers, others):
    lane = lax.broadcasted_iota(jnp.int32, (SUBLANES, LANES), 1)
    last = len(centers) - 1
    after = [pltpu.roll(c, 1, 1) for c in centers]
    before = [pltpu.roll(c, LANES - 1, 1) for c in centers]
    swept = []
    for i, center in enumerate(centers):
        left = jnp.where(lane == 0, after[i - 1] if i else FAR, after[i])
        right = jnp.where(lane == LANES - 1, before[i + 1] if i < last else FAR, before[i])
        nearest = jnp.minimum(left, right)
        for other in others[i]:
            nearest = jnp.minimum(nearest, other)
        swept.append(jnp.minimum(center, nearest + VOXEL))
    return swept


def padded_rows(rows, cols):
    return cols // LANES * (rows + SUBLANES) + SUBLANES


def row_of(column, row, rows):
    return column * (rows + SUBLANES) + SUBLANES + row


def fill_pads(ref, at, rows, cols):
    for column in range(cols // LANES + 1):
        first = row_of(column, -SUBLANES, rows)
        ref[(*at, pl.ds(first, SUBLANES), slice(None))] = jnp.full((SUBLANES, LANES), FAR)


def swept_plane(read, rows, cols, y, beside=(-1, 1)):
    firsts = [row_of(c, y, rows) for c in range(cols // LANES)]
    centers = [read(0, f) for f in firsts]
    others = [[read(dz, f) for dz in beside] + [read(0, f - 1), read(0, f + 1)] for f in firsts]
    return swept_tiles(centers, others)


def faces_kernel(start, rows, cols, field, low, high):
    planes, height, _ = field.shape
    lines = field.reshape(planes * height, LANES)
    columns = range(cols // LANES)

    def body(group, _):
        z = pl.multiple_of(group * SUBLANES, SUBLANES)
        at = pl.ds(z, SUBLANES)
        for out, row, inward in ((low, 0, 1), (high, rows - 1, rows - 2)):

            def read(column, y, dz=0):
                first = (start + z + 1 + dz) * height + row_of(column, y, rows)
                return lines[pl.ds(first, SUBLANES, stride=height), :]

            ends = [read(c, row) for c in columns]
            others = [(read(c, row, -1), read(c, row, 1), read(c, inward)) for c in columns]
            for column, tile in enumerate(swept_tiles(ends, others)):
                x = pl.ds(column * LANES, LANES)
                out[0, at, x] = ends[column]
                out[1, at, x] = tile
        return 0

    lax.fori_loop(0, low.shape[1] // SUBLANES, body, 0)


def faces(field, start, count, rows, cols):
    face = jax.ShapeDtypeStruct((2, count, cols), jnp.float32)
    return pl.pallas_call(
        functools.partial(faces_kernel, start, rows, cols),
        out_shape=(face, face),
        in_specs=[VMEM],
        out_specs=(VMEM, VMEM),
        compiler_params=params(8),
        cost_estimate=cost(2),
    )(field)


def raise_planes(start, count, dist, par, flags_at, occ, field, flags, buf, fsem, sem):
    _, rows, cols = dist.shape
    columns = range(cols // LANES)
    chunks = count // READ

    def reads(chunk):
        source, target = pl.ds(start + chunk * READ, READ), pl.ds(chunk * READ, READ)
        return [
            pltpu.make_async_copy(src.at[source], dst.at[target], sem.at[which, chunk])
            for which, (src, dst) in enumerate(zip((dist, par, occ), buf))
        ]

    table_in = pltpu.make_async_copy(flags_at, flags, fsem)
    table_in.start()
    for chunk in range(min(AHEAD, chunks)):
        for cp in reads(chunk):
            cp.start()
    for z in (0, field.shape[0] - 1):
        if start < z <= start + count + 1 or z == start == 0:
            field[z] = jnp.full(field.shape[1:], FAR)
    table_in.wait()
    table = packed_table(flags)

    def body(chunk, acc):
        @pl.when(chunk + AHEAD < chunks)
        def _():
            for cp in reads(chunk + AHEAD):
                cp.start()

        for cp in reads(chunk):
            cp.wait()

        def planes(group, acc):
            for part in range(RAISE_UNROLL):
                z = chunk * READ + group * RAISE_UNROLL + part
                fill_pads(field, (start + z + 1,), rows, cols)
                for y in range(0, rows, SUBLANES):
                    for column in columns:
                        at = (z, pl.ds(y, SUBLANES), pl.ds(column * LANES, LANES))
                        tile, cleared = raise_tile(table, *(b[at] for b in buf))
                        to = pl.ds(row_of(column, y, rows), SUBLANES)
                        field[start + z + 1, to, :] = tile
                        acc[part] = acc[part] + cleared
            return acc

        return lax.fori_loop(0, READ // RAISE_UNROLL, planes, acc)

    zeros = jnp.zeros((SUBLANES, LANES), jnp.int32)
    parts = lax.fori_loop(0, chunks, body, [zeros] * RAISE_UNROLL)
    return sum(parts[1:], parts[0])


def keep_end(field, z, inward, rows, cols, out):
    def read(dz, at):
        return field[z + 1 + dz, pl.ds(at, SUBLANES), :]

    for y in range(0, rows, SUBLANES):
        swept = swept_plane(read, rows, cols, y, (inward,))
        for column in range(cols // LANES):
            x = pl.ds(column * LANES, LANES)
            out[pl.ds(y, SUBLANES), x] = read(0, row_of(column, y, rows))
            out[pl.ds(rows + y, SUBLANES), x] = swept[column]


def raise_start_kernel(count, dist, par, flags_at, occ, field, end, total, flags, buf, fsem, sem):
    _, rows, cols = dist.shape
    total[...] = raise_planes(0, count, dist, par, flags_at, occ, field, flags, buf, fsem, sem)
    keep_end(field, 0, 1, rows, cols, end)


def raise_rest_kernel(
    start, dist, par, flags_at, occ, low, before, _, field, first, second, counts, flags, buf, high, fsem, sem
):
    depth, rows, cols = dist.shape
    total = raise_planes(
        start, depth - start, dist, par, flags_at, occ, field, flags, buf, fsem, sem
    )
    count = jnp.sum(total + before[...])
    row = lax.broadcasted_iota(jnp.int32, (SUBLANES, cols), 0)
    small = (count & (2**COUNT_BITS - 1)).astype(jnp.float32)
    large = (count >> COUNT_BITS).astype(jnp.float32)
    counts[...] = jnp.where(row == 2, small, jnp.where(row == 3, large, 0.0))
    keep_end(field, depth - 1, -1, rows, cols, high)
    odd = (lax.axis_index("gz") & 1) == 1
    for y in range(0, 2 * rows, SUBLANES):
        at = pl.ds(y, SUBLANES)
        first[at, :] = jnp.where(odd, high[at, :], low[at, :])
        second[at, :] = jnp.where(odd, low[at, :], high[at, :])
    first[pl.ds(2 * rows, SUBLANES), :] = counts[...]
    second[pl.ds(2 * rows, SUBLANES), :] = counts[...]


def raise_scratch(count, dist, par, flags, occ):
    return [
        pltpu.VMEM(flags.shape, jnp.int32),
        [pltpu.VMEM((count, *a.shape[1:]), a.dtype) for a in (dist, par, occ)],
        pltpu.SemaphoreType.DMA,
        pltpu.SemaphoreType.DMA((3, count // READ)),
    ]


def raise_start(dist, par, flags, occ, count):
    depth, rows, cols = dist.shape
    return pl.pallas_call(
        functools.partial(raise_start_kernel, count),
        name="raise_start",
        out_shape=(
            jax.ShapeDtypeStruct((depth + 2, padded_rows(rows, cols), LANES), jnp.float32),
            jax.ShapeDtypeStruct((2 * rows, cols), jnp.float32),
            jax.ShapeDtypeStruct((SUBLANES, LANES), jnp.int32),
        ),
        in_specs=[HBM] * 4,
        out_specs=(VMEM,) * 3,
        scratch_shapes=raise_scratch(count, dist, par, flags, occ),
        compiler_params=params(20),
        cost_estimate=cost(8),
    )(dist, par, flags, occ)


def raise_rest(dist, par, flags, occ, low, before, field, start):
    depth, rows, cols = dist.shape
    message = jax.ShapeDtypeStruct((2 * rows + SUBLANES, cols), jnp.float32)
    scratch = raise_scratch(depth - start, dist, par, flags, occ)
    return pl.pallas_call(
        functools.partial(raise_rest_kernel, start),
        name="raise_rest",
        out_shape=(
            jax.ShapeDtypeStruct(field.shape, jnp.float32),
            message,
            message,
            jax.ShapeDtypeStruct((SUBLANES, cols), jnp.float32),
        ),
        in_specs=[HBM] * 4 + [VMEM] * 3,
        out_specs=(VMEM,) * 4,
        input_output_aliases={6: 0},
        scratch_shapes=scratch[:2] + [pltpu.VMEM((2 * rows, cols), jnp.float32)] + scratch[2:],
        compiler_params=params(20),
        cost_estimate=cost(8),
    )(dist, par, flags, occ, low, before, field)


def sweep_once_kernel(start, count, rows, cols, field, once):
    depth = field.shape[0] - 2

    def sweep(z):
        def read(dz, at):
            return field[z + 1 + dz, pl.ds(at, SUBLANES), :]

        fill_pads(once, (z - start + 1,), rows, cols)
        for y in range(0, rows, SUBLANES):
            for column, tile in enumerate(swept_plane(read, rows, cols, y)):
                once[z - start + 1, pl.ds(row_of(column, y, rows), SUBLANES), :] = tile

    def body(group, _):
        for part in range(SWEEP_UNROLL):
            sweep(start + group * SWEEP_UNROLL + part)
        return 0

    for z in (start - 1, start + count):
        if 0 <= z < depth:
            sweep(z)
        else:
            once[z - start + 1] = jnp.full(once.shape[1:], FAR)
    lax.fori_loop(0, count // SWEEP_UNROLL, body, 0)


def sweep_once(field, start, count, rows, cols):
    return pl.pallas_call(
        functools.partial(sweep_once_kernel, start, count, rows, cols),
        out_shape=jax.ShapeDtypeStruct((count + 2, *field.shape[1:]), jnp.float32),
        in_specs=[VMEM],
        out_specs=VMEM,
        compiler_params=params(8),
        cost_estimate=cost(8),
    )(field)


def sweep_again_kernel(start, once, *refs):
    out, slab, stage, sem = refs[-4:]
    chunk, rows, cols = stage.shape[1:]
    columns = range(cols // LANES)
    count = once.shape[0] - 2
    slots = stage.shape[0]
    copies = []
    for step in range(count // chunk):
        slot = step % slots
        if step >= slots:
            copies[step - slots].wait()

        def body(group, _, step=step, slot=slot):
            for part in range(SWEEP_UNROLL):
                z = group * SWEEP_UNROLL + part
                plane = step * chunk + z

                def read(dz, at):
                    return once[plane + 1 + dz, pl.ds(at, SUBLANES), :]

                for y in range(0, rows, SUBLANES):
                    for column, tile in enumerate(swept_plane(read, rows, cols, y)):
                        stage[slot, z, pl.ds(y, SUBLANES), pl.ds(column * LANES, LANES)] = tile
                        at = plane * (rows * len(columns)) + column * rows + y
                        slab[pl.ds(pl.multiple_of(at, SUBLANES), SUBLANES), :] = tile
            return 0

        lax.fori_loop(0, chunk // SWEEP_UNROLL, body, 0)
        to = out.at[pl.ds(start + step * chunk, chunk)]
        cp = pltpu.make_async_copy(stage.at[slot], to, sem.at[slot])
        cp.start()
        copies.append(cp)
    for cp in copies[-slots:]:
        cp.wait()


def sweep_again(once, out, start, depth, rows, cols):
    count = once.shape[0] - 2
    given = [] if out is None else [out]
    return pl.pallas_call(
        functools.partial(sweep_again_kernel, start),
        out_shape=(
            jax.ShapeDtypeStruct((depth, rows, cols), jnp.float32),
            jax.ShapeDtypeStruct((count * rows * cols // LANES, LANES), jnp.float32),
        ),
        in_specs=[VMEM] + [HBM] * len(given),
        out_specs=(HBM, VMEM),
        input_output_aliases={1: 0} if given else {},
        scratch_shapes=[
            pltpu.VMEM((STORES, CHUNK, rows, cols), jnp.float32),
            pltpu.SemaphoreType.DMA((STORES,)),
        ],
        compiler_params=params(8),
        cost_estimate=cost(8),
    )(once, *given)


def corners_kernel(first, second, counts, more, low, high, total):
    rows = (first.shape[0] - SUBLANES) // 2
    odd = lax.axis_index("gz") & 1
    total[...] = counts[...] + more[...]
    low[...] = total[...]
    high[...] = total[...]
    for side in range(2):
        for out, row in ((low, 0), (high, rows - 1)):
            line = jnp.where(odd == side, first[pl.ds(row, 1), :], second[pl.ds(row, 1), :])
            out[pl.ds(side, 1), :] = line


def corners(first, second, counts, more):
    shape = jax.ShapeDtypeStruct(counts.shape, jnp.float32)
    return pl.pallas_call(
        corners_kernel,
        name="corners",
        out_shape=(shape,) * 3,
        in_specs=[VMEM] * 4,
        out_specs=(VMEM,) * 3,
        compiler_params=params(2),
        cost_estimate=cost(1),
    )(first, second, counts, more)


def patch_z_kernel(slabs, first, second, slab_low, slab_high, _, out, edges, planes, sem):
    depth, rows, cols = out.shape
    columns = range(cols // LANES)
    slab = lax.axis_index("gz")
    odd = slab & 1
    size = rows * len(columns)
    stores = []
    for side, own in enumerate((slab_low, slab_high)):
        missing = slab == (0, slabs - 1)[side]
        base = (0, own.shape[0] - 2 * size)[side]
        for away in range(2):
            plane = (away, 1 - away)[side]
            offered = (rows, 0)[away]
            for y in range(0, rows, SUBLANES):
                for column in columns:
                    x = pl.ds(column * LANES, LANES)
                    at = (pl.ds(offered + y, SUBLANES), x)
                    got = jnp.where(odd == side, first[at], second[at])
                    got = jnp.where(missing, FAR, got) + VOXEL
                    if away:
                        got = got + VOXEL
                    tile = own[pl.ds(base + plane * size + column * rows + y, SUBLANES), :]
                    planes[side, plane, pl.ds(y, SUBLANES), x] = jnp.minimum(tile, got)
        to = out.at[pl.ds((0, depth - 2)[side], 2)]
        cp = pltpu.make_async_copy(planes.at[side], to, sem.at[side])
        cp.start()
        stores.append(cp)
    for edge, row in enumerate((0, 1, rows - 2, rows - 1)):
        z = 0
        for own in (slab_low, slab_high):
            for base in range(0, own.shape[0], SUBLANES * size):
                for column in columns:
                    tile = own[pl.ds(base + column * rows + row, SUBLANES, stride=size), :]
                    edges[edge, pl.ds(z, SUBLANES), pl.ds(column * LANES, LANES)] = tile
                z += SUBLANES
        for side in range(2):
            for plane in range(2):
                at = pl.ds((0, depth - 2)[side] + plane, 1)
                edges[edge, at, :] = planes[side, plane, pl.ds(row, 1), :]
    for cp in stores:
        cp.wait()


def patch_z(first, second, slab_low, slab_high, out):
    depth, rows, cols = out.shape
    return pl.pallas_call(
        functools.partial(patch_z_kernel, lax.axis_size("gz")),
        name="patch_z",
        out_shape=(
            jax.ShapeDtypeStruct(out.shape, out.dtype),
            jax.ShapeDtypeStruct((4, depth, cols), jnp.float32),
        ),
        in_specs=[VMEM] * 4 + [HBM],
        out_specs=(HBM, VMEM),
        input_output_aliases={4: 0},
        scratch_shapes=[
            pltpu.VMEM((2, 2, rows, cols), jnp.float32),
            pltpu.SemaphoreType.DMA((2,)),
        ],
        compiler_params=params(4),
        cost_estimate=cost(1),
    )(first, second, slab_low, slab_high, out)


def patch_y_kernel(scale, slabs, edges, low0, low1, high0, high1, clow, chigh, counts, _, out, share, buf, sem):
    depth, rows, _ = out.shape
    slab = lax.axis_index("gz")
    copies = []
    for side, (parts, corner) in enumerate((((low0, low1), clow), ((high0, high1), chigh))):
        for away in range(2):
            edge = (away, 3 - away)[side]
            row = (away, rows - 1 - away)[side]
            at = 2 * side + away
            z = 0
            for face in parts:
                planes = pl.ds(z, face.shape[1])
                reach = face[1 - away] + VOXEL
                if away:
                    reach = reach + VOXEL
                buf[at, planes, :] = jnp.minimum(edges[edge, planes, :], reach)
                z += face.shape[1]
            if not away:
                for end, z in enumerate((0, depth - 1)):
                    missing = slab == (0, slabs - 1)[end]
                    offer = jnp.where(missing, FAR, corner[pl.ds(end, 1), :])
                    line = jnp.minimum(buf[at, pl.ds(z, 1), :], offer + VOXEL + VOXEL)
                    buf[at, pl.ds(z, 1), :] = line
            cp = pltpu.make_async_copy(buf.at[at], out.at[:, row, :], sem.at[at])
            cp.start()
            copies.append(cp)
    x = pl.ds(0, LANES)
    both = (counts[:, x] + clow[:, x]).astype(jnp.int32)
    row = lax.broadcasted_iota(jnp.int32, both.shape, 0)
    both = jnp.where(row == 2, both, jnp.where(row == 3, both << COUNT_BITS, 0))
    count = jnp.sum(both, axis=0, keepdims=True)
    share[...] = count[:, :1].astype(jnp.float32) * jnp.float32(scale)
    for cp in copies:
        cp.wait()


def patch_y(scale, edges, lows, highs, clow, chigh, counts, out):
    depth, _, cols = out.shape
    return pl.pallas_call(
        functools.partial(patch_y_kernel, scale, lax.axis_size("gz")),
        name="patch_y",
        out_shape=(
            jax.ShapeDtypeStruct(out.shape, out.dtype),
            jax.ShapeDtypeStruct((1, 1), jnp.float32),
        ),
        in_specs=[VMEM] * 8 + [HBM],
        out_specs=(HBM, VMEM),
        input_output_aliases={8: 0},
        scratch_shapes=[pltpu.VMEM((4, depth, cols), jnp.float32), pltpu.SemaphoreType.DMA((4,))],
        compiler_params=params(8),
        cost_estimate=cost(2),
    )(edges, *lows, *highs, clow, chigh, counts, out)


def swapped(value, axis, partner):
    count = lax.axis_size(axis)
    return lax.ppermute(value, axis, [(i, partner(i) % count) for i in range(count)])


def shifted(value, axis, by):
    return swapped(value, axis, lambda i: i + by)


def on_device(distance, parent, removed, occupied):
    depth, rows, cols = distance.shape
    half = depth // 2
    slabs, columns = lax.axis_size("gz"), lax.axis_size("gy")
    tied = lax.optimization_barrier
    distance, parent, flags, occupied = (
        pltpu.with_memory_space_constraint(a, pltpu.HBM)
        for a in (distance, parent, removed.reshape(-1, LANES), occupied)
    )
    lows, highs = [], []

    def send(field, start, count):
        ylow, yhigh = faces(field, start, count, rows, cols)
        lows.append(shifted(yhigh, "gy", 1))
        highs.append(shifted(ylow, "gy", -1))

    early = half + READ
    field, end, total = raise_start(distance, parent, flags, occupied, early)
    send(field, 0, half)
    field, first, second, counts = raise_rest(
        distance, parent, flags, occupied, end, total, field, early
    )

    bit = 2
    while bit < columns:
        masks = [m for m in (bit, 2 * bit, 3 * bit) if m < columns]
        got = []
        for mask in masks:
            got.append(swapped(counts, "gy", lambda i: i ^ mask))
        counts = sum(got, counts)
        bit *= 4
    send(field, half, depth - half)
    once0 = sweep_once(field, 0, half, rows, cols)
    counts, once0 = tied((counts, once0))

    first = first.at[2 * rows :].set(counts)
    got_first = swapped(first, "gz", lambda i: i - 1 + 2 * (i % 2))
    once1 = sweep_once(field, half, half, rows, cols)
    lowered, half0 = sweep_again(once0, None, 0, depth, rows, cols)
    got_first, half0 = tied((got_first, half0))
    counts = counts + got_first[2 * rows :]
    second = second.at[2 * rows :].set(counts)
    got_second = swapped(second, "gz", lambda i: i ^ 1)
    lowered, half1 = sweep_again(once1, lowered, half, depth, rows, cols)
    got_second, half1 = tied((got_second, half1))
    clow, chigh, counts = corners(got_first, got_second, counts, got_second[2 * rows :])
    from_low = shifted(chigh, "gy", 1)
    from_high = shifted(clow, "gy", -1)
    lowered, edges = patch_z(got_first, got_second, half0, half1, lowered)
    total = distance.size * slabs * columns
    lowered, share = patch_y(
        100.0 / total, edges, lows, highs, from_low, from_high, counts, lowered
    )
    return (lowered, share[0, 0])


def solution(mesh):
    slabs, columns = mesh.shape["gz"], mesh.shape["gy"]
    if slabs != 4 or columns < 8 or columns & (columns - 1):
        raise ValueError("unsupported mesh")
    placed = (P("gz", "gy", None), P("gz", "gy", None), P(), P("gz", "gy", None))
    return jax.shard_map(
        on_device, mesh=mesh, in_specs=placed, out_specs=(P("gz", "gy", None), P()), check_vma=False
    )
```

```python
import functools

import jax
import jax.numpy as jnp
from jax import lax
from jax.experimental import pallas as pl
from jax.experimental.pallas import tpu as pltpu
from jax.sharding import PartitionSpec as P


FAR = 1000000.0
VOXEL = 0.1
TRUNC = 2.0
LANES = 128
SUBLANES = 8
CHUNK = 8
READ = 8
AHEAD = 3
RAISE_UNROLL = 8
SWEEP_UNROLL = 4
STORES = 4
MIB = 2**20

HBM = pl.BlockSpec(memory_space=pltpu.HBM)
VMEM = pl.BlockSpec(memory_space=pltpu.VMEM)

COUNT_BITS = 12


def params(mib):
    return pltpu.CompilerParams(vmem_limit_bytes=mib * MIB)


def cost(mib):
    return pl.CostEstimate(flops=0, bytes_accessed=mib * MIB, transcendentals=0)


def packed_table(flags_ref):
    bits = (flags_ref[...] == 1).astype(jnp.int32)
    bits = bits << lax.broadcasted_iota(jnp.int32, bits.shape, 0)
    words = jnp.sum(bits, axis=0, keepdims=True)
    return jnp.broadcast_to(words, (SUBLANES, LANES))


PICK = lax.GatherDimensionNumbers(
    offset_dims=(),
    collapsed_slice_dims=(1,),
    start_index_map=(1,),
    operand_batching_dims=(0,),
    start_indices_batching_dims=(0,),
)


def raise_tile(words, dist, par, occ):
    lane = par & (LANES - 1)
    word = lax.gather(words, lane[..., None], PICK, (1, 1), mode="promise_in_bounds")
    cleared = (word >> (par >> 7)) & (occ ^ 1)
    raised = jnp.where(occ == 1, 0.0, jnp.where(cleared == 1, TRUNC, dist))
    return raised, cleared


def swept_tiles(centers, others):
    lane = lax.broadcasted_iota(jnp.int32, (SUBLANES, LANES), 1)
    last = len(centers) - 1
    after = [pltpu.roll(c, 1, 1) for c in centers]
    before = [pltpu.roll(c, LANES - 1, 1) for c in centers]
    swept = []
    for i, center in enumerate(centers):
        left = jnp.where(lane == 0, after[i - 1] if i else FAR, after[i])
        right = jnp.where(lane == LANES - 1, before[i + 1] if i < last else FAR, before[i])
        nearest = jnp.minimum(left, right)
        for other in others[i]:
            nearest = jnp.minimum(nearest, other)
        swept.append(jnp.minimum(center, nearest + VOXEL))
    return swept


def padded_rows(rows, cols):
    return cols // LANES * (rows + SUBLANES) + SUBLANES


def row_of(column, row, rows):
    return column * (rows + SUBLANES) + SUBLANES + row


def fill_pads(ref, at, rows, cols):
    for column in range(cols // LANES + 1):
        first = row_of(column, -SUBLANES, rows)
        ref[(*at, pl.ds(first, SUBLANES), slice(None))] = jnp.full((SUBLANES, LANES), FAR)


def swept_plane(read, rows, cols, y, beside=(-1, 1)):
    firsts = [row_of(c, y, rows) for c in range(cols // LANES)]
    centers = [read(0, f) for f in firsts]
    others = [[read(dz, f) for dz in beside] + [read(0, f - 1), read(0, f + 1)] for f in firsts]
    return swept_tiles(centers, others)


def face_tiles(field, rows, cols, row, inward, z):
    planes, height, _ = field.shape
    lines = field.reshape(planes * height, LANES)
    columns = range(cols // LANES)

    def read(column, y, dz=0):
        first = (z + 1 + dz) * height + row_of(column, y, rows)
        return lines[pl.ds(first, SUBLANES, stride=height), :]

    ends = [read(c, row) for c in columns]
    others = [(read(c, row, -1), read(c, row, 1), read(c, inward)) for c in columns]
    return ends, swept_tiles(ends, others)


def write_faces(field, rows, cols, top, start, out):
    def body(group, _):
        at = pl.ds(pl.multiple_of(group * SUBLANES, SUBLANES), SUBLANES)

        def write(row, inward):
            ends, swept = face_tiles(field, rows, cols, row, inward, start + group * SUBLANES)
            for column, (end, tile) in enumerate(zip(ends, swept)):
                x = pl.ds(column * LANES, LANES)
                out[0, at, x] = end
                out[1, at, x] = tile

        pl.when(top)(lambda: write(rows - 1, rows - 2))
        pl.when(jnp.logical_not(top))(lambda: write(0, 1))
        return 0

    lax.fori_loop(0, out.shape[1] // SUBLANES, body, 0)


def faces_kernel(start, rows, cols, field, near, *far):
    odd = (lax.axis_index("gy") & 1) == 1
    write_faces(field, rows, cols, jnp.logical_not(odd), start, near)
    for out in far:
        write_faces(field, rows, cols, odd, 0, out)


def faces(field, start, count, rows, cols, both):
    face = jax.ShapeDtypeStruct((2, count, cols), jnp.float32)
    whole = jax.ShapeDtypeStruct((2, field.shape[0] - 2, cols), jnp.float32)
    shapes = (face, whole) if both else (face,)
    return pl.pallas_call(
        functools.partial(faces_kernel, start, rows, cols),
        out_shape=shapes,
        in_specs=[VMEM],
        out_specs=(VMEM,) * len(shapes),
        compiler_params=params(8),
        cost_estimate=cost(2),
    )(field)


def raise_planes(start, count, dist, par, flags_at, occ, field, flags, buf, fsem, sem):
    _, rows, cols = dist.shape
    columns = range(cols // LANES)
    chunks = count // READ

    def reads(chunk):
        source, target = pl.ds(start + chunk * READ, READ), pl.ds(chunk * READ, READ)
        return [
            pltpu.make_async_copy(src.at[source], dst.at[target], sem.at[which, chunk])
            for which, (src, dst) in enumerate(zip((dist, par, occ), buf))
        ]

    table_in = pltpu.make_async_copy(flags_at, flags, fsem)
    table_in.start()
    for chunk in range(min(AHEAD, chunks)):
        for cp in reads(chunk):
            cp.start()
    for z in (0, field.shape[0] - 1):
        if start < z <= start + count + 1 or z == start == 0:
            field[z] = jnp.full(field.shape[1:], FAR)
    table_in.wait()
    table = packed_table(flags)

    def body(chunk, acc):
        @pl.when(chunk + AHEAD < chunks)
        def _():
            for cp in reads(chunk + AHEAD):
                cp.start()

        for cp in reads(chunk):
            cp.wait()

        def planes(group, acc):
            for part in range(RAISE_UNROLL):
                z = chunk * READ + group * RAISE_UNROLL + part
                fill_pads(field, (start + z + 1,), rows, cols)
                for y in range(0, rows, SUBLANES):
                    for column in columns:
                        at = (z, pl.ds(y, SUBLANES), pl.ds(column * LANES, LANES))
                        tile, cleared = raise_tile(table, *(b[at] for b in buf))
                        to = pl.ds(row_of(column, y, rows), SUBLANES)
                        field[start + z + 1, to, :] = tile
                        acc[part] = acc[part] + cleared
            return acc

        return lax.fori_loop(0, READ // RAISE_UNROLL, planes, acc)

    zeros = jnp.zeros((SUBLANES, LANES), jnp.int32)
    parts = lax.fori_loop(0, chunks, body, [zeros] * RAISE_UNROLL)
    return sum(parts[1:], parts[0])


def keep_end(field, z, inward, rows, cols, out):
    def read(dz, at):
        return field[z + 1 + dz, pl.ds(at, SUBLANES), :]

    for y in range(0, rows, SUBLANES):
        swept = swept_plane(read, rows, cols, y, (inward,))
        for column in range(cols // LANES):
            x = pl.ds(column * LANES, LANES)
            out[pl.ds(y, SUBLANES), x] = read(0, row_of(column, y, rows))
            out[pl.ds(rows + y, SUBLANES), x] = swept[column]


def raise_start_kernel(count, dist, par, flags_at, occ, field, end, total, flags, buf, fsem, sem):
    _, rows, cols = dist.shape
    total[...] = raise_planes(0, count, dist, par, flags_at, occ, field, flags, buf, fsem, sem)
    keep_end(field, 0, 1, rows, cols, end)


def raise_rest_kernel(
    start, dist, par, flags_at, occ, low, before, _, field, first, second, counts, flags, buf, high, fsem, sem
):
    depth, rows, cols = dist.shape
    total = raise_planes(
        start, depth - start, dist, par, flags_at, occ, field, flags, buf, fsem, sem
    )
    count = jnp.sum(total + before[...])
    row = lax.broadcasted_iota(jnp.int32, (SUBLANES, cols), 0)
    small = (count & (2**COUNT_BITS - 1)).astype(jnp.float32)
    large = (count >> COUNT_BITS).astype(jnp.float32)
    counts[...] = jnp.where(row == 2, small, jnp.where(row == 3, large, 0.0))
    keep_end(field, depth - 1, -1, rows, cols, high)
    odd = (lax.axis_index("gz") & 1) == 1
    for y in range(0, 2 * rows, SUBLANES):
        at = pl.ds(y, SUBLANES)
        first[at, :] = jnp.where(odd, high[at, :], low[at, :])
        second[at, :] = jnp.where(odd, low[at, :], high[at, :])
    first[pl.ds(2 * rows, SUBLANES), :] = counts[...]
    second[pl.ds(2 * rows, SUBLANES), :] = counts[...]


def raise_scratch(count, dist, par, flags, occ):
    return [
        pltpu.VMEM(flags.shape, jnp.int32),
        [pltpu.VMEM((count, *a.shape[1:]), a.dtype) for a in (dist, par, occ)],
        pltpu.SemaphoreType.DMA,
        pltpu.SemaphoreType.DMA((3, count // READ)),
    ]


def raise_start(dist, par, flags, occ, count):
    depth, rows, cols = dist.shape
    return pl.pallas_call(
        functools.partial(raise_start_kernel, count),
        name="raise_start",
        out_shape=(
            jax.ShapeDtypeStruct((depth + 2, padded_rows(rows, cols), LANES), jnp.float32),
            jax.ShapeDtypeStruct((2 * rows, cols), jnp.float32),
            jax.ShapeDtypeStruct((SUBLANES, LANES), jnp.int32),
        ),
        in_specs=[HBM] * 4,
        out_specs=(VMEM,) * 3,
        scratch_shapes=raise_scratch(count, dist, par, flags, occ),
        compiler_params=params(20),
        cost_estimate=cost(8),
    )(dist, par, flags, occ)


def raise_rest(dist, par, flags, occ, low, before, field, start):
    depth, rows, cols = dist.shape
    message = jax.ShapeDtypeStruct((2 * rows + SUBLANES, cols), jnp.float32)
    scratch = raise_scratch(depth - start, dist, par, flags, occ)
    return pl.pallas_call(
        functools.partial(raise_rest_kernel, start),
        name="raise_rest",
        out_shape=(
            jax.ShapeDtypeStruct(field.shape, jnp.float32),
            message,
            message,
            jax.ShapeDtypeStruct((SUBLANES, cols), jnp.float32),
        ),
        in_specs=[HBM] * 4 + [VMEM] * 3,
        out_specs=(VMEM,) * 4,
        input_output_aliases={6: 0},
        scratch_shapes=scratch[:2] + [pltpu.VMEM((2 * rows, cols), jnp.float32)] + scratch[2:],
        compiler_params=params(20),
        cost_estimate=cost(8),
    )(dist, par, flags, occ, low, before, field)


def sweep_once_kernel(start, count, rows, cols, field, once):
    depth = field.shape[0] - 2

    def sweep(z):
        def read(dz, at):
            return field[z + 1 + dz, pl.ds(at, SUBLANES), :]

        fill_pads(once, (z - start + 1,), rows, cols)
        for y in range(0, rows, SUBLANES):
            for column, tile in enumerate(swept_plane(read, rows, cols, y)):
                once[z - start + 1, pl.ds(row_of(column, y, rows), SUBLANES), :] = tile

    def body(group, _):
        for part in range(SWEEP_UNROLL):
            sweep(start + group * SWEEP_UNROLL + part)
        return 0

    for z in (start - 1, start + count):
        if 0 <= z < depth:
            sweep(z)
        else:
            once[z - start + 1] = jnp.full(once.shape[1:], FAR)
    lax.fori_loop(0, count // SWEEP_UNROLL, body, 0)


def sweep_once(field, start, count, rows, cols):
    return pl.pallas_call(
        functools.partial(sweep_once_kernel, start, count, rows, cols),
        out_shape=jax.ShapeDtypeStruct((count + 2, *field.shape[1:]), jnp.float32),
        in_specs=[VMEM],
        out_specs=VMEM,
        compiler_params=params(8),
        cost_estimate=cost(8),
    )(field)


def sweep_again_kernel(start, once, *refs):
    out, slab, stage, sem = refs[-4:]
    chunk, rows, cols = stage.shape[1:]
    columns = range(cols // LANES)
    count = once.shape[0] - 2
    slots = stage.shape[0]
    copies = []
    for step in range(count // chunk):
        slot = step % slots
        if step >= slots:
            copies[step - slots].wait()

        def body(group, _, step=step, slot=slot):
            for part in range(SWEEP_UNROLL):
                z = group * SWEEP_UNROLL + part
                plane = step * chunk + z

                def read(dz, at):
                    return once[plane + 1 + dz, pl.ds(at, SUBLANES), :]

                for y in range(0, rows, SUBLANES):
                    for column, tile in enumerate(swept_plane(read, rows, cols, y)):
                        stage[slot, z, pl.ds(y, SUBLANES), pl.ds(column * LANES, LANES)] = tile
                        at = plane * (rows * len(columns)) + column * rows + y
                        slab[pl.ds(pl.multiple_of(at, SUBLANES), SUBLANES), :] = tile
            return 0

        lax.fori_loop(0, chunk // SWEEP_UNROLL, body, 0)
        to = out.at[pl.ds(start + step * chunk, chunk)]
        cp = pltpu.make_async_copy(stage.at[slot], to, sem.at[slot])
        cp.start()
        copies.append(cp)
    for cp in copies[-slots:]:
        cp.wait()


def sweep_again(once, out, start, depth, rows, cols):
    count = once.shape[0] - 2
    given = [] if out is None else [out]
    return pl.pallas_call(
        functools.partial(sweep_again_kernel, start),
        out_shape=(
            jax.ShapeDtypeStruct((depth, rows, cols), jnp.float32),
            jax.ShapeDtypeStruct((count * rows * cols // LANES, LANES), jnp.float32),
        ),
        in_specs=[VMEM] + [HBM] * len(given),
        out_specs=(HBM, VMEM),
        input_output_aliases={1: 0} if given else {},
        scratch_shapes=[
            pltpu.VMEM((STORES, CHUNK, rows, cols), jnp.float32),
            pltpu.SemaphoreType.DMA((STORES,)),
        ],
        compiler_params=params(8),
        cost_estimate=cost(8),
    )(once, *given)


def corners_kernel(first, second, counts, more, low, high, total):
    rows = (first.shape[0] - SUBLANES) // 2
    odd = lax.axis_index("gz") & 1
    total[...] = counts[...] + more[...]
    low[...] = total[...]
    high[...] = total[...]
    for side in range(2):
        for out, row in ((low, 0), (high, rows - 1)):
            line = jnp.where(odd == side, first[pl.ds(row, 1), :], second[pl.ds(row, 1), :])
            out[pl.ds(side, 1), :] = line


def corners(first, second, counts, more):
    shape = jax.ShapeDtypeStruct(counts.shape, jnp.float32)
    return pl.pallas_call(
        corners_kernel,
        name="corners",
        out_shape=(shape,) * 3,
        in_specs=[VMEM] * 4,
        out_specs=(VMEM,) * 3,
        compiler_params=params(2),
        cost_estimate=cost(1),
    )(first, second, counts, more)


def patch_z_kernel(slabs, first, second, slab_low, slab_high, _, out, edges, planes, sem):
    depth, rows, cols = out.shape
    columns = range(cols // LANES)
    slab = lax.axis_index("gz")
    odd = slab & 1
    size = rows * len(columns)
    stores = []
    for side, own in enumerate((slab_low, slab_high)):
        missing = slab == (0, slabs - 1)[side]
        base = (0, own.shape[0] - 2 * size)[side]
        for away in range(2):
            plane = (away, 1 - away)[side]
            offered = (rows, 0)[away]
            for y in range(0, rows, SUBLANES):
                for column in columns:
                    x = pl.ds(column * LANES, LANES)
                    at = (pl.ds(offered + y, SUBLANES), x)
                    got = jnp.where(odd == side, first[at], second[at])
                    got = jnp.where(missing, FAR, got) + VOXEL
                    if away:
                        got = got + VOXEL
                    tile = own[pl.ds(base + plane * size + column * rows + y, SUBLANES), :]
                    planes[side, plane, pl.ds(y, SUBLANES), x] = jnp.minimum(tile, got)
        to = out.at[pl.ds((0, depth - 2)[side], 2)]
        cp = pltpu.make_async_copy(planes.at[side], to, sem.at[side])
        cp.start()
        stores.append(cp)
    for edge, row in enumerate((0, 1, rows - 2, rows - 1)):
        z = 0
        for own in (slab_low, slab_high):
            for base in range(0, own.shape[0], SUBLANES * size):
                for column in columns:
                    tile = own[pl.ds(base + column * rows + row, SUBLANES, stride=size), :]
                    edges[edge, pl.ds(z, SUBLANES), pl.ds(column * LANES, LANES)] = tile
                z += SUBLANES
        for side in range(2):
            for plane in range(2):
                at = pl.ds((0, depth - 2)[side] + plane, 1)
                edges[edge, at, :] = planes[side, plane, pl.ds(row, 1), :]
    for cp in stores:
        cp.wait()


def patch_z(first, second, slab_low, slab_high, out):
    depth, rows, cols = out.shape
    return pl.pallas_call(
        functools.partial(patch_z_kernel, lax.axis_size("gz")),
        name="patch_z",
        out_shape=(
            jax.ShapeDtypeStruct(out.shape, out.dtype),
            jax.ShapeDtypeStruct((4, depth, cols), jnp.float32),
        ),
        in_specs=[VMEM] * 4 + [HBM],
        out_specs=(HBM, VMEM),
        input_output_aliases={4: 0},
        scratch_shapes=[
            pltpu.VMEM((2, 2, rows, cols), jnp.float32),
            pltpu.SemaphoreType.DMA((2,)),
        ],
        compiler_params=params(4),
        cost_estimate=cost(1),
    )(first, second, slab_low, slab_high, out)


def patch_y_kernel(scale, slabs, edges, near0, near1, far, clow, chigh, counts, _, out, share, buf, sem):
    depth, rows, _ = out.shape
    slab = lax.axis_index("gz")
    copies = []
    odd = (lax.axis_index("gy") & 1) == 1
    for side, corner in enumerate((clow, chigh)):
        for away in range(2):
            edge = (away, 3 - away)[side]
            row = (away, rows - 1 - away)[side]
            at = 2 * side + away
            z = 0
            for face in (near0, near1):
                planes = pl.ds(z, face.shape[1])
                ours, theirs = face[1 - away], far[1 - away, planes, :]
                is_near = odd if side == 0 else jnp.logical_not(odd)
                reach = jnp.where(is_near, ours, theirs) + VOXEL
                if away:
                    reach = reach + VOXEL
                buf[at, planes, :] = jnp.minimum(edges[edge, planes, :], reach)
                z += face.shape[1]
            if not away:
                for end, z in enumerate((0, depth - 1)):
                    missing = slab == (0, slabs - 1)[end]
                    offer = jnp.where(missing, FAR, corner[pl.ds(end, 1), :])
                    line = jnp.minimum(buf[at, pl.ds(z, 1), :], offer + VOXEL + VOXEL)
                    buf[at, pl.ds(z, 1), :] = line
            cp = pltpu.make_async_copy(buf.at[at], out.at[:, row, :], sem.at[at])
            cp.start()
            copies.append(cp)
    x = pl.ds(0, LANES)
    both = (counts[:, x] + clow[:, x]).astype(jnp.int32)
    row = lax.broadcasted_iota(jnp.int32, both.shape, 0)
    both = jnp.where(row == 2, both, jnp.where(row == 3, both << COUNT_BITS, 0))
    count = jnp.sum(both, axis=0, keepdims=True)
    share[...] = count[:, :1].astype(jnp.float32) * jnp.float32(scale)
    for cp in copies:
        cp.wait()


def patch_y(scale, edges, near0, near1, far, clow, chigh, counts, out):
    depth, _, cols = out.shape
    return pl.pallas_call(
        functools.partial(patch_y_kernel, scale, lax.axis_size("gz")),
        name="patch_y",
        out_shape=(
            jax.ShapeDtypeStruct(out.shape, out.dtype),
            jax.ShapeDtypeStruct((1, 1), jnp.float32),
        ),
        in_specs=[VMEM] * 7 + [HBM],
        out_specs=(HBM, VMEM),
        input_output_aliases={7: 0},
        scratch_shapes=[pltpu.VMEM((4, depth, cols), jnp.float32), pltpu.SemaphoreType.DMA((4,))],
        compiler_params=params(8),
        cost_estimate=cost(2),
    )(edges, near0, near1, far, clow, chigh, counts, out)


def swapped(value, axis, partner):
    count = lax.axis_size(axis)
    return lax.ppermute(value, axis, [(i, partner(i) % count) for i in range(count)])


def shifted(value, axis, by):
    return swapped(value, axis, lambda i: i + by)


def on_device(distance, parent, removed, occupied):
    depth, rows, cols = distance.shape
    half = depth // 2
    slabs, columns = lax.axis_size("gz"), lax.axis_size("gy")
    tied = lax.optimization_barrier
    distance, parent, flags, occupied = (
        pltpu.with_memory_space_constraint(a, pltpu.HBM)
        for a in (distance, parent, removed.reshape(-1, LANES), occupied)
    )
    early = half + READ
    field, end, total = raise_start(distance, parent, flags, occupied, early)
    (face0,) = faces(field, 0, half, rows, cols, False)
    near0 = swapped(face0, "gy", lambda i: i ^ 1)
    field, first, second, counts = raise_rest(
        distance, parent, flags, occupied, end, total, field, early
    )
    face1, face = faces(field, half, depth - half, rows, cols, True)
    near1 = swapped(face1, "gy", lambda i: i ^ 1)
    once0 = sweep_once(field, 0, half, rows, cols)
    once1 = sweep_once(field, half, half, rows, cols)

    mask = columns // 2
    while mask > 1:
        got = swapped(counts, "gy", lambda i: i ^ mask)
        if mask == 4:
            got, once0 = tied((got, once0))
        if mask == 2:
            got, once1 = tied((got, once1))
        counts = counts + got
        mask //= 2
    counts, face = tied((counts, face))
    far = swapped(face, "gy", lambda i: i - 1 + 2 * (i % 2))

    first = first.at[2 * rows :].set(counts)
    got_first = swapped(first, "gz", lambda i: i - 1 + 2 * (i % 2))
    lowered, half0 = sweep_again(once0, None, 0, depth, rows, cols)
    got_first, half0 = tied((got_first, half0))
    counts = counts + got_first[2 * rows :]
    second = second.at[2 * rows :].set(counts)
    got_second = swapped(second, "gz", lambda i: i ^ 1)
    lowered, half1 = sweep_again(once1, lowered, half, depth, rows, cols)
    got_second, half1 = tied((got_second, half1))
    clow, chigh, counts = corners(got_first, got_second, counts, got_second[2 * rows :])
    from_low = shifted(chigh, "gy", 1)
    from_high = shifted(clow, "gy", -1)
    lowered, edges = patch_z(got_first, got_second, half0, half1, lowered)
    total = distance.size * slabs * columns
    lowered, share = patch_y(
        100.0 / total, edges, near0, near1, far, from_low, from_high, counts, lowered
    )
    return (lowered, share[0, 0])


def solution(mesh):
    slabs, columns = mesh.shape["gz"], mesh.shape["gy"]
    if slabs != 4 or columns < 8 or columns & (columns - 1):
        raise ValueError("unsupported mesh")
    placed = (P("gz", "gy", None), P("gz", "gy", None), P(), P("gz", "gy", None))
    return jax.shard_map(
        on_device, mesh=mesh, in_specs=placed, out_specs=(P("gz", "gy", None), P()), check_vma=False
    )
```

```python
import functools

import jax
import jax.numpy as jnp
from jax import lax
from jax.experimental import pallas as pl
from jax.experimental.pallas import tpu as pltpu
from jax.sharding import PartitionSpec as P


FAR = 1000000.0
VOXEL = 0.1
TRUNC = 2.0
LANES = 128
SUBLANES = 8
CHUNK = 8
READ = 8
AHEAD = 3
RAISE_UNROLL = 8
SWEEP_UNROLL = 4
STORES = 4
MIB = 2**20

HBM = pl.BlockSpec(memory_space=pltpu.HBM)
VMEM = pl.BlockSpec(memory_space=pltpu.VMEM)

COUNT_BITS = 12


def params(mib):
    return pltpu.CompilerParams(vmem_limit_bytes=mib * MIB)


def cost(mib):
    return pl.CostEstimate(flops=0, bytes_accessed=mib * MIB, transcendentals=0)


def packed_table(flags_ref):
    bits = (flags_ref[...] == 1).astype(jnp.int32)
    bits = bits << lax.broadcasted_iota(jnp.int32, bits.shape, 0)
    words = jnp.sum(bits, axis=0, keepdims=True)
    return jnp.broadcast_to(words, (SUBLANES, LANES))


PICK = lax.GatherDimensionNumbers(
    offset_dims=(),
    collapsed_slice_dims=(1,),
    start_index_map=(1,),
    operand_batching_dims=(0,),
    start_indices_batching_dims=(0,),
)


def raise_tile(words, dist, par, occ):
    lane = par & (LANES - 1)
    word = lax.gather(words, lane[..., None], PICK, (1, 1), mode="promise_in_bounds")
    cleared = (word >> (par >> 7)) & (occ ^ 1)
    raised = jnp.where(occ == 1, 0.0, jnp.where(cleared == 1, TRUNC, dist))
    return raised, cleared


def swept_tiles(centers, others):
    lane = lax.broadcasted_iota(jnp.int32, (SUBLANES, LANES), 1)
    last = len(centers) - 1
    after = [pltpu.roll(c, 1, 1) for c in centers]
    before = [pltpu.roll(c, LANES - 1, 1) for c in centers]
    swept = []
    for i, center in enumerate(centers):
        left = jnp.where(lane == 0, after[i - 1] if i else FAR, after[i])
        right = jnp.where(lane == LANES - 1, before[i + 1] if i < last else FAR, before[i])
        nearest = jnp.minimum(left, right)
        for other in others[i]:
            nearest = jnp.minimum(nearest, other)
        swept.append(jnp.minimum(center, nearest + VOXEL))
    return swept


def padded_rows(rows, cols):
    return cols // LANES * (rows + SUBLANES) + SUBLANES


def row_of(column, row, rows):
    return column * (rows + SUBLANES) + SUBLANES + row


def fill_pads(ref, at, rows, cols):
    for column in range(cols // LANES + 1):
        first = row_of(column, -SUBLANES, rows)
        ref[(*at, pl.ds(first, SUBLANES), slice(None))] = jnp.full((SUBLANES, LANES), FAR)


def swept_plane(read, rows, cols, y, beside=(-1, 1)):
    firsts = [row_of(c, y, rows) for c in range(cols // LANES)]
    centers = [read(0, f) for f in firsts]
    others = [[read(dz, f) for dz in beside] + [read(0, f - 1), read(0, f + 1)] for f in firsts]
    return swept_tiles(centers, others)


def face_tiles(field, rows, cols, row, inward, z):
    planes, height, _ = field.shape
    lines = field.reshape(planes * height, LANES)
    columns = range(cols // LANES)

    def read(column, y, dz=0):
        first = (z + 1 + dz) * height + row_of(column, y, rows)
        return lines[pl.ds(first, SUBLANES, stride=height), :]

    ends = [read(c, row) for c in columns]
    others = [(read(c, row, -1), read(c, row, 1), read(c, inward)) for c in columns]
    return ends, swept_tiles(ends, others)


def write_faces(field, rows, cols, top, start, out):
    def body(group, _):
        at = pl.ds(pl.multiple_of(group * SUBLANES, SUBLANES), SUBLANES)

        def write(row, inward):
            ends, swept = face_tiles(field, rows, cols, row, inward, start + group * SUBLANES)
            for column, (end, tile) in enumerate(zip(ends, swept)):
                x = pl.ds(column * LANES, LANES)
                out[0, at, x] = end
                out[1, at, x] = tile

        pl.when(top)(lambda: write(rows - 1, rows - 2))
        pl.when(jnp.logical_not(top))(lambda: write(0, 1))
        return 0

    lax.fori_loop(0, out.shape[1] // SUBLANES, body, 0)


def faces_kernel(start, rows, cols, field, near, *far):
    odd = (lax.axis_index("gy") & 1) == 1
    write_faces(field, rows, cols, jnp.logical_not(odd), start, near)
    for out in far:
        write_faces(field, rows, cols, odd, 0, out)


def faces(field, start, count, rows, cols, both):
    face = jax.ShapeDtypeStruct((2, count, cols), jnp.float32)
    whole = jax.ShapeDtypeStruct((2, field.shape[0] - 2, cols), jnp.float32)
    shapes = (face, whole) if both else (face,)
    return pl.pallas_call(
        functools.partial(faces_kernel, start, rows, cols),
        out_shape=shapes,
        in_specs=[VMEM],
        out_specs=(VMEM,) * len(shapes),
        compiler_params=params(8),
        cost_estimate=cost(2),
    )(field)


def raise_planes(start, count, dist, par, flags_at, occ, field, flags, buf, fsem, sem):
    _, rows, cols = dist.shape
    columns = range(cols // LANES)
    chunks = count // READ

    def reads(chunk):
        source, target = pl.ds(start + chunk * READ, READ), pl.ds(chunk * READ, READ)
        return [
            pltpu.make_async_copy(src.at[source], dst.at[target], sem.at[which, chunk])
            for which, (src, dst) in enumerate(zip((dist, par, occ), buf))
        ]

    table_in = pltpu.make_async_copy(flags_at, flags, fsem)
    table_in.start()
    for chunk in range(min(AHEAD, chunks)):
        for cp in reads(chunk):
            cp.start()
    for z in (0, field.shape[0] - 1):
        if start < z <= start + count + 1 or z == start == 0:
            field[z] = jnp.full(field.shape[1:], FAR)
    table_in.wait()
    table = packed_table(flags)

    def body(chunk, acc):
        @pl.when(chunk + AHEAD < chunks)
        def _():
            for cp in reads(chunk + AHEAD):
                cp.start()

        for cp in reads(chunk):
            cp.wait()

        def planes(group, acc):
            for part in range(RAISE_UNROLL):
                z = chunk * READ + group * RAISE_UNROLL + part
                fill_pads(field, (start + z + 1,), rows, cols)
                for y in range(0, rows, SUBLANES):
                    for column in columns:
                        at = (z, pl.ds(y, SUBLANES), pl.ds(column * LANES, LANES))
                        tile, cleared = raise_tile(table, *(b[at] for b in buf))
                        to = pl.ds(row_of(column, y, rows), SUBLANES)
                        field[start + z + 1, to, :] = tile
                        acc[part] = acc[part] + cleared
            return acc

        return lax.fori_loop(0, READ // RAISE_UNROLL, planes, acc)

    zeros = jnp.zeros((SUBLANES, LANES), jnp.int32)
    parts = lax.fori_loop(0, chunks, body, [zeros] * RAISE_UNROLL)
    return sum(parts[1:], parts[0])


def keep_end(field, z, inward, rows, cols, out):
    def read(dz, at):
        return field[z + 1 + dz, pl.ds(at, SUBLANES), :]

    for y in range(0, rows, SUBLANES):
        swept = swept_plane(read, rows, cols, y, (inward,))
        for column in range(cols // LANES):
            x = pl.ds(column * LANES, LANES)
            out[pl.ds(y, SUBLANES), x] = read(0, row_of(column, y, rows))
            out[pl.ds(rows + y, SUBLANES), x] = swept[column]


def raise_start_kernel(count, dist, par, flags_at, occ, field, end, total, flags, buf, fsem, sem):
    _, rows, cols = dist.shape
    total[...] = raise_planes(0, count, dist, par, flags_at, occ, field, flags, buf, fsem, sem)
    keep_end(field, 0, 1, rows, cols, end)


def raise_rest_kernel(
    start, dist, par, flags_at, occ, low, before, _, field, first, second, counts, flags, buf, high, fsem, sem
):
    depth, rows, cols = dist.shape
    total = raise_planes(
        start, depth - start, dist, par, flags_at, occ, field, flags, buf, fsem, sem
    )
    count = jnp.sum(total + before[...])
    row = lax.broadcasted_iota(jnp.int32, (SUBLANES, cols), 0)
    small = (count & (2**COUNT_BITS - 1)).astype(jnp.float32)
    large = (count >> COUNT_BITS).astype(jnp.float32)
    counts[...] = jnp.where(row == 2, small, jnp.where(row == 3, large, 0.0))
    keep_end(field, depth - 1, -1, rows, cols, high)
    odd = (lax.axis_index("gz") & 1) == 1
    for y in range(0, 2 * rows, SUBLANES):
        at = pl.ds(y, SUBLANES)
        first[at, :] = jnp.where(odd, high[at, :], low[at, :])
        second[at, :] = jnp.where(odd, low[at, :], high[at, :])
    first[pl.ds(2 * rows, SUBLANES), :] = counts[...]
    second[pl.ds(2 * rows, SUBLANES), :] = counts[...]


def raise_scratch(count, dist, par, flags, occ):
    return [
        pltpu.VMEM(flags.shape, jnp.int32),
        [pltpu.VMEM((count, *a.shape[1:]), a.dtype) for a in (dist, par, occ)],
        pltpu.SemaphoreType.DMA,
        pltpu.SemaphoreType.DMA((3, count // READ)),
    ]


def raise_start(dist, par, flags, occ, count):
    depth, rows, cols = dist.shape
    return pl.pallas_call(
        functools.partial(raise_start_kernel, count),
        name="raise_start",
        out_shape=(
            jax.ShapeDtypeStruct((depth + 2, padded_rows(rows, cols), LANES), jnp.float32),
            jax.ShapeDtypeStruct((2 * rows, cols), jnp.float32),
            jax.ShapeDtypeStruct((SUBLANES, LANES), jnp.int32),
        ),
        in_specs=[HBM] * 4,
        out_specs=(VMEM,) * 3,
        scratch_shapes=raise_scratch(count, dist, par, flags, occ),
        compiler_params=params(20),
        cost_estimate=cost(8),
    )(dist, par, flags, occ)


def raise_rest(dist, par, flags, occ, low, before, field, start):
    depth, rows, cols = dist.shape
    message = jax.ShapeDtypeStruct((2 * rows + SUBLANES, cols), jnp.float32)
    scratch = raise_scratch(depth - start, dist, par, flags, occ)
    return pl.pallas_call(
        functools.partial(raise_rest_kernel, start),
        name="raise_rest",
        out_shape=(
            jax.ShapeDtypeStruct(field.shape, jnp.float32),
            message,
            message,
            jax.ShapeDtypeStruct((SUBLANES, cols), jnp.float32),
        ),
        in_specs=[HBM] * 4 + [VMEM] * 3,
        out_specs=(VMEM,) * 4,
        input_output_aliases={6: 0},
        scratch_shapes=scratch[:2] + [pltpu.VMEM((2 * rows, cols), jnp.float32)] + scratch[2:],
        compiler_params=params(20),
        cost_estimate=cost(8),
    )(dist, par, flags, occ, low, before, field)


def sweep_once_kernel(start, count, rows, cols, field, once):
    depth = field.shape[0] - 2

    def sweep(z):
        def read(dz, at):
            return field[z + 1 + dz, pl.ds(at, SUBLANES), :]

        fill_pads(once, (z - start + 1,), rows, cols)
        for y in range(0, rows, SUBLANES):
            for column, tile in enumerate(swept_plane(read, rows, cols, y)):
                once[z - start + 1, pl.ds(row_of(column, y, rows), SUBLANES), :] = tile

    def body(group, _):
        for part in range(SWEEP_UNROLL):
            sweep(start + group * SWEEP_UNROLL + part)
        return 0

    for z in (start - 1, start + count):
        if 0 <= z < depth:
            sweep(z)
        else:
            once[z - start + 1] = jnp.full(once.shape[1:], FAR)
    lax.fori_loop(0, count // SWEEP_UNROLL, body, 0)


def sweep_once(field, start, count, rows, cols):
    return pl.pallas_call(
        functools.partial(sweep_once_kernel, start, count, rows, cols),
        out_shape=jax.ShapeDtypeStruct((count + 2, *field.shape[1:]), jnp.float32),
        in_specs=[VMEM],
        out_specs=VMEM,
        compiler_params=params(8),
        cost_estimate=cost(8),
    )(field)


def sweep_again_kernel(start, once, *refs):
    out, slab, stage, sem = refs[-4:]
    chunk, rows, cols = stage.shape[1:]
    columns = range(cols // LANES)
    count = once.shape[0] - 2
    slots = stage.shape[0]
    copies = []
    for step in range(count // chunk):
        slot = step % slots
        if step >= slots:
            copies[step - slots].wait()

        def body(group, _, step=step, slot=slot):
            for part in range(SWEEP_UNROLL):
                z = group * SWEEP_UNROLL + part
                plane = step * chunk + z

                def read(dz, at):
                    return once[plane + 1 + dz, pl.ds(at, SUBLANES), :]

                for y in range(0, rows, SUBLANES):
                    for column, tile in enumerate(swept_plane(read, rows, cols, y)):
                        stage[slot, z, pl.ds(y, SUBLANES), pl.ds(column * LANES, LANES)] = tile
                        at = plane * (rows * len(columns)) + column * rows + y
                        slab[pl.ds(pl.multiple_of(at, SUBLANES), SUBLANES), :] = tile
            return 0

        lax.fori_loop(0, chunk // SWEEP_UNROLL, body, 0)
        to = out.at[pl.ds(start + step * chunk, chunk)]
        cp = pltpu.make_async_copy(stage.at[slot], to, sem.at[slot])
        cp.start()
        copies.append(cp)
    for cp in copies[-slots:]:
        cp.wait()


def sweep_again(once, out, start, depth, rows, cols):
    count = once.shape[0] - 2
    given = [] if out is None else [out]
    return pl.pallas_call(
        functools.partial(sweep_again_kernel, start),
        out_shape=(
            jax.ShapeDtypeStruct((depth, rows, cols), jnp.float32),
            jax.ShapeDtypeStruct((count * rows * cols // LANES, LANES), jnp.float32),
        ),
        in_specs=[VMEM] + [HBM] * len(given),
        out_specs=(HBM, VMEM),
        input_output_aliases={1: 0} if given else {},
        scratch_shapes=[
            pltpu.VMEM((STORES, CHUNK, rows, cols), jnp.float32),
            pltpu.SemaphoreType.DMA((STORES,)),
        ],
        compiler_params=params(8),
        cost_estimate=cost(8),
    )(once, *given)


def corners_kernel(first, second, counts, more, low, high, total):
    rows = (first.shape[0] - SUBLANES) // 2
    odd = lax.axis_index("gz") & 1
    total[...] = counts[...] + more[...]
    low[...] = total[...]
    high[...] = total[...]
    for side in range(2):
        for out, row in ((low, 0), (high, rows - 1)):
            line = jnp.where(odd == side, first[pl.ds(row, 1), :], second[pl.ds(row, 1), :])
            out[pl.ds(side, 1), :] = line


def corners(first, second, counts, more):
    shape = jax.ShapeDtypeStruct(counts.shape, jnp.float32)
    return pl.pallas_call(
        corners_kernel,
        name="corners",
        out_shape=(shape,) * 3,
        in_specs=[VMEM] * 4,
        out_specs=(VMEM,) * 3,
        compiler_params=params(2),
        cost_estimate=cost(1),
    )(first, second, counts, more)


def patch_z_kernel(slabs, first, second, slab_low, slab_high, _, out, edges, planes, sem):
    depth, rows, cols = out.shape
    columns = range(cols // LANES)
    slab = lax.axis_index("gz")
    odd = slab & 1
    size = rows * len(columns)
    stores = []
    for side, own in enumerate((slab_low, slab_high)):
        missing = slab == (0, slabs - 1)[side]
        base = (0, own.shape[0] - 2 * size)[side]
        for away in range(2):
            plane = (away, 1 - away)[side]
            offered = (rows, 0)[away]
            for y in range(0, rows, SUBLANES):
                for column in columns:
                    x = pl.ds(column * LANES, LANES)
                    at = (pl.ds(offered + y, SUBLANES), x)
                    got = jnp.where(odd == side, first[at], second[at])
                    got = jnp.where(missing, FAR, got) + VOXEL
                    if away:
                        got = got + VOXEL
                    tile = own[pl.ds(base + plane * size + column * rows + y, SUBLANES), :]
                    planes[side, plane, pl.ds(y, SUBLANES), x] = jnp.minimum(tile, got)
        to = out.at[pl.ds((0, depth - 2)[side], 2)]
        cp = pltpu.make_async_copy(planes.at[side], to, sem.at[side])
        cp.start()
        stores.append(cp)
    for edge, row in enumerate((0, 1, rows - 2, rows - 1)):
        z = 0
        for own in (slab_low, slab_high):
            for base in range(0, own.shape[0], SUBLANES * size):
                for column in columns:
                    tile = own[pl.ds(base + column * rows + row, SUBLANES, stride=size), :]
                    edges[edge, pl.ds(z, SUBLANES), pl.ds(column * LANES, LANES)] = tile
                z += SUBLANES
        for side in range(2):
            for plane in range(2):
                at = pl.ds((0, depth - 2)[side] + plane, 1)
                edges[edge, at, :] = planes[side, plane, pl.ds(row, 1), :]
    for cp in stores:
        cp.wait()


def patch_z(first, second, slab_low, slab_high, out):
    depth, rows, cols = out.shape
    return pl.pallas_call(
        functools.partial(patch_z_kernel, lax.axis_size("gz")),
        name="patch_z",
        out_shape=(
            jax.ShapeDtypeStruct(out.shape, out.dtype),
            jax.ShapeDtypeStruct((4, depth, cols), jnp.float32),
        ),
        in_specs=[VMEM] * 4 + [HBM],
        out_specs=(HBM, VMEM),
        input_output_aliases={4: 0},
        scratch_shapes=[
            pltpu.VMEM((2, 2, rows, cols), jnp.float32),
            pltpu.SemaphoreType.DMA((2,)),
        ],
        compiler_params=params(4),
        cost_estimate=cost(1),
    )(first, second, slab_low, slab_high, out)


def merge_rows(away, edges, faces, corner, missing, buf):
    z = 0
    for face, first in faces:
        planes = pl.ds(z, buf.shape[0] // len(faces))
        reach = face[1 - away, pl.ds(first, planes.size), :] + VOXEL
        if away:
            reach = reach + VOXEL
        buf[planes, :] = jnp.minimum(edges[planes, :], reach)
        z += planes.size
    if corner is not None:
        for end, z in enumerate((0, buf.shape[0] - 1)):
            offer = jnp.where(missing[end], FAR, corner[pl.ds(end, 1), :])
            line = pl.ds(z, 1)
            buf[line, :] = jnp.minimum(buf[line, :], offer + VOXEL + VOXEL)


def sides(rows):
    return (((0, 0), (1, 1)), ((rows - 1, 3), (rows - 2, 2)))


def patch_near_kernel(edges, near0, near1, _, out, buf, sem):
    odd = lax.axis_index("gy") & 1
    for side, places in enumerate(sides(out.shape[1])):

        @pl.when(odd == 1 - side)
        def _():
            copies = []
            for away, (row, edge) in enumerate(places):
                faces = ((near0, 0), (near1, 0))
                merge_rows(away, edges.at[edge], faces, None, None, buf.at[away])
                cp = pltpu.make_async_copy(buf.at[away], out.at[:, row, :], sem.at[away])
                cp.start()
                copies.append(cp)
            for cp in copies:
                cp.wait()


def patch_far_kernel(
    scale, slabs, edges, near0, near1, far, clow, chigh, counts, _, out, share, buf, lines, sem
):
    depth, rows, _ = out.shape
    odd = lax.axis_index("gy") & 1
    slab = lax.axis_index("gz")
    missing = (slab == 0, slab == slabs - 1)
    corners = (clow, chigh)
    for side, places in enumerate(sides(rows)):

        @pl.when(odd == side)
        def _():
            copies = []
            for away, (row, edge) in enumerate(places):
                corner = None if away else corners[side]
                faces = ((far, 0), (far, depth // 2))
                merge_rows(away, edges.at[edge], faces, corner, missing, buf.at[away])
                cp = pltpu.make_async_copy(buf.at[away], out.at[:, row, :], sem.at[away])
                cp.start()
                copies.append(cp)
            row, edge = sides(rows)[1 - side][0]
            for end, face in enumerate((near0, near1)):
                z, line = ((0, 0), (depth - 1, face.shape[1] - 1))[end]
                reach = jnp.minimum(edges[edge, pl.ds(z, 1), :], face[1, pl.ds(line, 1), :] + VOXEL)
                offer = jnp.where(missing[end], FAR, corners[1 - side][pl.ds(end, 1), :])
                lines[end] = jnp.minimum(reach, offer + VOXEL + VOXEL)
                cp = pltpu.make_async_copy(
                    lines.at[end], out.at[pl.ds(z, 1), row, :], sem.at[2 + end]
                )
                cp.start()
                copies.append(cp)
            for cp in copies:
                cp.wait()

    x = pl.ds(0, LANES)
    both = (counts[:, x] + clow[:, x]).astype(jnp.int32)
    row = lax.broadcasted_iota(jnp.int32, both.shape, 0)
    both = jnp.where(row == 2, both, jnp.where(row == 3, both << COUNT_BITS, 0))
    count = jnp.sum(both, axis=0, keepdims=True)
    share[...] = count[:, :1].astype(jnp.float32) * jnp.float32(scale)


def patch_near(edges, near0, near1, out):
    depth, _, cols = out.shape
    return pl.pallas_call(
        patch_near_kernel,
        name="patch_near",
        out_shape=jax.ShapeDtypeStruct(out.shape, out.dtype),
        in_specs=[VMEM] * 3 + [HBM],
        out_specs=HBM,
        input_output_aliases={3: 0},
        scratch_shapes=[pltpu.VMEM((2, depth, cols), jnp.float32), pltpu.SemaphoreType.DMA((2,))],
        compiler_params=params(4),
        cost_estimate=cost(1),
    )(edges, near0, near1, out)


def patch_far(scale, edges, near0, near1, far, clow, chigh, counts, out):
    depth, _, cols = out.shape
    return pl.pallas_call(
        functools.partial(patch_far_kernel, scale, lax.axis_size("gz")),
        name="patch_far",
        out_shape=(
            jax.ShapeDtypeStruct(out.shape, out.dtype),
            jax.ShapeDtypeStruct((1, 1), jnp.float32),
        ),
        in_specs=[VMEM] * 7 + [HBM],
        out_specs=(HBM, VMEM),
        input_output_aliases={7: 0},
        scratch_shapes=[
            pltpu.VMEM((2, depth, cols), jnp.float32),
            pltpu.VMEM((2, 1, cols), jnp.float32),
            pltpu.SemaphoreType.DMA((4,)),
        ],
        compiler_params=params(4),
        cost_estimate=cost(1),
    )(edges, near0, near1, far, clow, chigh, counts, out)


def swapped(value, axis, partner):
    count = lax.axis_size(axis)
    return lax.ppermute(value, axis, [(i, partner(i) % count) for i in range(count)])


def shifted(value, axis, by):
    return swapped(value, axis, lambda i: i + by)


def on_device(distance, parent, removed, occupied):
    depth, rows, cols = distance.shape
    half = depth // 2
    slabs, columns = lax.axis_size("gz"), lax.axis_size("gy")
    tied = lax.optimization_barrier
    distance, parent, flags, occupied = (
        pltpu.with_memory_space_constraint(a, pltpu.HBM)
        for a in (distance, parent, removed.reshape(-1, LANES), occupied)
    )
    early = half + READ
    field, end, total = raise_start(distance, parent, flags, occupied, early)
    (face0,) = faces(field, 0, half, rows, cols, False)
    near0 = swapped(face0, "gy", lambda i: i ^ 1)
    field, first, second, counts = raise_rest(
        distance, parent, flags, occupied, end, total, field, early
    )
    face1, face = faces(field, half, depth - half, rows, cols, True)
    near1 = swapped(face1, "gy", lambda i: i ^ 1)
    once0 = sweep_once(field, 0, half, rows, cols)

    mask = columns // 2
    while mask > 1:
        got = swapped(counts, "gy", lambda i: i ^ mask)
        if mask == 2:
            got, once0 = tied((got, once0))
        counts = counts + got
        mask //= 2
    far = swapped(face, "gy", lambda i: i - 1 + 2 * (i % 2))

    first = first.at[2 * rows :].set(counts)
    got_first = swapped(first, "gz", lambda i: i - 1 + 2 * (i % 2))
    once1 = sweep_once(field, half, half, rows, cols)
    lowered, half0 = sweep_again(once0, None, 0, depth, rows, cols)
    got_first, half0 = tied((got_first, half0))
    counts = counts + got_first[2 * rows :]
    second = second.at[2 * rows :].set(counts)
    got_second = swapped(second, "gz", lambda i: i ^ 1)
    lowered, half1 = sweep_again(once1, lowered, half, depth, rows, cols)
    got_second, half1 = tied((got_second, half1))
    clow, chigh, counts = corners(got_first, got_second, counts, got_second[2 * rows :])
    from_low = shifted(chigh, "gy", 1)
    from_high = shifted(clow, "gy", -1)
    lowered, edges = patch_z(got_first, got_second, half0, half1, lowered)
    total = distance.size * slabs * columns
    lowered = patch_near(edges, near0, near1, lowered)
    lowered, share = patch_far(
        100.0 / total, edges, near0, near1, far, from_low, from_high, counts, lowered
    )
    return (lowered, share[0, 0])


def solution(mesh):
    slabs, columns = mesh.shape["gz"], mesh.shape["gy"]
    if slabs != 4 or columns < 8 or columns & (columns - 1):
        raise ValueError("unsupported mesh")
    placed = (P("gz", "gy", None), P("gz", "gy", None), P(), P("gz", "gy", None))
    return jax.shard_map(
        on_device, mesh=mesh, in_specs=placed, out_specs=(P("gz", "gy", None), P()), check_vma=False
    )
```

```python
import functools

import jax
import jax.numpy as jnp
from jax import lax
from jax.experimental import pallas as pl
from jax.experimental.pallas import tpu as pltpu
from jax.sharding import PartitionSpec as P


FAR = 1000000.0
VOXEL = 0.1
TRUNC = 2.0
LANES = 128
SUBLANES = 8
CHUNK = 8
READ = 8
AHEAD = 3
RAISE_UNROLL = 8
SWEEP_UNROLL = 4
STORES = 4
MIB = 2**20

HBM = pl.BlockSpec(memory_space=pltpu.HBM)
VMEM = pl.BlockSpec(memory_space=pltpu.VMEM)

COUNT_BITS = 12


def params(mib):
    return pltpu.CompilerParams(vmem_limit_bytes=mib * MIB)


def cost(mib):
    return pl.CostEstimate(flops=0, bytes_accessed=mib * MIB, transcendentals=0)


def packed_table(flags_ref):
    bits = (flags_ref[...] == 1).astype(jnp.int32)
    bits = bits << lax.broadcasted_iota(jnp.int32, bits.shape, 0)
    words = jnp.sum(bits, axis=0, keepdims=True)
    return jnp.broadcast_to(words, (SUBLANES, LANES))


PICK = lax.GatherDimensionNumbers(
    offset_dims=(),
    collapsed_slice_dims=(1,),
    start_index_map=(1,),
    operand_batching_dims=(0,),
    start_indices_batching_dims=(0,),
)


def raise_tile(words, dist, par, occ):
    lane = par & (LANES - 1)
    word = lax.gather(words, lane[..., None], PICK, (1, 1), mode="promise_in_bounds")
    cleared = (word >> (par >> 7)) & (occ ^ 1)
    raised = jnp.where(occ == 1, 0.0, jnp.where(cleared == 1, TRUNC, dist))
    return raised, cleared


def swept_tiles(centers, others):
    lane = lax.broadcasted_iota(jnp.int32, (SUBLANES, LANES), 1)
    last = len(centers) - 1
    after = [pltpu.roll(c, 1, 1) for c in centers]
    before = [pltpu.roll(c, LANES - 1, 1) for c in centers]
    swept = []
    for i, center in enumerate(centers):
        left = jnp.where(lane == 0, after[i - 1] if i else FAR, after[i])
        right = jnp.where(lane == LANES - 1, before[i + 1] if i < last else FAR, before[i])
        nearest = jnp.minimum(left, right)
        for other in others[i]:
            nearest = jnp.minimum(nearest, other)
        swept.append(jnp.minimum(center, nearest + VOXEL))
    return swept


def padded_rows(rows, cols):
    return cols // LANES * (rows + SUBLANES) + SUBLANES


def row_of(column, row, rows):
    return column * (rows + SUBLANES) + SUBLANES + row


def fill_pads(ref, at, rows, cols):
    for column in range(cols // LANES + 1):
        first = row_of(column, -SUBLANES, rows)
        ref[(*at, pl.ds(first, SUBLANES), slice(None))] = jnp.full((SUBLANES, LANES), FAR)


def swept_plane(read, rows, cols, y, beside=(-1, 1)):
    firsts = [row_of(c, y, rows) for c in range(cols // LANES)]
    centers = [read(0, f) for f in firsts]
    others = [[read(dz, f) for dz in beside] + [read(0, f - 1), read(0, f + 1)] for f in firsts]
    return swept_tiles(centers, others)


def face_tiles(field, rows, cols, row, inward, z):
    planes, height, _ = field.shape
    lines = field.reshape(planes * height, LANES)
    columns = range(cols // LANES)

    def read(column, y, dz=0):
        first = (z + 1 + dz) * height + row_of(column, y, rows)
        return lines[pl.ds(first, SUBLANES, stride=height), :]

    ends = [read(c, row) for c in columns]
    others = [(read(c, row, -1), read(c, row, 1), read(c, inward)) for c in columns]
    return ends, swept_tiles(ends, others)


def write_faces(field, rows, cols, top, start, out):
    def body(group, _):
        at = pl.ds(pl.multiple_of(group * SUBLANES, SUBLANES), SUBLANES)

        def write(row, inward):
            ends, swept = face_tiles(field, rows, cols, row, inward, start + group * SUBLANES)
            for column, (end, tile) in enumerate(zip(ends, swept)):
                x = pl.ds(column * LANES, LANES)
                out[0, at, x] = end
                out[1, at, x] = tile

        pl.when(top)(lambda: write(rows - 1, rows - 2))
        pl.when(jnp.logical_not(top))(lambda: write(0, 1))
        return 0

    lax.fori_loop(0, out.shape[1] // SUBLANES, body, 0)


def faces_kernel(start, rows, cols, field, near, *far):
    odd = (lax.axis_index("gy") & 1) == 1
    write_faces(field, rows, cols, odd, start, near)
    for out in far:
        write_faces(field, rows, cols, jnp.logical_not(odd), 0, out)


def faces(field, start, count, rows, cols, both):
    face = jax.ShapeDtypeStruct((2, count, cols), jnp.float32)
    whole = jax.ShapeDtypeStruct((2, field.shape[0] - 2, cols), jnp.float32)
    shapes = (face, whole) if both else (face,)
    return pl.pallas_call(
        functools.partial(faces_kernel, start, rows, cols),
        out_shape=shapes,
        in_specs=[VMEM],
        out_specs=(VMEM,) * len(shapes),
        compiler_params=params(8),
        cost_estimate=cost(2),
    )(field)


def raise_planes(start, count, dist, par, flags_at, occ, field, flags, buf, fsem, sem):
    _, rows, cols = dist.shape
    columns = range(cols // LANES)
    chunks = count // READ

    def reads(chunk):
        source, target = pl.ds(start + chunk * READ, READ), pl.ds(chunk * READ, READ)
        return [
            pltpu.make_async_copy(src.at[source], dst.at[target], sem.at[which, chunk])
            for which, (src, dst) in enumerate(zip((dist, par, occ), buf))
        ]

    table_in = pltpu.make_async_copy(flags_at, flags, fsem)
    table_in.start()
    for chunk in range(min(AHEAD, chunks)):
        for cp in reads(chunk):
            cp.start()
    for z in (0, field.shape[0] - 1):
        if start < z <= start + count + 1 or z == start == 0:
            field[z] = jnp.full(field.shape[1:], FAR)
    table_in.wait()
    table = packed_table(flags)

    def body(chunk, acc):
        @pl.when(chunk + AHEAD < chunks)
        def _():
            for cp in reads(chunk + AHEAD):
                cp.start()

        for cp in reads(chunk):
            cp.wait()

        def planes(group, acc):
            for part in range(RAISE_UNROLL):
                z = chunk * READ + group * RAISE_UNROLL + part
                fill_pads(field, (start + z + 1,), rows, cols)
                for y in range(0, rows, SUBLANES):
                    for column in columns:
                        at = (z, pl.ds(y, SUBLANES), pl.ds(column * LANES, LANES))
                        tile, cleared = raise_tile(table, *(b[at] for b in buf))
                        to = pl.ds(row_of(column, y, rows), SUBLANES)
                        field[start + z + 1, to, :] = tile
                        acc[part] = acc[part] + cleared
            return acc

        return lax.fori_loop(0, READ // RAISE_UNROLL, planes, acc)

    zeros = jnp.zeros((SUBLANES, LANES), jnp.int32)
    parts = lax.fori_loop(0, chunks, body, [zeros] * RAISE_UNROLL)
    return sum(parts[1:], parts[0])


def keep_end(field, z, inward, rows, cols, out):
    def read(dz, at):
        return field[z + 1 + dz, pl.ds(at, SUBLANES), :]

    for y in range(0, rows, SUBLANES):
        swept = swept_plane(read, rows, cols, y, (inward,))
        for column in range(cols // LANES):
            x = pl.ds(column * LANES, LANES)
            out[pl.ds(y, SUBLANES), x] = read(0, row_of(column, y, rows))
            out[pl.ds(rows + y, SUBLANES), x] = swept[column]


def raise_start_kernel(count, dist, par, flags_at, occ, field, end, total, flags, buf, fsem, sem):
    _, rows, cols = dist.shape
    total[...] = raise_planes(0, count, dist, par, flags_at, occ, field, flags, buf, fsem, sem)
    keep_end(field, 0, 1, rows, cols, end)


def raise_rest_kernel(
    start, dist, par, flags_at, occ, low, before, _, field, first, second, counts, flags, buf, high, fsem, sem
):
    depth, rows, cols = dist.shape
    total = raise_planes(
        start, depth - start, dist, par, flags_at, occ, field, flags, buf, fsem, sem
    )
    count = jnp.sum(total + before[...])
    row = lax.broadcasted_iota(jnp.int32, (SUBLANES, cols), 0)
    small = (count & (2**COUNT_BITS - 1)).astype(jnp.float32)
    large = (count >> COUNT_BITS).astype(jnp.float32)
    counts[...] = jnp.where(row == 2, small, jnp.where(row == 3, large, 0.0))
    keep_end(field, depth - 1, -1, rows, cols, high)
    odd = (lax.axis_index("gz") & 1) == 1
    for y in range(0, 2 * rows, SUBLANES):
        at = pl.ds(y, SUBLANES)
        first[at, :] = jnp.where(odd, high[at, :], low[at, :])
        second[at, :] = jnp.where(odd, low[at, :], high[at, :])
    first[pl.ds(2 * rows, SUBLANES), :] = counts[...]
    second[pl.ds(2 * rows, SUBLANES), :] = counts[...]


def raise_scratch(count, dist, par, flags, occ):
    return [
        pltpu.VMEM(flags.shape, jnp.int32),
        [pltpu.VMEM((count, *a.shape[1:]), a.dtype) for a in (dist, par, occ)],
        pltpu.SemaphoreType.DMA,
        pltpu.SemaphoreType.DMA((3, count // READ)),
    ]


def raise_start(dist, par, flags, occ, count):
    depth, rows, cols = dist.shape
    return pl.pallas_call(
        functools.partial(raise_start_kernel, count),
        name="raise_start",
        out_shape=(
            jax.ShapeDtypeStruct((depth + 2, padded_rows(rows, cols), LANES), jnp.float32),
            jax.ShapeDtypeStruct((2 * rows, cols), jnp.float32),
            jax.ShapeDtypeStruct((SUBLANES, LANES), jnp.int32),
        ),
        in_specs=[HBM] * 4,
        out_specs=(VMEM,) * 3,
        scratch_shapes=raise_scratch(count, dist, par, flags, occ),
        compiler_params=params(20),
        cost_estimate=cost(8),
    )(dist, par, flags, occ)


def raise_rest(dist, par, flags, occ, low, before, field, start):
    depth, rows, cols = dist.shape
    message = jax.ShapeDtypeStruct((2 * rows + SUBLANES, cols), jnp.float32)
    scratch = raise_scratch(depth - start, dist, par, flags, occ)
    return pl.pallas_call(
        functools.partial(raise_rest_kernel, start),
        name="raise_rest",
        out_shape=(
            jax.ShapeDtypeStruct(field.shape, jnp.float32),
            message,
            message,
            jax.ShapeDtypeStruct((SUBLANES, cols), jnp.float32),
        ),
        in_specs=[HBM] * 4 + [VMEM] * 3,
        out_specs=(VMEM,) * 4,
        input_output_aliases={6: 0},
        scratch_shapes=scratch[:2] + [pltpu.VMEM((2 * rows, cols), jnp.float32)] + scratch[2:],
        compiler_params=params(20),
        cost_estimate=cost(8),
    )(dist, par, flags, occ, low, before, field)


def sweep_once_kernel(start, count, rows, cols, field, once):
    depth = field.shape[0] - 2

    def sweep(z):
        def read(dz, at):
            return field[z + 1 + dz, pl.ds(at, SUBLANES), :]

        fill_pads(once, (z - start + 1,), rows, cols)
        for y in range(0, rows, SUBLANES):
            for column, tile in enumerate(swept_plane(read, rows, cols, y)):
                once[z - start + 1, pl.ds(row_of(column, y, rows), SUBLANES), :] = tile

    def body(group, _):
        for part in range(SWEEP_UNROLL):
            sweep(start + group * SWEEP_UNROLL + part)
        return 0

    for z in (start - 1, start + count):
        if 0 <= z < depth:
            sweep(z)
        else:
            once[z - start + 1] = jnp.full(once.shape[1:], FAR)
    lax.fori_loop(0, count // SWEEP_UNROLL, body, 0)


def sweep_once(field, start, count, rows, cols):
    return pl.pallas_call(
        functools.partial(sweep_once_kernel, start, count, rows, cols),
        out_shape=jax.ShapeDtypeStruct((count + 2, *field.shape[1:]), jnp.float32),
        in_specs=[VMEM],
        out_specs=VMEM,
        compiler_params=params(8),
        cost_estimate=cost(8),
    )(field)


def sweep_again_kernel(start, once, *refs):
    out, slab, stage, sem = refs[-4:]
    chunk, rows, cols = stage.shape[1:]
    columns = range(cols // LANES)
    count = once.shape[0] - 2
    slots = stage.shape[0]
    copies = []
    for step in range(count // chunk):
        slot = step % slots
        if step >= slots:
            copies[step - slots].wait()

        def body(group, _, step=step, slot=slot):
            for part in range(SWEEP_UNROLL):
                z = group * SWEEP_UNROLL + part
                plane = step * chunk + z

                def read(dz, at):
                    return once[plane + 1 + dz, pl.ds(at, SUBLANES), :]

                for y in range(0, rows, SUBLANES):
                    for column, tile in enumerate(swept_plane(read, rows, cols, y)):
                        stage[slot, z, pl.ds(y, SUBLANES), pl.ds(column * LANES, LANES)] = tile
                        at = plane * (rows * len(columns)) + column * rows + y
                        slab[pl.ds(pl.multiple_of(at, SUBLANES), SUBLANES), :] = tile
            return 0

        lax.fori_loop(0, chunk // SWEEP_UNROLL, body, 0)
        to = out.at[pl.ds(start + step * chunk, chunk)]
        cp = pltpu.make_async_copy(stage.at[slot], to, sem.at[slot])
        cp.start()
        copies.append(cp)
    for cp in copies[-slots:]:
        cp.wait()


def sweep_again(once, out, start, depth, rows, cols):
    count = once.shape[0] - 2
    given = [] if out is None else [out]
    return pl.pallas_call(
        functools.partial(sweep_again_kernel, start),
        out_shape=(
            jax.ShapeDtypeStruct((depth, rows, cols), jnp.float32),
            jax.ShapeDtypeStruct((count * rows * cols // LANES, LANES), jnp.float32),
        ),
        in_specs=[VMEM] + [HBM] * len(given),
        out_specs=(HBM, VMEM),
        input_output_aliases={1: 0} if given else {},
        scratch_shapes=[
            pltpu.VMEM((STORES, CHUNK, rows, cols), jnp.float32),
            pltpu.SemaphoreType.DMA((STORES,)),
        ],
        compiler_params=params(8),
        cost_estimate=cost(8),
    )(once, *given)


def corners_kernel(first, second, counts, more, low, high, total):
    rows = (first.shape[0] - SUBLANES) // 2
    odd = lax.axis_index("gz") & 1
    total[...] = counts[...] + more[...]
    low[...] = total[...]
    high[...] = total[...]
    for side in range(2):
        for out, row in ((low, 0), (high, rows - 1)):
            line = jnp.where(odd == side, first[pl.ds(row, 1), :], second[pl.ds(row, 1), :])
            out[pl.ds(side, 1), :] = line


def corners(first, second, counts, more):
    shape = jax.ShapeDtypeStruct(counts.shape, jnp.float32)
    return pl.pallas_call(
        corners_kernel,
        name="corners",
        out_shape=(shape,) * 3,
        in_specs=[VMEM] * 4,
        out_specs=(VMEM,) * 3,
        compiler_params=params(2),
        cost_estimate=cost(1),
    )(first, second, counts, more)


def patch_z_kernel(slabs, first, second, slab_low, slab_high, _, out, edges, planes, sem):
    depth, rows, cols = out.shape
    columns = range(cols // LANES)
    slab = lax.axis_index("gz")
    odd = slab & 1
    size = rows * len(columns)
    stores = []
    for side, own in enumerate((slab_low, slab_high)):
        missing = slab == (0, slabs - 1)[side]
        base = (0, own.shape[0] - 2 * size)[side]
        for away in range(2):
            plane = (away, 1 - away)[side]
            offered = (rows, 0)[away]
            for y in range(0, rows, SUBLANES):
                for column in columns:
                    x = pl.ds(column * LANES, LANES)
                    at = (pl.ds(offered + y, SUBLANES), x)
                    got = jnp.where(odd == side, first[at], second[at])
                    got = jnp.where(missing, FAR, got) + VOXEL
                    if away:
                        got = got + VOXEL
                    tile = own[pl.ds(base + plane * size + column * rows + y, SUBLANES), :]
                    planes[side, plane, pl.ds(y, SUBLANES), x] = jnp.minimum(tile, got)
        to = out.at[pl.ds((0, depth - 2)[side], 2)]
        cp = pltpu.make_async_copy(planes.at[side], to, sem.at[side])
        cp.start()
        stores.append(cp)
    for edge, row in enumerate((0, 1, rows - 2, rows - 1)):
        z = 0
        for own in (slab_low, slab_high):
            for base in range(0, own.shape[0], SUBLANES * size):
                for column in columns:
                    tile = own[pl.ds(base + column * rows + row, SUBLANES, stride=size), :]
                    edges[edge, pl.ds(z, SUBLANES), pl.ds(column * LANES, LANES)] = tile
                z += SUBLANES
        for side in range(2):
            for plane in range(2):
                at = pl.ds((0, depth - 2)[side] + plane, 1)
                edges[edge, at, :] = planes[side, plane, pl.ds(row, 1), :]
    for cp in stores:
        cp.wait()


def patch_z(first, second, slab_low, slab_high, out):
    depth, rows, cols = out.shape
    return pl.pallas_call(
        functools.partial(patch_z_kernel, lax.axis_size("gz")),
        name="patch_z",
        out_shape=(
            jax.ShapeDtypeStruct(out.shape, out.dtype),
            jax.ShapeDtypeStruct((4, depth, cols), jnp.float32),
        ),
        in_specs=[VMEM] * 4 + [HBM],
        out_specs=(HBM, VMEM),
        input_output_aliases={4: 0},
        scratch_shapes=[
            pltpu.VMEM((2, 2, rows, cols), jnp.float32),
            pltpu.SemaphoreType.DMA((2,)),
        ],
        compiler_params=params(4),
        cost_estimate=cost(1),
    )(first, second, slab_low, slab_high, out)


def merge_rows(away, edges, faces, corner, missing, buf):
    z = 0
    for face, first in faces:
        planes = pl.ds(z, buf.shape[0] // len(faces))
        reach = face[1 - away, pl.ds(first, planes.size), :] + VOXEL
        if away:
            reach = reach + VOXEL
        buf[planes, :] = jnp.minimum(edges[planes, :], reach)
        z += planes.size
    if corner is not None:
        for end, z in enumerate((0, buf.shape[0] - 1)):
            offer = jnp.where(missing[end], FAR, corner[pl.ds(end, 1), :])
            line = pl.ds(z, 1)
            buf[line, :] = jnp.minimum(buf[line, :], offer + VOXEL + VOXEL)


def sides(rows):
    return (((0, 0), (1, 1)), ((rows - 1, 3), (rows - 2, 2)))


def patch_near_kernel(edges, near0, near1, _, out, buf, sem):
    odd = lax.axis_index("gy") & 1
    for side, places in enumerate(sides(out.shape[1])):

        @pl.when(odd == side)
        def _():
            copies = []
            for away, (row, edge) in enumerate(places):
                faces = ((near0, 0), (near1, 0))
                merge_rows(away, edges.at[edge], faces, None, None, buf.at[away])
                cp = pltpu.make_async_copy(buf.at[away], out.at[:, row, :], sem.at[away])
                cp.start()
                copies.append(cp)
            for cp in copies:
                cp.wait()


def patch_far_kernel(
    scale, slabs, edges, near0, near1, far, clow, chigh, counts, _, out, share, buf, lines, sem
):
    depth, rows, _ = out.shape
    odd = lax.axis_index("gy") & 1
    slab = lax.axis_index("gz")
    missing = (slab == 0, slab == slabs - 1)
    corners = (clow, chigh)
    for side, places in enumerate(sides(rows)):

        @pl.when(odd == 1 - side)
        def _():
            copies = []
            for away, (row, edge) in enumerate(places):
                corner = None if away else corners[side]
                faces = ((far, 0), (far, depth // 2))
                merge_rows(away, edges.at[edge], faces, corner, missing, buf.at[away])
                cp = pltpu.make_async_copy(buf.at[away], out.at[:, row, :], sem.at[away])
                cp.start()
                copies.append(cp)
            row, edge = sides(rows)[1 - side][0]
            for end, face in enumerate((near0, near1)):
                z, line = ((0, 0), (depth - 1, face.shape[1] - 1))[end]
                reach = jnp.minimum(edges[edge, pl.ds(z, 1), :], face[1, pl.ds(line, 1), :] + VOXEL)
                offer = jnp.where(missing[end], FAR, corners[1 - side][pl.ds(end, 1), :])
                lines[end] = jnp.minimum(reach, offer + VOXEL + VOXEL)
                cp = pltpu.make_async_copy(
                    lines.at[end], out.at[pl.ds(z, 1), row, :], sem.at[2 + end]
                )
                cp.start()
                copies.append(cp)
            for cp in copies:
                cp.wait()

    x = pl.ds(0, LANES)
    both = (counts[:, x] + clow[:, x]).astype(jnp.int32)
    row = lax.broadcasted_iota(jnp.int32, both.shape, 0)
    both = jnp.where(row == 2, both, jnp.where(row == 3, both << COUNT_BITS, 0))
    count = jnp.sum(both, axis=0, keepdims=True)
    share[...] = count[:, :1].astype(jnp.float32) * jnp.float32(scale)


def patch_near(edges, near0, near1, out):
    depth, _, cols = out.shape
    return pl.pallas_call(
        patch_near_kernel,
        name="patch_near",
        out_shape=jax.ShapeDtypeStruct(out.shape, out.dtype),
        in_specs=[VMEM] * 3 + [HBM],
        out_specs=HBM,
        input_output_aliases={3: 0},
        scratch_shapes=[pltpu.VMEM((2, depth, cols), jnp.float32), pltpu.SemaphoreType.DMA((2,))],
        compiler_params=params(4),
        cost_estimate=cost(1),
    )(edges, near0, near1, out)


def patch_far(scale, edges, near0, near1, far, clow, chigh, counts, out):
    depth, _, cols = out.shape
    return pl.pallas_call(
        functools.partial(patch_far_kernel, scale, lax.axis_size("gz")),
        name="patch_far",
        out_shape=(
            jax.ShapeDtypeStruct(out.shape, out.dtype),
            jax.ShapeDtypeStruct((1, 1), jnp.float32),
        ),
        in_specs=[VMEM] * 7 + [HBM],
        out_specs=(HBM, VMEM),
        input_output_aliases={7: 0},
        scratch_shapes=[
            pltpu.VMEM((2, depth, cols), jnp.float32),
            pltpu.VMEM((2, 1, cols), jnp.float32),
            pltpu.SemaphoreType.DMA((4,)),
        ],
        compiler_params=params(4),
        cost_estimate=cost(1),
    )(edges, near0, near1, far, clow, chigh, counts, out)


def swapped(value, axis, partner):
    count = lax.axis_size(axis)
    return lax.ppermute(value, axis, [(i, partner(i) % count) for i in range(count)])


def after_odd(i):
    return i - 1 + 2 * (i % 2)


def shifted(value, axis, by):
    return swapped(value, axis, lambda i: i + by)


def on_device(distance, parent, removed, occupied):
    depth, rows, cols = distance.shape
    half = depth // 2
    slabs, columns = lax.axis_size("gz"), lax.axis_size("gy")
    tied = lax.optimization_barrier
    distance, parent, flags, occupied = (
        pltpu.with_memory_space_constraint(a, pltpu.HBM)
        for a in (distance, parent, removed.reshape(-1, LANES), occupied)
    )
    early = half + READ
    field, end, total = raise_start(distance, parent, flags, occupied, early)
    (face0,) = faces(field, 0, half, rows, cols, False)
    near0 = swapped(face0, "gy", after_odd)
    field, first, second, counts = raise_rest(
        distance, parent, flags, occupied, end, total, field, early
    )

    got_first = swapped(first, "gz", after_odd)
    face1, face = faces(field, half, depth - half, rows, cols, True)
    near1 = swapped(face1, "gy", after_odd)
    far = swapped(face, "gy", lambda i: i ^ 1)
    once0 = sweep_once(field, 0, half, rows, cols)
    got_first, once0 = tied((got_first, once0))
    second = second.at[2 * rows :].add(got_first[2 * rows :])
    got_second = swapped(second, "gz", lambda i: i ^ 1)
    once1 = sweep_once(field, half, half, rows, cols)
    got_second, once1 = tied((got_second, once1))
    counts = second[2 * rows :] + got_second[2 * rows :]
    lowered, half0 = sweep_again(once0, None, 0, depth, rows, cols)
    lowered, half1 = sweep_again(once1, lowered, half, depth, rows, cols)

    more = jnp.zeros_like(counts)
    mask = columns // 2
    while mask > 1:
        counts = counts + more
        more = swapped(counts, "gy", lambda i: i ^ mask)
        if mask == 4:
            more, half0 = tied((more, half0))
        if mask == 2:
            more, half1 = tied((more, half1))
        mask //= 2
    clow, chigh, counts = corners(got_first, got_second, counts, more)
    from_low = shifted(chigh, "gy", 1)
    from_high = shifted(clow, "gy", -1)
    lowered, edges = patch_z(got_first, got_second, half0, half1, lowered)
    total = distance.size * slabs * columns
    lowered = patch_near(edges, near0, near1, lowered)
    lowered, share = patch_far(
        100.0 / total, edges, near0, near1, far, from_low, from_high, counts, lowered
    )
    return (lowered, share[0, 0])


def solution(mesh):
    slabs, columns = mesh.shape["gz"], mesh.shape["gy"]
    if slabs != 4 or columns < 8 or columns & (columns - 1):
        raise ValueError("unsupported mesh")
    placed = (P("gz", "gy", None), P("gz", "gy", None), P(), P("gz", "gy", None))
    return jax.shard_map(
        on_device, mesh=mesh, in_specs=placed, out_specs=(P("gz", "gy", None), P()), check_vma=False
    )
```

```python
import functools

import jax
import jax.numpy as jnp
from jax import lax
from jax.experimental import pallas as pl
from jax.experimental.pallas import tpu as pltpu
from jax.sharding import PartitionSpec as P


FAR = 1000000.0
VOXEL = 0.1
TRUNC = 2.0
LANES = 128
SUBLANES = 8
CHUNK = 8
READ = 8
AHEAD = 3
RAISE_UNROLL = 8
SWEEP_UNROLL = 8
MIB = 2**20

HBM = pl.BlockSpec(memory_space=pltpu.HBM)
VMEM = pl.BlockSpec(memory_space=pltpu.VMEM)

COUNT_BITS = 12


def params(mib):
    return pltpu.CompilerParams(vmem_limit_bytes=mib * MIB)


def cost(mib):
    return pl.CostEstimate(flops=0, bytes_accessed=mib * MIB, transcendentals=0)


def packed_table(flags_ref):
    bits = (flags_ref[...] == 1).astype(jnp.int32)
    bits = bits << lax.broadcasted_iota(jnp.int32, bits.shape, 0)
    words = jnp.sum(bits, axis=0, keepdims=True)
    return jnp.broadcast_to(words, (SUBLANES, LANES))


PICK = lax.GatherDimensionNumbers(
    offset_dims=(),
    collapsed_slice_dims=(1,),
    start_index_map=(1,),
    operand_batching_dims=(0,),
    start_indices_batching_dims=(0,),
)


def raise_tile(words, dist, par, occ):
    lane = par & (LANES - 1)
    word = lax.gather(words, lane[..., None], PICK, (1, 1), mode="promise_in_bounds")
    cleared = (word >> (par >> 7)) & (occ ^ 1)
    raised = jnp.where(occ == 1, 0.0, jnp.where(cleared == 1, TRUNC, dist))
    return raised, cleared


def swept_tiles(centers, others):
    lane = lax.broadcasted_iota(jnp.int32, (SUBLANES, LANES), 1)
    last = len(centers) - 1
    after = [pltpu.roll(c, 1, 1) for c in centers]
    before = [pltpu.roll(c, LANES - 1, 1) for c in centers]
    swept = []
    for i, center in enumerate(centers):
        left = jnp.where(lane == 0, after[i - 1] if i else FAR, after[i])
        right = jnp.where(lane == LANES - 1, before[i + 1] if i < last else FAR, before[i])
        nearest = jnp.minimum(left, right)
        for other in others[i]:
            nearest = jnp.minimum(nearest, other)
        swept.append(jnp.minimum(center, nearest + VOXEL))
    return swept


def padded_rows(rows, cols):
    return cols // LANES * (rows + SUBLANES) + SUBLANES


def row_of(column, row, rows):
    return column * (rows + SUBLANES) + SUBLANES + row


def fill_pads(ref, at, rows, cols):
    for column in range(cols // LANES + 1):
        first = row_of(column, -SUBLANES, rows)
        ref[(*at, pl.ds(first, SUBLANES), slice(None))] = jnp.full((SUBLANES, LANES), FAR)


def swept_plane(read, rows, cols, y, beside=(-1, 1)):
    firsts = [row_of(c, y, rows) for c in range(cols // LANES)]
    centers = [read(0, f) for f in firsts]
    others = [[read(dz, f) for dz in beside] + [read(0, f - 1), read(0, f + 1)] for f in firsts]
    return swept_tiles(centers, others)


def face_tiles(field, rows, cols, row, inward, z):
    planes, height, _ = field.shape
    lines = field.reshape(planes * height, LANES)
    columns = range(cols // LANES)

    def read(column, y, dz=0):
        first = (z + 1 + dz) * height + row_of(column, y, rows)
        return lines[pl.ds(first, SUBLANES, stride=height), :]

    ends = [read(c, row) for c in columns]
    others = [(read(c, row, -1), read(c, row, 1), read(c, inward)) for c in columns]
    return ends, swept_tiles(ends, others)


def write_faces(field, rows, cols, top, start, out):
    def body(group, _):
        at = pl.ds(pl.multiple_of(group * SUBLANES, SUBLANES), SUBLANES)

        def write(row, inward):
            ends, swept = face_tiles(field, rows, cols, row, inward, start + group * SUBLANES)
            for column, (end, tile) in enumerate(zip(ends, swept)):
                x = pl.ds(column * LANES, LANES)
                out[0, at, x] = end
                out[1, at, x] = tile

        pl.when(top)(lambda: write(rows - 1, rows - 2))
        pl.when(jnp.logical_not(top))(lambda: write(0, 1))
        return 0

    lax.fori_loop(0, out.shape[1] // SUBLANES, body, 0)


def faces_kernel(rows, cols, toward_odd, field, out):
    odd = lax.axis_index("gy") & 1
    write_faces(field, rows, cols, odd == toward_odd, 0, out)


def faces(field, rows, cols, toward_odd):
    return pl.pallas_call(
        functools.partial(faces_kernel, rows, cols, toward_odd),
        out_shape=jax.ShapeDtypeStruct((2, field.shape[0] - 2, cols), jnp.float32),
        in_specs=[VMEM],
        out_specs=VMEM,
        compiler_params=params(4),
        cost_estimate=cost(2),
    )(field)


def raise_planes(start, count, dist, par, flags_at, occ, field, flags, buf, fsem, sem):
    _, rows, cols = dist.shape
    columns = range(cols // LANES)
    chunks = count // READ

    def reads(chunk):
        source, target = pl.ds(start + chunk * READ, READ), pl.ds(chunk * READ, READ)
        return [
            pltpu.make_async_copy(src.at[source], dst.at[target], sem.at[which, chunk])
            for which, (src, dst) in enumerate(zip((dist, par, occ), buf))
        ]

    table_in = pltpu.make_async_copy(flags_at, flags, fsem)
    table_in.start()
    for chunk in range(min(AHEAD, chunks)):
        for cp in reads(chunk):
            cp.start()
    for z in (0, field.shape[0] - 1):
        if start < z <= start + count + 1 or z == start == 0:
            field[z] = jnp.full(field.shape[1:], FAR)
    table_in.wait()
    table = packed_table(flags)

    def body(chunk, acc):
        @pl.when(chunk + AHEAD < chunks)
        def _():
            for cp in reads(chunk + AHEAD):
                cp.start()

        for cp in reads(chunk):
            cp.wait()

        def planes(group, acc):
            for part in range(RAISE_UNROLL):
                z = chunk * READ + group * RAISE_UNROLL + part
                fill_pads(field, (start + z + 1,), rows, cols)
                for y in range(0, rows, SUBLANES):
                    for column in columns:
                        at = (z, pl.ds(y, SUBLANES), pl.ds(column * LANES, LANES))
                        tile, cleared = raise_tile(table, *(b[at] for b in buf))
                        to = pl.ds(row_of(column, y, rows), SUBLANES)
                        field[start + z + 1, to, :] = tile
                        acc[part] = acc[part] + cleared
            return acc

        return lax.fori_loop(0, READ // RAISE_UNROLL, planes, acc)

    zeros = jnp.zeros((SUBLANES, LANES), jnp.int32)
    parts = lax.fori_loop(0, chunks, body, [zeros] * RAISE_UNROLL)
    return sum(parts[1:], parts[0])


def keep_end(field, z, inward, rows, cols, out):
    def read(dz, at):
        return field[z + 1 + dz, pl.ds(at, SUBLANES), :]

    for y in range(0, rows, SUBLANES):
        swept = swept_plane(read, rows, cols, y, (inward,))
        for column in range(cols // LANES):
            x = pl.ds(column * LANES, LANES)
            out[pl.ds(y, SUBLANES), x] = read(0, row_of(column, y, rows))
            out[pl.ds(rows + y, SUBLANES), x] = swept[column]


def raise_kernel(dist, par, flags_at, occ, field, first, second, flags, buf, ends, fsem, sem):
    depth, rows, cols = dist.shape
    total = raise_planes(0, depth, dist, par, flags_at, occ, field, flags, buf, fsem, sem)
    keep_end(field, 0, 1, rows, cols, ends.at[0])
    keep_end(field, depth - 1, -1, rows, cols, ends.at[1])
    count = jnp.sum(total)
    row = lax.broadcasted_iota(jnp.int32, (SUBLANES, cols), 0)
    small = (count & (2**COUNT_BITS - 1)).astype(jnp.float32)
    large = (count >> COUNT_BITS).astype(jnp.float32)
    counts = jnp.where(row == 2, small, jnp.where(row == 3, large, 0.0))
    odd = lax.axis_index("gz") & 1
    for out, side in ((first, odd), (second, 1 - odd)):
        out[pl.ds(0, 2 * rows), :] = ends[side]
        out[pl.ds(2 * rows, SUBLANES), :] = counts


def raise_scratch(count, dist, par, flags, occ):
    return [
        pltpu.VMEM(flags.shape, jnp.int32),
        [pltpu.VMEM((count, *a.shape[1:]), a.dtype) for a in (dist, par, occ)],
        pltpu.SemaphoreType.DMA,
        pltpu.SemaphoreType.DMA((3, count // READ)),
    ]


def raise_all(dist, par, flags, occ):
    depth, rows, cols = dist.shape
    message = jax.ShapeDtypeStruct((2 * rows + SUBLANES, cols), jnp.float32)
    scratch = raise_scratch(depth, dist, par, flags, occ)
    return pl.pallas_call(
        raise_kernel,
        name="raise_all",
        out_shape=(
            jax.ShapeDtypeStruct((depth + 2, padded_rows(rows, cols), LANES), jnp.float32),
            message,
            message,
        ),
        in_specs=[HBM] * 4,
        out_specs=(VMEM,) * 3,
        scratch_shapes=scratch[:2] + [pltpu.VMEM((2, 2 * rows, cols), jnp.float32)] + scratch[2:],
        compiler_params=params(20),
        cost_estimate=cost(12),
    )(dist, par, flags, occ)


def sweep_once_kernel(start, count, rows, cols, field, once):
    depth = field.shape[0] - 2

    def sweep(z):
        def read(dz, at):
            return field[z + 1 + dz, pl.ds(at, SUBLANES), :]

        fill_pads(once, (z - start + 1,), rows, cols)
        for y in range(0, rows, SUBLANES):
            for column, tile in enumerate(swept_plane(read, rows, cols, y)):
                once[z - start + 1, pl.ds(row_of(column, y, rows), SUBLANES), :] = tile

    def body(group, _):
        for part in range(SWEEP_UNROLL):
            sweep(start + group * SWEEP_UNROLL + part)
        return 0

    for z in (start - 1, start + count):
        if 0 <= z < depth:
            sweep(z)
        else:
            once[z - start + 1] = jnp.full(once.shape[1:], FAR)
    lax.fori_loop(0, count // SWEEP_UNROLL, body, 0)


def sweep_once(field, start, count, rows, cols):
    return pl.pallas_call(
        functools.partial(sweep_once_kernel, start, count, rows, cols),
        out_shape=jax.ShapeDtypeStruct((count + 2, *field.shape[1:]), jnp.float32),
        in_specs=[VMEM],
        out_specs=VMEM,
        compiler_params=params(8),
        cost_estimate=cost(8),
    )(field)


def sweep_again_planes(once, first, count, tiles, slab):
    _, rows, cols = tiles.shape
    columns = range(cols // LANES)

    def body(group, _):
        for part in range(SWEEP_UNROLL):
            plane = first + group * SWEEP_UNROLL + part

            def read(dz, at):
                return once[plane + 1 + dz, pl.ds(at, SUBLANES), :]

            for y in range(0, rows, SUBLANES):
                for column, tile in enumerate(swept_plane(read, rows, cols, y)):
                    tiles[plane, pl.ds(y, SUBLANES), pl.ds(column * LANES, LANES)] = tile
                    at = plane * (rows * len(columns)) + column * rows + y
                    slab[pl.ds(pl.multiple_of(at, SUBLANES), SUBLANES), :] = tile
        return 0

    lax.fori_loop(0, count // SWEEP_UNROLL, body, 0)


def sweep_again_low_kernel(once, tiles, slab):
    sweep_again_planes(once, 0, tiles.shape[0], tiles, slab)


def sweep_again_high_kernel(once, low, out, slab, tiles, sem):
    half = low.shape[0]
    copies = [pltpu.make_async_copy(low, out.at[pl.ds(0, half)], sem.at[0])]
    copies[0].start()
    for step, first in enumerate(range(0, tiles.shape[0], CHUNK)):
        sweep_again_planes(once, first, CHUNK, tiles, slab)
        at = pl.ds(first, CHUNK)
        to = out.at[pl.ds(half + first, CHUNK)]
        cp = pltpu.make_async_copy(tiles.at[at], to, sem.at[step + 1])
        cp.start()
        copies.append(cp)
    for cp in copies:
        cp.wait()


def sweep_again_low(once, rows, cols):
    count = once.shape[0] - 2
    return pl.pallas_call(
        sweep_again_low_kernel,
        name="sweep_again_low",
        out_shape=(
            jax.ShapeDtypeStruct((count, rows, cols), jnp.float32),
            jax.ShapeDtypeStruct((count * rows * cols // LANES, LANES), jnp.float32),
        ),
        in_specs=[VMEM],
        out_specs=(VMEM, VMEM),
        compiler_params=params(4),
        cost_estimate=cost(8),
    )(once)


def sweep_again_high(once, low):
    count = once.shape[0] - 2
    _, rows, cols = low.shape
    return pl.pallas_call(
        sweep_again_high_kernel,
        name="sweep_again_high",
        out_shape=(
            jax.ShapeDtypeStruct((low.shape[0] + count, rows, cols), jnp.float32),
            jax.ShapeDtypeStruct((count * rows * cols // LANES, LANES), jnp.float32),
        ),
        in_specs=[VMEM, VMEM],
        out_specs=(HBM, VMEM),
        scratch_shapes=[
            pltpu.VMEM((count, rows, cols), jnp.float32),
            pltpu.SemaphoreType.DMA((count // CHUNK + 1,)),
        ],
        compiler_params=params(8),
        cost_estimate=cost(8),
    )(once, low)


def corners_kernel(first, second, counts, more, low, high, total):
    rows = (first.shape[0] - SUBLANES) // 2
    odd = lax.axis_index("gz") & 1
    total[...] = counts[...] + more[...]
    low[...] = total[...]
    high[...] = total[...]
    for side in range(2):
        for out, row in ((low, 0), (high, rows - 1)):
            line = jnp.where(odd == side, first[pl.ds(row, 1), :], second[pl.ds(row, 1), :])
            out[pl.ds(side, 1), :] = line


def corners(first, second, counts, more):
    shape = jax.ShapeDtypeStruct(counts.shape, jnp.float32)
    return pl.pallas_call(
        corners_kernel,
        name="corners",
        out_shape=(shape,) * 3,
        in_specs=[VMEM] * 4,
        out_specs=(VMEM,) * 3,
        compiler_params=params(2),
        cost_estimate=cost(1),
    )(first, second, counts, more)


def patch_z_kernel(slabs, first, second, slab_low, slab_high, _, out, edges, planes, sem):
    depth, rows, cols = out.shape
    columns = range(cols // LANES)
    slab = lax.axis_index("gz")
    odd = slab & 1
    size = rows * len(columns)
    stores = []
    for side, own in enumerate((slab_low, slab_high)):
        missing = slab == (0, slabs - 1)[side]
        base = (0, own.shape[0] - 2 * size)[side]
        for away in range(2):
            plane = (away, 1 - away)[side]
            offered = (rows, 0)[away]
            for y in range(0, rows, SUBLANES):
                for column in columns:
                    x = pl.ds(column * LANES, LANES)
                    at = (pl.ds(offered + y, SUBLANES), x)
                    got = jnp.where(odd == side, first[at], second[at])
                    got = jnp.where(missing, FAR, got) + VOXEL
                    if away:
                        got = got + VOXEL
                    tile = own[pl.ds(base + plane * size + column * rows + y, SUBLANES), :]
                    planes[side, plane, pl.ds(y, SUBLANES), x] = jnp.minimum(tile, got)
        to = out.at[pl.ds((0, depth - 2)[side], 2)]
        cp = pltpu.make_async_copy(planes.at[side], to, sem.at[side])
        cp.start()
        stores.append(cp)
    for edge, row in enumerate((0, 1, rows - 2, rows - 1)):
        z = 0
        for own in (slab_low, slab_high):
            for base in range(0, own.shape[0], SUBLANES * size):
                for column in columns:
                    tile = own[pl.ds(base + column * rows + row, SUBLANES, stride=size), :]
                    edges[edge, pl.ds(z, SUBLANES), pl.ds(column * LANES, LANES)] = tile
                z += SUBLANES
        for side in range(2):
            for plane in range(2):
                at = pl.ds((0, depth - 2)[side] + plane, 1)
                edges[edge, at, :] = planes[side, plane, pl.ds(row, 1), :]
    for cp in stores:
        cp.wait()


def patch_z(first, second, slab_low, slab_high, out):
    depth, rows, cols = out.shape
    return pl.pallas_call(
        functools.partial(patch_z_kernel, lax.axis_size("gz")),
        name="patch_z",
        out_shape=(
            jax.ShapeDtypeStruct(out.shape, out.dtype),
            jax.ShapeDtypeStruct((4, depth, cols), jnp.float32),
        ),
        in_specs=[VMEM] * 4 + [HBM],
        out_specs=(HBM, VMEM),
        input_output_aliases={4: 0},
        scratch_shapes=[
            pltpu.VMEM((2, 2, rows, cols), jnp.float32),
            pltpu.SemaphoreType.DMA((2,)),
        ],
        compiler_params=params(4),
        cost_estimate=cost(1),
    )(first, second, slab_low, slab_high, out)


def merge_rows(away, edges, face, corner, missing, buf):
    reach = face[1 - away] + VOXEL
    if away:
        reach = reach + VOXEL
    buf[...] = jnp.minimum(edges[...], reach)
    if corner is not None:
        for end, z in enumerate((0, buf.shape[0] - 1)):
            offer = jnp.where(missing[end], FAR, corner[pl.ds(end, 1), :])
            line = pl.ds(z, 1)
            buf[line, :] = jnp.minimum(buf[line, :], offer + VOXEL + VOXEL)


def sides(rows):
    return (((0, 0), (1, 1)), ((rows - 1, 3), (rows - 2, 2)))


def patch_near_kernel(edges, near, _, out, buf, sem):
    odd = lax.axis_index("gy") & 1
    for side, places in enumerate(sides(out.shape[1])):

        @pl.when(odd == side)
        def _():
            copies = []
            for away, (row, edge) in enumerate(places):
                merge_rows(away, edges.at[edge], near, None, None, buf.at[away])
                cp = pltpu.make_async_copy(buf.at[away], out.at[:, row, :], sem.at[away])
                cp.start()
                copies.append(cp)
            for cp in copies:
                cp.wait()


def patch_far_kernel(
    scale, slabs, edges, near, far, clow, chigh, counts, _, out, share, buf, lines, sem
):
    depth, rows, _ = out.shape
    odd = lax.axis_index("gy") & 1
    slab = lax.axis_index("gz")
    missing = (slab == 0, slab == slabs - 1)
    corners = (clow, chigh)
    for side, places in enumerate(sides(rows)):

        @pl.when(odd == 1 - side)
        def _():
            copies = []
            for away, (row, edge) in enumerate(places):
                corner = None if away else corners[side]
                merge_rows(away, edges.at[edge], far, corner, missing, buf.at[away])
                cp = pltpu.make_async_copy(buf.at[away], out.at[:, row, :], sem.at[away])
                cp.start()
                copies.append(cp)
            row, edge = sides(rows)[1 - side][0]
            for end, z in enumerate((0, depth - 1)):
                line = pl.ds(z, 1)
                reach = jnp.minimum(edges[edge, line, :], near[1, line, :] + VOXEL)
                offer = jnp.where(missing[end], FAR, corners[1 - side][pl.ds(end, 1), :])
                lines[end] = jnp.minimum(reach, offer + VOXEL + VOXEL)
                cp = pltpu.make_async_copy(
                    lines.at[end], out.at[line, row, :], sem.at[2 + end]
                )
                cp.start()
                copies.append(cp)
            for cp in copies:
                cp.wait()

    x = pl.ds(0, LANES)
    both = (counts[:, x] + clow[:, x]).astype(jnp.int32)
    row = lax.broadcasted_iota(jnp.int32, both.shape, 0)
    both = jnp.where(row == 2, both, jnp.where(row == 3, both << COUNT_BITS, 0))
    count = jnp.sum(both, axis=0, keepdims=True)
    share[...] = count[:, :1].astype(jnp.float32) * jnp.float32(scale)


def patch_near(edges, near, out):
    depth, _, cols = out.shape
    return pl.pallas_call(
        patch_near_kernel,
        name="patch_near",
        out_shape=jax.ShapeDtypeStruct(out.shape, out.dtype),
        in_specs=[VMEM] * 2 + [HBM],
        out_specs=HBM,
        input_output_aliases={2: 0},
        scratch_shapes=[pltpu.VMEM((2, depth, cols), jnp.float32), pltpu.SemaphoreType.DMA((2,))],
        compiler_params=params(4),
        cost_estimate=cost(1),
    )(edges, near, out)


def patch_far(scale, edges, near, far, clow, chigh, counts, out):
    depth, _, cols = out.shape
    return pl.pallas_call(
        functools.partial(patch_far_kernel, scale, lax.axis_size("gz")),
        name="patch_far",
        out_shape=(
            jax.ShapeDtypeStruct(out.shape, out.dtype),
            jax.ShapeDtypeStruct((1, 1), jnp.float32),
        ),
        in_specs=[VMEM] * 6 + [HBM],
        out_specs=(HBM, VMEM),
        input_output_aliases={6: 0},
        scratch_shapes=[
            pltpu.VMEM((2, depth, cols), jnp.float32),
            pltpu.VMEM((2, 1, cols), jnp.float32),
            pltpu.SemaphoreType.DMA((4,)),
        ],
        compiler_params=params(4),
        cost_estimate=cost(1),
    )(edges, near, far, clow, chigh, counts, out)


def swapped(value, axis, partner):
    count = lax.axis_size(axis)
    return lax.ppermute(value, axis, [(i, partner(i) % count) for i in range(count)])


def after_odd(i):
    return i - 1 + 2 * (i % 2)


def shifted(value, axis, by):
    return swapped(value, axis, lambda i: i + by)


def on_device(distance, parent, removed, occupied):
    depth, rows, cols = distance.shape
    half = depth // 2
    slabs, columns = lax.axis_size("gz"), lax.axis_size("gy")
    tied = lax.optimization_barrier
    distance, parent, flags, occupied = (
        pltpu.with_memory_space_constraint(a, pltpu.HBM)
        for a in (distance, parent, removed.reshape(-1, LANES), occupied)
    )
    field, first, second = raise_all(distance, parent, flags, occupied)
    face0 = faces(field, rows, cols, 1)
    near = swapped(face0, "gy", after_odd)
    got_first = swapped(first, "gz", after_odd)
    face1 = faces(field, rows, cols, 0)
    once0 = sweep_once(field, 0, half, rows, cols)
    got_first, once0 = tied((got_first, once0))
    second = second.at[2 * rows :].add(got_first[2 * rows :])
    got_second = swapped(second, "gz", lambda i: i ^ 1)
    once1 = sweep_once(field, half, half, rows, cols)
    got_second, once1 = tied((got_second, once1))
    counts = second[2 * rows :] + got_second[2 * rows :]
    tiles, half0 = sweep_again_low(once0, rows, cols)
    face1, tiles = tied((face1, tiles))
    far = swapped(face1, "gy", lambda i: i ^ 1)
    lowered, half1 = sweep_again_high(once1, tiles)

    more = jnp.zeros_like(counts)
    mask = columns // 2
    while mask > 1:
        counts = counts + more
        more = swapped(counts, "gy", lambda i: i ^ mask)
        if mask == 4:
            more, half0 = tied((more, half0))
        if mask == 2:
            more, half1 = tied((more, half1))
        mask //= 2
    clow, chigh, counts = corners(got_first, got_second, counts, more)
    from_low = shifted(chigh, "gy", 1)
    from_high = shifted(clow, "gy", -1)
    lowered, edges = patch_z(got_first, got_second, half0, half1, lowered)
    total = distance.size * slabs * columns
    lowered = patch_near(edges, near, lowered)
    lowered, share = patch_far(
        100.0 / total, edges, near, far, from_low, from_high, counts, lowered
    )
    return (lowered, share[0, 0])


def solution(mesh):
    slabs, columns = mesh.shape["gz"], mesh.shape["gy"]
    if slabs != 4 or columns < 8 or columns & (columns - 1):
        raise ValueError("unsupported mesh")
    placed = (P("gz", "gy", None), P("gz", "gy", None), P(), P("gz", "gy", None))
    return jax.shard_map(
        on_device, mesh=mesh, in_specs=placed, out_specs=(P("gz", "gy", None), P()), check_vma=False
    )
```

```python
import functools

import jax
import jax.numpy as jnp
from jax import lax
from jax.experimental import pallas as pl
from jax.experimental.pallas import tpu as pltpu
from jax.sharding import PartitionSpec as P


FAR = 1000000.0
VOXEL = 0.1
TRUNC = 2.0
LANES = 128
SUBLANES = 8
CHUNK = 8
READ = 8
AHEAD = 3
RAISE_UNROLL = 8
SWEEP_UNROLL = 8
MIB = 2**20

HBM = pl.BlockSpec(memory_space=pltpu.HBM)
VMEM = pl.BlockSpec(memory_space=pltpu.VMEM)

COUNT_BITS = 12


def params(mib):
    return pltpu.CompilerParams(vmem_limit_bytes=mib * MIB)


def cost(mib):
    return pl.CostEstimate(flops=0, bytes_accessed=mib * MIB, transcendentals=0)


def packed_table(flags_ref):
    bits = (flags_ref[...] == 1).astype(jnp.int32)
    bits = bits << lax.broadcasted_iota(jnp.int32, bits.shape, 0)
    words = jnp.sum(bits, axis=0, keepdims=True)
    return jnp.broadcast_to(words, (SUBLANES, LANES))


PICK = lax.GatherDimensionNumbers(
    offset_dims=(),
    collapsed_slice_dims=(1,),
    start_index_map=(1,),
    operand_batching_dims=(0,),
    start_indices_batching_dims=(0,),
)


def raise_tile(words, dist, par, occ):
    lane = par & (LANES - 1)
    word = lax.gather(words, lane[..., None], PICK, (1, 1), mode="promise_in_bounds")
    cleared = (word >> (par >> 7)) & (occ ^ 1)
    raised = jnp.where(occ == 1, 0.0, jnp.where(cleared == 1, TRUNC, dist))
    return raised, cleared


def swept_tiles(centers, others):
    lane = lax.broadcasted_iota(jnp.int32, (SUBLANES, LANES), 1)
    last = len(centers) - 1
    after = [pltpu.roll(c, 1, 1) for c in centers]
    before = [pltpu.roll(c, LANES - 1, 1) for c in centers]
    swept = []
    for i, center in enumerate(centers):
        left = jnp.where(lane == 0, after[i - 1] if i else FAR, after[i])
        right = jnp.where(lane == LANES - 1, before[i + 1] if i < last else FAR, before[i])
        nearest = jnp.minimum(left, right)
        for other in others[i]:
            nearest = jnp.minimum(nearest, other)
        swept.append(jnp.minimum(center, nearest + VOXEL))
    return swept


def padded_rows(rows, cols):
    return cols // LANES * (rows + SUBLANES) + SUBLANES


def row_of(column, row, rows):
    return column * (rows + SUBLANES) + SUBLANES + row


def fill_pads(ref, at, rows, cols):
    for column in range(cols // LANES + 1):
        first = row_of(column, -SUBLANES, rows)
        ref[(*at, pl.ds(first, SUBLANES), slice(None))] = jnp.full((SUBLANES, LANES), FAR)


def swept_plane(read, rows, cols, y, beside=(-1, 1)):
    firsts = [row_of(c, y, rows) for c in range(cols // LANES)]
    centers = [read(0, f) for f in firsts]
    others = [[read(dz, f) for dz in beside] + [read(0, f - 1), read(0, f + 1)] for f in firsts]
    return swept_tiles(centers, others)


def face_tiles(field, rows, cols, row, inward, z):
    planes, height, _ = field.shape
    lines = field.reshape(planes * height, LANES)
    columns = range(cols // LANES)

    def read(column, y, dz=0):
        first = (z + 1 + dz) * height + row_of(column, y, rows)
        return lines[pl.ds(first, SUBLANES, stride=height), :]

    ends = [read(c, row) for c in columns]
    others = [(read(c, row, -1), read(c, row, 1), read(c, inward)) for c in columns]
    return ends, swept_tiles(ends, others)


def write_faces(field, rows, cols, top, start, out):
    def body(group, _):
        at = pl.ds(pl.multiple_of(group * SUBLANES, SUBLANES), SUBLANES)

        def write(row, inward):
            ends, swept = face_tiles(field, rows, cols, row, inward, start + group * SUBLANES)
            for column, (end, tile) in enumerate(zip(ends, swept)):
                x = pl.ds(column * LANES, LANES)
                out[0, at, x] = end
                out[1, at, x] = tile

        pl.when(top)(lambda: write(rows - 1, rows - 2))
        pl.when(jnp.logical_not(top))(lambda: write(0, 1))
        return 0

    lax.fori_loop(0, out.shape[1] // SUBLANES, body, 0)


def faces_kernel(rows, cols, toward_odd, field, *outs):
    odd = lax.axis_index("gy") & 1
    start = 0
    for out in outs:
        write_faces(field, rows, cols, odd == toward_odd, start, out)
        start += out.shape[1]


def faces(field, rows, cols, toward_odd, parts):
    count = (field.shape[0] - 2) // parts
    return pl.pallas_call(
        functools.partial(faces_kernel, rows, cols, toward_odd),
        out_shape=(jax.ShapeDtypeStruct((2, count, cols), jnp.float32),) * parts,
        in_specs=[VMEM],
        out_specs=(VMEM,) * parts,
        compiler_params=params(4),
        cost_estimate=cost(2),
    )(field)


def raise_planes(start, count, dist, par, flags_at, occ, field, flags, buf, fsem, sem):
    _, rows, cols = dist.shape
    columns = range(cols // LANES)
    chunks = count // READ

    def reads(chunk):
        source, target = pl.ds(start + chunk * READ, READ), pl.ds(chunk * READ, READ)
        return [
            pltpu.make_async_copy(src.at[source], dst.at[target], sem.at[which, chunk])
            for which, (src, dst) in enumerate(zip((dist, par, occ), buf))
        ]

    table_in = pltpu.make_async_copy(flags_at, flags, fsem)
    table_in.start()
    for chunk in range(min(AHEAD, chunks)):
        for cp in reads(chunk):
            cp.start()
    for z in (0, field.shape[0] - 1):
        if start < z <= start + count + 1 or z == start == 0:
            field[z] = jnp.full(field.shape[1:], FAR)
    table_in.wait()
    table = packed_table(flags)

    def body(chunk, acc):
        @pl.when(chunk + AHEAD < chunks)
        def _():
            for cp in reads(chunk + AHEAD):
                cp.start()

        for cp in reads(chunk):
            cp.wait()

        def planes(group, acc):
            for part in range(RAISE_UNROLL):
                z = chunk * READ + group * RAISE_UNROLL + part
                fill_pads(field, (start + z + 1,), rows, cols)
                for y in range(0, rows, SUBLANES):
                    for column in columns:
                        at = (z, pl.ds(y, SUBLANES), pl.ds(column * LANES, LANES))
                        tile, cleared = raise_tile(table, *(b[at] for b in buf))
                        to = pl.ds(row_of(column, y, rows), SUBLANES)
                        field[start + z + 1, to, :] = tile
                        acc[part] = acc[part] + cleared
            return acc

        return lax.fori_loop(0, READ // RAISE_UNROLL, planes, acc)

    zeros = jnp.zeros((SUBLANES, LANES), jnp.int32)
    parts = lax.fori_loop(0, chunks, body, [zeros] * RAISE_UNROLL)
    return sum(parts[1:], parts[0])


def keep_end(field, z, inward, rows, cols, out):
    def read(dz, at):
        return field[z + 1 + dz, pl.ds(at, SUBLANES), :]

    for y in range(0, rows, SUBLANES):
        swept = swept_plane(read, rows, cols, y, (inward,))
        for column in range(cols // LANES):
            x = pl.ds(column * LANES, LANES)
            out[pl.ds(y, SUBLANES), x] = read(0, row_of(column, y, rows))
            out[pl.ds(rows + y, SUBLANES), x] = swept[column]


def raise_kernel(dist, par, flags_at, occ, field, first, second, flags, buf, ends, fsem, sem):
    depth, rows, cols = dist.shape
    total = raise_planes(0, depth, dist, par, flags_at, occ, field, flags, buf, fsem, sem)
    keep_end(field, 0, 1, rows, cols, ends.at[0])
    keep_end(field, depth - 1, -1, rows, cols, ends.at[1])
    count = jnp.sum(total)
    row = lax.broadcasted_iota(jnp.int32, (SUBLANES, cols), 0)
    small = (count & (2**COUNT_BITS - 1)).astype(jnp.float32)
    large = (count >> COUNT_BITS).astype(jnp.float32)
    counts = jnp.where(row == 2, small, jnp.where(row == 3, large, 0.0))
    odd = lax.axis_index("gz") & 1
    for out, side in ((first, odd), (second, 1 - odd)):
        out[pl.ds(0, 2 * rows), :] = ends[side]
        out[pl.ds(2 * rows, SUBLANES), :] = counts


def raise_scratch(count, dist, par, flags, occ):
    return [
        pltpu.VMEM(flags.shape, jnp.int32),
        [pltpu.VMEM((count, *a.shape[1:]), a.dtype) for a in (dist, par, occ)],
        pltpu.SemaphoreType.DMA,
        pltpu.SemaphoreType.DMA((3, count // READ)),
    ]


def raise_all(dist, par, flags, occ):
    depth, rows, cols = dist.shape
    message = jax.ShapeDtypeStruct((2 * rows + SUBLANES, cols), jnp.float32)
    scratch = raise_scratch(depth, dist, par, flags, occ)
    return pl.pallas_call(
        raise_kernel,
        name="raise_all",
        out_shape=(
            jax.ShapeDtypeStruct((depth + 2, padded_rows(rows, cols), LANES), jnp.float32),
            message,
            message,
        ),
        in_specs=[HBM] * 4,
        out_specs=(VMEM,) * 3,
        scratch_shapes=scratch[:2] + [pltpu.VMEM((2, 2 * rows, cols), jnp.float32)] + scratch[2:],
        compiler_params=params(20),
        cost_estimate=cost(12),
    )(dist, par, flags, occ)


def sweep_once_kernel(start, count, rows, cols, field, once):
    depth = field.shape[0] - 2

    def sweep(z):
        def read(dz, at):
            return field[z + 1 + dz, pl.ds(at, SUBLANES), :]

        fill_pads(once, (z - start + 1,), rows, cols)
        for y in range(0, rows, SUBLANES):
            for column, tile in enumerate(swept_plane(read, rows, cols, y)):
                once[z - start + 1, pl.ds(row_of(column, y, rows), SUBLANES), :] = tile

    def body(group, _):
        for part in range(SWEEP_UNROLL):
            sweep(start + group * SWEEP_UNROLL + part)
        return 0

    for z in (start - 1, start + count):
        if 0 <= z < depth:
            sweep(z)
        else:
            once[z - start + 1] = jnp.full(once.shape[1:], FAR)
    lax.fori_loop(0, count // SWEEP_UNROLL, body, 0)


def sweep_once(field, start, count, rows, cols):
    return pl.pallas_call(
        functools.partial(sweep_once_kernel, start, count, rows, cols),
        out_shape=jax.ShapeDtypeStruct((count + 2, *field.shape[1:]), jnp.float32),
        in_specs=[VMEM],
        out_specs=VMEM,
        compiler_params=params(8),
        cost_estimate=cost(8),
    )(field)


def sweep_again_planes(once, first, count, tiles, slab):
    _, rows, cols = tiles.shape
    columns = range(cols // LANES)

    def body(group, _):
        for part in range(SWEEP_UNROLL):
            plane = first + group * SWEEP_UNROLL + part

            def read(dz, at):
                return once[plane + 1 + dz, pl.ds(at, SUBLANES), :]

            for y in range(0, rows, SUBLANES):
                for column, tile in enumerate(swept_plane(read, rows, cols, y)):
                    tiles[plane, pl.ds(y, SUBLANES), pl.ds(column * LANES, LANES)] = tile
                    at = plane * (rows * len(columns)) + column * rows + y
                    slab[pl.ds(pl.multiple_of(at, SUBLANES), SUBLANES), :] = tile
        return 0

    lax.fori_loop(0, count // SWEEP_UNROLL, body, 0)


def sweep_again_low_kernel(once, tiles, slab):
    sweep_again_planes(once, 0, tiles.shape[0], tiles, slab)


def sweep_again_high_kernel(once, low, out, slab, tiles, sem):
    half = low.shape[0]
    copies = [pltpu.make_async_copy(low, out.at[pl.ds(0, half)], sem.at[0])]
    copies[0].start()
    for step, first in enumerate(range(0, tiles.shape[0], CHUNK)):
        sweep_again_planes(once, first, CHUNK, tiles, slab)
        at = pl.ds(first, CHUNK)
        to = out.at[pl.ds(half + first, CHUNK)]
        cp = pltpu.make_async_copy(tiles.at[at], to, sem.at[step + 1])
        cp.start()
        copies.append(cp)
    for cp in copies:
        cp.wait()


def sweep_again_low(once, rows, cols):
    count = once.shape[0] - 2
    return pl.pallas_call(
        sweep_again_low_kernel,
        name="sweep_again_low",
        out_shape=(
            jax.ShapeDtypeStruct((count, rows, cols), jnp.float32),
            jax.ShapeDtypeStruct((count * rows * cols // LANES, LANES), jnp.float32),
        ),
        in_specs=[VMEM],
        out_specs=(VMEM, VMEM),
        compiler_params=params(4),
        cost_estimate=cost(8),
    )(once)


def sweep_again_high(once, low):
    count = once.shape[0] - 2
    _, rows, cols = low.shape
    return pl.pallas_call(
        sweep_again_high_kernel,
        name="sweep_again_high",
        out_shape=(
            jax.ShapeDtypeStruct((low.shape[0] + count, rows, cols), jnp.float32),
            jax.ShapeDtypeStruct((count * rows * cols // LANES, LANES), jnp.float32),
        ),
        in_specs=[VMEM, VMEM],
        out_specs=(HBM, VMEM),
        scratch_shapes=[
            pltpu.VMEM((count, rows, cols), jnp.float32),
            pltpu.SemaphoreType.DMA((count // CHUNK + 1,)),
        ],
        compiler_params=params(8),
        cost_estimate=cost(8),
    )(once, low)


def corners_kernel(first, second, counts, more, low, high, total):
    rows = (first.shape[0] - SUBLANES) // 2
    odd = lax.axis_index("gz") & 1
    total[...] = counts[...] + more[...]
    low[...] = total[...]
    high[...] = total[...]
    for side in range(2):
        for out, row in ((low, 0), (high, rows - 1)):
            line = jnp.where(odd == side, first[pl.ds(row, 1), :], second[pl.ds(row, 1), :])
            out[pl.ds(side, 1), :] = line


def corners(first, second, counts, more):
    shape = jax.ShapeDtypeStruct(counts.shape, jnp.float32)
    return pl.pallas_call(
        corners_kernel,
        name="corners",
        out_shape=(shape,) * 3,
        in_specs=[VMEM] * 4,
        out_specs=(VMEM,) * 3,
        compiler_params=params(2),
        cost_estimate=cost(1),
    )(first, second, counts, more)


def patch_z_kernel(slabs, first, second, slab_low, slab_high, _, out, edges, planes, sem):
    depth, rows, cols = out.shape
    columns = range(cols // LANES)
    slab = lax.axis_index("gz")
    odd = slab & 1
    size = rows * len(columns)
    stores = []
    for side, own in enumerate((slab_low, slab_high)):
        missing = slab == (0, slabs - 1)[side]
        base = (0, own.shape[0] - 2 * size)[side]
        for away in range(2):
            plane = (away, 1 - away)[side]
            offered = (rows, 0)[away]
            for y in range(0, rows, SUBLANES):
                for column in columns:
                    x = pl.ds(column * LANES, LANES)
                    at = (pl.ds(offered + y, SUBLANES), x)
                    got = jnp.where(odd == side, first[at], second[at])
                    got = jnp.where(missing, FAR, got) + VOXEL
                    if away:
                        got = got + VOXEL
                    tile = own[pl.ds(base + plane * size + column * rows + y, SUBLANES), :]
                    planes[side, plane, pl.ds(y, SUBLANES), x] = jnp.minimum(tile, got)
        to = out.at[pl.ds((0, depth - 2)[side], 2)]
        cp = pltpu.make_async_copy(planes.at[side], to, sem.at[side])
        cp.start()
        stores.append(cp)
    for edge, row in enumerate((0, 1, rows - 2, rows - 1)):
        z = 0
        for own in (slab_low, slab_high):
            for base in range(0, own.shape[0], SUBLANES * size):
                for column in columns:
                    tile = own[pl.ds(base + column * rows + row, SUBLANES, stride=size), :]
                    edges[edge, pl.ds(z, SUBLANES), pl.ds(column * LANES, LANES)] = tile
                z += SUBLANES
        for side in range(2):
            for plane in range(2):
                at = pl.ds((0, depth - 2)[side] + plane, 1)
                edges[edge, at, :] = planes[side, plane, pl.ds(row, 1), :]
    for cp in stores:
        cp.wait()


def patch_z(first, second, slab_low, slab_high, out):
    depth, rows, cols = out.shape
    return pl.pallas_call(
        functools.partial(patch_z_kernel, lax.axis_size("gz")),
        name="patch_z",
        out_shape=(
            jax.ShapeDtypeStruct(out.shape, out.dtype),
            jax.ShapeDtypeStruct((4, depth, cols), jnp.float32),
        ),
        in_specs=[VMEM] * 4 + [HBM],
        out_specs=(HBM, VMEM),
        input_output_aliases={4: 0},
        scratch_shapes=[
            pltpu.VMEM((2, 2, rows, cols), jnp.float32),
            pltpu.SemaphoreType.DMA((2,)),
        ],
        compiler_params=params(4),
        cost_estimate=cost(1),
    )(first, second, slab_low, slab_high, out)


def merge_rows(away, edges, parts, corner, missing, buf):
    z = 0
    for face in parts:
        planes = pl.ds(z, face.shape[1])
        reach = face[1 - away] + VOXEL
        if away:
            reach = reach + VOXEL
        buf[planes, :] = jnp.minimum(edges[planes, :], reach)
        z += face.shape[1]
    if corner is not None:
        for end, z in enumerate((0, buf.shape[0] - 1)):
            offer = jnp.where(missing[end], FAR, corner[pl.ds(end, 1), :])
            line = pl.ds(z, 1)
            buf[line, :] = jnp.minimum(buf[line, :], offer + VOXEL + VOXEL)


def sides(rows):
    return (((0, 0), (1, 1)), ((rows - 1, 3), (rows - 2, 2)))


def patch_far_kernel(edges, far, _, out, buf, sem):
    odd = lax.axis_index("gy") & 1
    for side, places in enumerate(sides(out.shape[1])):

        @pl.when(odd == 1 - side)
        def _():
            copies = []
            for away, (row, edge) in enumerate(places):
                merge_rows(away, edges.at[edge], (far,), None, None, buf.at[away])
                cp = pltpu.make_async_copy(buf.at[away], out.at[:, row, :], sem.at[away])
                cp.start()
                copies.append(cp)
            for cp in copies:
                cp.wait()


def patch_near_kernel(
    scale, slabs, edges, near0, near1, far, clow, chigh, counts, _, out, share, buf, lines, sem
):
    depth, rows, _ = out.shape
    odd = lax.axis_index("gy") & 1
    slab = lax.axis_index("gz")
    missing = (slab == 0, slab == slabs - 1)
    corners = (clow, chigh)
    for side, places in enumerate(sides(rows)):

        @pl.when(odd == side)
        def _():
            copies = []
            for away, (row, edge) in enumerate(places):
                corner = None if away else corners[side]
                merge_rows(away, edges.at[edge], (near0, near1), corner, missing, buf.at[away])
                cp = pltpu.make_async_copy(buf.at[away], out.at[:, row, :], sem.at[away])
                cp.start()
                copies.append(cp)
            row, edge = sides(rows)[1 - side][0]
            for end, z in enumerate((0, depth - 1)):
                line = pl.ds(z, 1)
                reach = jnp.minimum(edges[edge, line, :], far[1, line, :] + VOXEL)
                offer = jnp.where(missing[end], FAR, corners[1 - side][pl.ds(end, 1), :])
                lines[end] = jnp.minimum(reach, offer + VOXEL + VOXEL)
                cp = pltpu.make_async_copy(
                    lines.at[end], out.at[line, row, :], sem.at[2 + end]
                )
                cp.start()
                copies.append(cp)
            for cp in copies:
                cp.wait()

    x = pl.ds(0, LANES)
    both = (counts[:, x] + clow[:, x]).astype(jnp.int32)
    row = lax.broadcasted_iota(jnp.int32, both.shape, 0)
    both = jnp.where(row == 2, both, jnp.where(row == 3, both << COUNT_BITS, 0))
    count = jnp.sum(both, axis=0, keepdims=True)
    share[...] = count[:, :1].astype(jnp.float32) * jnp.float32(scale)


def patch_far(edges, far, out):
    depth, _, cols = out.shape
    return pl.pallas_call(
        patch_far_kernel,
        name="patch_far",
        out_shape=jax.ShapeDtypeStruct(out.shape, out.dtype),
        in_specs=[VMEM] * 2 + [HBM],
        out_specs=HBM,
        input_output_aliases={2: 0},
        scratch_shapes=[pltpu.VMEM((2, depth, cols), jnp.float32), pltpu.SemaphoreType.DMA((2,))],
        compiler_params=params(4),
        cost_estimate=cost(1),
    )(edges, far, out)


def patch_near(scale, edges, near0, near1, far, clow, chigh, counts, out):
    depth, _, cols = out.shape
    return pl.pallas_call(
        functools.partial(patch_near_kernel, scale, lax.axis_size("gz")),
        name="patch_near",
        out_shape=(
            jax.ShapeDtypeStruct(out.shape, out.dtype),
            jax.ShapeDtypeStruct((1, 1), jnp.float32),
        ),
        in_specs=[VMEM] * 7 + [HBM],
        out_specs=(HBM, VMEM),
        input_output_aliases={7: 0},
        scratch_shapes=[
            pltpu.VMEM((2, depth, cols), jnp.float32),
            pltpu.VMEM((2, 1, cols), jnp.float32),
            pltpu.SemaphoreType.DMA((4,)),
        ],
        compiler_params=params(4),
        cost_estimate=cost(1),
    )(edges, near0, near1, far, clow, chigh, counts, out)


def swapped(value, axis, partner):
    count = lax.axis_size(axis)
    return lax.ppermute(value, axis, [(i, partner(i) % count) for i in range(count)])


def after_odd(i):
    return i - 1 + 2 * (i % 2)


def shifted(value, axis, by):
    return swapped(value, axis, lambda i: i + by)


def on_device(distance, parent, removed, occupied):
    depth, rows, cols = distance.shape
    half = depth // 2
    slabs, columns = lax.axis_size("gz"), lax.axis_size("gy")
    tied = lax.optimization_barrier
    distance, parent, flags, occupied = (
        pltpu.with_memory_space_constraint(a, pltpu.HBM)
        for a in (distance, parent, removed.reshape(-1, LANES), occupied)
    )
    field, first, second = raise_all(distance, parent, flags, occupied)
    face0, face1 = faces(field, rows, cols, 1, 2)
    near0 = swapped(face0, "gy", after_odd)
    got_first = swapped(first, "gz", after_odd)
    (face,) = faces(field, rows, cols, 0, 1)
    once0 = sweep_once(field, 0, half, rows, cols)
    face, once0 = tied((face, once0))
    far = swapped(face, "gy", lambda i: i ^ 1)
    got_first, once0 = tied((got_first, once0))
    second = second.at[2 * rows :].add(got_first[2 * rows :])
    got_second = swapped(second, "gz", lambda i: i ^ 1)
    once1 = sweep_once(field, half, half, rows, cols)
    got_second, once1 = tied((got_second, once1))
    counts = second[2 * rows :] + got_second[2 * rows :]
    tiles, half0 = sweep_again_low(once0, rows, cols)
    lowered, half1 = sweep_again_high(once1, tiles)

    more = jnp.zeros_like(counts)
    mask = columns // 2
    while mask > 1:
        counts = counts + more
        more = swapped(counts, "gy", lambda i: i ^ mask)
        if mask == 4:
            more, half0 = tied((more, half0))
        if mask == 2:
            more, half1, face1 = tied((more, half1, face1))
        mask //= 2
    near1 = swapped(face1, "gy", after_odd)
    clow, chigh, counts = corners(got_first, got_second, counts, more)
    from_low = shifted(chigh, "gy", 1)
    from_high = shifted(clow, "gy", -1)
    lowered, edges = patch_z(got_first, got_second, half0, half1, lowered)
    total = distance.size * slabs * columns
    lowered = patch_far(edges, far, lowered)
    lowered, share = patch_near(
        100.0 / total, edges, near0, near1, far, from_low, from_high, counts, lowered
    )
    return (lowered, share[0, 0])


def solution(mesh):
    slabs, columns = mesh.shape["gz"], mesh.shape["gy"]
    if slabs != 4 or columns < 8 or columns & (columns - 1):
        raise ValueError("unsupported mesh")
    placed = (P("gz", "gy", None), P("gz", "gy", None), P(), P("gz", "gy", None))
    return jax.shard_map(
        on_device, mesh=mesh, in_specs=placed, out_specs=(P("gz", "gy", None), P()), check_vma=False
    )
```

```python
import functools

import jax
import jax.numpy as jnp
from jax import lax
from jax.experimental import pallas as pl
from jax.experimental.pallas import tpu as pltpu
from jax.sharding import PartitionSpec as P


FAR = 1000000.0
VOXEL = 0.1
TRUNC = 2.0
LANES = 128
SUBLANES = 8
CHUNK = 8
READ = 8
AHEAD = 3
RAISE_UNROLL = 8
SWEEP_UNROLL = 8
MIB = 2**20

HBM = pl.BlockSpec(memory_space=pltpu.HBM)
VMEM = pl.BlockSpec(memory_space=pltpu.VMEM)

COUNT_BITS = 12


def params(mib):
    return pltpu.CompilerParams(vmem_limit_bytes=mib * MIB)


def cost(mib):
    return pl.CostEstimate(flops=0, bytes_accessed=mib * MIB, transcendentals=0)


def packed_table(flags_ref):
    bits = (flags_ref[...] == 1).astype(jnp.int32)
    bits = bits << lax.broadcasted_iota(jnp.int32, bits.shape, 0)
    words = jnp.sum(bits, axis=0, keepdims=True)
    return jnp.broadcast_to(words, (SUBLANES, LANES))


PICK = lax.GatherDimensionNumbers(
    offset_dims=(),
    collapsed_slice_dims=(1,),
    start_index_map=(1,),
    operand_batching_dims=(0,),
    start_indices_batching_dims=(0,),
)


def raise_tile(words, dist, par, occ):
    lane = par & (LANES - 1)
    word = lax.gather(words, lane[..., None], PICK, (1, 1), mode="promise_in_bounds")
    cleared = (word >> (par >> 7)) & (occ ^ 1)
    raised = jnp.where(occ == 1, 0.0, jnp.where(cleared == 1, TRUNC, dist))
    return raised, cleared


def swept_tiles(centers, others):
    lane = lax.broadcasted_iota(jnp.int32, (SUBLANES, LANES), 1)
    last = len(centers) - 1
    after = [pltpu.roll(c, 1, 1) for c in centers]
    before = [pltpu.roll(c, LANES - 1, 1) for c in centers]
    swept = []
    for i, center in enumerate(centers):
        left = jnp.where(lane == 0, after[i - 1] if i else FAR, after[i])
        right = jnp.where(lane == LANES - 1, before[i + 1] if i < last else FAR, before[i])
        nearest = jnp.minimum(left, right)
        for other in others[i]:
            nearest = jnp.minimum(nearest, other)
        swept.append(jnp.minimum(center, nearest + VOXEL))
    return swept


def padded_rows(rows, cols):
    return cols // LANES * (rows + SUBLANES) + SUBLANES


def row_of(column, row, rows):
    return column * (rows + SUBLANES) + SUBLANES + row


def fill_pads(ref, at, rows, cols):
    for column in range(cols // LANES + 1):
        first = row_of(column, -SUBLANES, rows)
        ref[(*at, pl.ds(first, SUBLANES), slice(None))] = jnp.full((SUBLANES, LANES), FAR)


def swept_plane(read, rows, cols, y, beside=(-1, 1)):
    firsts = [row_of(c, y, rows) for c in range(cols // LANES)]
    centers = [read(0, f) for f in firsts]
    others = [[read(dz, f) for dz in beside] + [read(0, f - 1), read(0, f + 1)] for f in firsts]
    return swept_tiles(centers, others)


def face_tiles(field, rows, cols, row, inward, z):
    planes, height, _ = field.shape
    lines = field.reshape(planes * height, LANES)
    columns = range(cols // LANES)

    def read(column, y, dz=0):
        first = (z + 1 + dz) * height + row_of(column, y, rows)
        return lines[pl.ds(first, SUBLANES, stride=height), :]

    ends = [read(c, row) for c in columns]
    others = [(read(c, row, -1), read(c, row, 1), read(c, inward)) for c in columns]
    return ends, swept_tiles(ends, others)


def write_faces(field, rows, cols, top, start, out):
    def body(group, _):
        at = pl.ds(pl.multiple_of(group * SUBLANES, SUBLANES), SUBLANES)

        def write(row, inward):
            ends, swept = face_tiles(field, rows, cols, row, inward, start + group * SUBLANES)
            for column, (end, tile) in enumerate(zip(ends, swept)):
                x = pl.ds(column * LANES, LANES)
                out[0, at, x] = end
                out[1, at, x] = tile

        pl.when(top)(lambda: write(rows - 1, rows - 2))
        pl.when(jnp.logical_not(top))(lambda: write(0, 1))
        return 0

    lax.fori_loop(0, out.shape[1] // SUBLANES, body, 0)


def faces_kernel(rows, cols, toward_odd, field, *outs):
    odd = lax.axis_index("gy") & 1
    start = 0
    for out in outs:
        write_faces(field, rows, cols, odd == toward_odd, start, out)
        start += out.shape[1]


def faces(field, rows, cols, toward_odd, counts):
    return pl.pallas_call(
        functools.partial(faces_kernel, rows, cols, toward_odd),
        out_shape=tuple(jax.ShapeDtypeStruct((2, n, cols), jnp.float32) for n in counts),
        in_specs=[VMEM],
        out_specs=(VMEM,) * len(counts),
        compiler_params=params(4),
        cost_estimate=cost(2),
    )(field)


def raise_planes(start, count, dist, par, flags_at, occ, field, flags, buf, fsem, sem):
    _, rows, cols = dist.shape
    columns = range(cols // LANES)
    chunks = count // READ

    def reads(chunk):
        source, target = pl.ds(start + chunk * READ, READ), pl.ds(chunk * READ, READ)
        return [
            pltpu.make_async_copy(src.at[source], dst.at[target], sem.at[which, chunk])
            for which, (src, dst) in enumerate(zip((dist, par, occ), buf))
        ]

    table_in = pltpu.make_async_copy(flags_at, flags, fsem)
    table_in.start()
    for chunk in range(min(AHEAD, chunks)):
        for cp in reads(chunk):
            cp.start()
    for z in (0, field.shape[0] - 1):
        if start < z <= start + count + 1 or z == start == 0:
            field[z] = jnp.full(field.shape[1:], FAR)
    table_in.wait()
    table = packed_table(flags)

    def body(chunk, acc):
        @pl.when(chunk + AHEAD < chunks)
        def _():
            for cp in reads(chunk + AHEAD):
                cp.start()

        for cp in reads(chunk):
            cp.wait()

        def planes(group, acc):
            for part in range(RAISE_UNROLL):
                z = chunk * READ + group * RAISE_UNROLL + part
                fill_pads(field, (start + z + 1,), rows, cols)
                for y in range(0, rows, SUBLANES):
                    for column in columns:
                        at = (z, pl.ds(y, SUBLANES), pl.ds(column * LANES, LANES))
                        tile, cleared = raise_tile(table, *(b[at] for b in buf))
                        to = pl.ds(row_of(column, y, rows), SUBLANES)
                        field[start + z + 1, to, :] = tile
                        acc[part] = acc[part] + cleared
            return acc

        return lax.fori_loop(0, READ // RAISE_UNROLL, planes, acc)

    zeros = jnp.zeros((SUBLANES, LANES), jnp.int32)
    parts = lax.fori_loop(0, chunks, body, [zeros] * RAISE_UNROLL)
    return sum(parts[1:], parts[0])


def keep_end(field, z, inward, rows, cols, out):
    def read(dz, at):
        return field[z + 1 + dz, pl.ds(at, SUBLANES), :]

    for y in range(0, rows, SUBLANES):
        swept = swept_plane(read, rows, cols, y, (inward,))
        for column in range(cols // LANES):
            x = pl.ds(column * LANES, LANES)
            out[pl.ds(y, SUBLANES), x] = read(0, row_of(column, y, rows))
            out[pl.ds(rows + y, SUBLANES), x] = swept[column]


def raise_kernel(dist, par, flags_at, occ, field, first, second, flags, buf, ends, fsem, sem):
    depth, rows, cols = dist.shape
    total = raise_planes(0, depth, dist, par, flags_at, occ, field, flags, buf, fsem, sem)
    keep_end(field, 0, 1, rows, cols, ends.at[0])
    keep_end(field, depth - 1, -1, rows, cols, ends.at[1])
    count = jnp.sum(total)
    row = lax.broadcasted_iota(jnp.int32, (SUBLANES, cols), 0)
    small = (count & (2**COUNT_BITS - 1)).astype(jnp.float32)
    large = (count >> COUNT_BITS).astype(jnp.float32)
    counts = jnp.where(row == 2, small, jnp.where(row == 3, large, 0.0))
    odd = lax.axis_index("gz") & 1
    for out, side in ((first, odd), (second, 1 - odd)):
        out[pl.ds(0, 2 * rows), :] = ends[side]
        out[pl.ds(2 * rows, SUBLANES), :] = counts


def raise_scratch(count, dist, par, flags, occ):
    return [
        pltpu.VMEM(flags.shape, jnp.int32),
        [pltpu.VMEM((count, *a.shape[1:]), a.dtype) for a in (dist, par, occ)],
        pltpu.SemaphoreType.DMA,
        pltpu.SemaphoreType.DMA((3, count // READ)),
    ]


def raise_all(dist, par, flags, occ):
    depth, rows, cols = dist.shape
    message = jax.ShapeDtypeStruct((2 * rows + SUBLANES, cols), jnp.float32)
    scratch = raise_scratch(depth, dist, par, flags, occ)
    return pl.pallas_call(
        raise_kernel,
        name="raise_all",
        out_shape=(
            jax.ShapeDtypeStruct((depth + 2, padded_rows(rows, cols), LANES), jnp.float32),
            message,
            message,
        ),
        in_specs=[HBM] * 4,
        out_specs=(VMEM,) * 3,
        scratch_shapes=scratch[:2] + [pltpu.VMEM((2, 2 * rows, cols), jnp.float32)] + scratch[2:],
        compiler_params=params(20),
        cost_estimate=cost(12),
    )(dist, par, flags, occ)


def sweep_once_kernel(start, count, rows, cols, field, once):
    depth = field.shape[0] - 2

    def sweep(z):
        def read(dz, at):
            return field[z + 1 + dz, pl.ds(at, SUBLANES), :]

        fill_pads(once, (z - start + 1,), rows, cols)
        for y in range(0, rows, SUBLANES):
            for column, tile in enumerate(swept_plane(read, rows, cols, y)):
                once[z - start + 1, pl.ds(row_of(column, y, rows), SUBLANES), :] = tile

    def body(group, _):
        for part in range(SWEEP_UNROLL):
            sweep(start + group * SWEEP_UNROLL + part)
        return 0

    for z in (start - 1, start + count):
        if 0 <= z < depth:
            sweep(z)
        else:
            once[z - start + 1] = jnp.full(once.shape[1:], FAR)
    lax.fori_loop(0, count // SWEEP_UNROLL, body, 0)


def sweep_once(field, start, count, rows, cols):
    return pl.pallas_call(
        functools.partial(sweep_once_kernel, start, count, rows, cols),
        out_shape=jax.ShapeDtypeStruct((count + 2, *field.shape[1:]), jnp.float32),
        in_specs=[VMEM],
        out_specs=VMEM,
        compiler_params=params(8),
        cost_estimate=cost(8),
    )(field)


def sweep_again_planes(once, first, count, tiles, slab):
    _, rows, cols = tiles.shape
    columns = range(cols // LANES)

    def body(group, _):
        for part in range(SWEEP_UNROLL):
            plane = first + group * SWEEP_UNROLL + part

            def read(dz, at):
                return once[plane + 1 + dz, pl.ds(at, SUBLANES), :]

            for y in range(0, rows, SUBLANES):
                for column, tile in enumerate(swept_plane(read, rows, cols, y)):
                    tiles[plane, pl.ds(y, SUBLANES), pl.ds(column * LANES, LANES)] = tile
                    at = plane * (rows * len(columns)) + column * rows + y
                    slab[pl.ds(pl.multiple_of(at, SUBLANES), SUBLANES), :] = tile
        return 0

    lax.fori_loop(0, count // SWEEP_UNROLL, body, 0)


def sweep_again_low_kernel(once, tiles, slab):
    sweep_again_planes(once, 0, tiles.shape[0], tiles, slab)


def sweep_again_high_kernel(once, low, out, slab, tiles, sem):
    half = low.shape[0]
    copies = [pltpu.make_async_copy(low, out.at[pl.ds(0, half)], sem.at[0])]
    copies[0].start()
    for step, first in enumerate(range(0, tiles.shape[0], CHUNK)):
        sweep_again_planes(once, first, CHUNK, tiles, slab)
        at = pl.ds(first, CHUNK)
        to = out.at[pl.ds(half + first, CHUNK)]
        cp = pltpu.make_async_copy(tiles.at[at], to, sem.at[step + 1])
        cp.start()
        copies.append(cp)
    for cp in copies:
        cp.wait()


def sweep_again_low(once, rows, cols):
    count = once.shape[0] - 2
    return pl.pallas_call(
        sweep_again_low_kernel,
        name="sweep_again_low",
        out_shape=(
            jax.ShapeDtypeStruct((count, rows, cols), jnp.float32),
            jax.ShapeDtypeStruct((count * rows * cols // LANES, LANES), jnp.float32),
        ),
        in_specs=[VMEM],
        out_specs=(VMEM, VMEM),
        compiler_params=params(4),
        cost_estimate=cost(8),
    )(once)


def sweep_again_high(once, low):
    count = once.shape[0] - 2
    _, rows, cols = low.shape
    return pl.pallas_call(
        sweep_again_high_kernel,
        name="sweep_again_high",
        out_shape=(
            jax.ShapeDtypeStruct((low.shape[0] + count, rows, cols), jnp.float32),
            jax.ShapeDtypeStruct((count * rows * cols // LANES, LANES), jnp.float32),
        ),
        in_specs=[VMEM, VMEM],
        out_specs=(HBM, VMEM),
        scratch_shapes=[
            pltpu.VMEM((count, rows, cols), jnp.float32),
            pltpu.SemaphoreType.DMA((count // CHUNK + 1,)),
        ],
        compiler_params=params(8),
        cost_estimate=cost(8),
    )(once, low)


def corners_kernel(first, second, counts, more, low, high, total):
    rows = (first.shape[0] - SUBLANES) // 2
    odd = lax.axis_index("gz") & 1
    total[...] = counts[...] + more[...]
    low[...] = total[...]
    high[...] = total[...]
    for side in range(2):
        for out, row in ((low, 0), (high, rows - 1)):
            line = jnp.where(odd == side, first[pl.ds(row, 1), :], second[pl.ds(row, 1), :])
            out[pl.ds(side, 1), :] = line


def corners(first, second, counts, more):
    shape = jax.ShapeDtypeStruct(counts.shape, jnp.float32)
    return pl.pallas_call(
        corners_kernel,
        name="corners",
        out_shape=(shape,) * 3,
        in_specs=[VMEM] * 4,
        out_specs=(VMEM,) * 3,
        compiler_params=params(2),
        cost_estimate=cost(1),
    )(first, second, counts, more)


def patch_z_kernel(slabs, first, second, slab_low, slab_high, _, out, edges, planes, sem):
    depth, rows, cols = out.shape
    columns = range(cols // LANES)
    slab = lax.axis_index("gz")
    odd = slab & 1
    size = rows * len(columns)
    stores = []
    for side, own in enumerate((slab_low, slab_high)):
        missing = slab == (0, slabs - 1)[side]
        base = (0, own.shape[0] - 2 * size)[side]
        for away in range(2):
            plane = (away, 1 - away)[side]
            offered = (rows, 0)[away]
            for y in range(0, rows, SUBLANES):
                for column in columns:
                    x = pl.ds(column * LANES, LANES)
                    at = (pl.ds(offered + y, SUBLANES), x)
                    got = jnp.where(odd == side, first[at], second[at])
                    got = jnp.where(missing, FAR, got) + VOXEL
                    if away:
                        got = got + VOXEL
                    tile = own[pl.ds(base + plane * size + column * rows + y, SUBLANES), :]
                    planes[side, plane, pl.ds(y, SUBLANES), x] = jnp.minimum(tile, got)
        to = out.at[pl.ds((0, depth - 2)[side], 2)]
        cp = pltpu.make_async_copy(planes.at[side], to, sem.at[side])
        cp.start()
        stores.append(cp)
    for edge, row in enumerate((0, 1, rows - 2, rows - 1)):
        z = 0
        for own in (slab_low, slab_high):
            for base in range(0, own.shape[0], SUBLANES * size):
                for column in columns:
                    tile = own[pl.ds(base + column * rows + row, SUBLANES, stride=size), :]
                    edges[edge, pl.ds(z, SUBLANES), pl.ds(column * LANES, LANES)] = tile
                z += SUBLANES
        for side in range(2):
            for plane in range(2):
                at = pl.ds((0, depth - 2)[side] + plane, 1)
                edges[edge, at, :] = planes[side, plane, pl.ds(row, 1), :]
    for cp in stores:
        cp.wait()


def patch_z(first, second, slab_low, slab_high, out):
    depth, rows, cols = out.shape
    return pl.pallas_call(
        functools.partial(patch_z_kernel, lax.axis_size("gz")),
        name="patch_z",
        out_shape=(
            jax.ShapeDtypeStruct(out.shape, out.dtype),
            jax.ShapeDtypeStruct((4, depth, cols), jnp.float32),
        ),
        in_specs=[VMEM] * 4 + [HBM],
        out_specs=(HBM, VMEM),
        input_output_aliases={4: 0},
        scratch_shapes=[
            pltpu.VMEM((2, 2, rows, cols), jnp.float32),
            pltpu.SemaphoreType.DMA((2,)),
        ],
        compiler_params=params(4),
        cost_estimate=cost(1),
    )(first, second, slab_low, slab_high, out)


def merge_rows(away, edges, parts, corner, missing, buf):
    z = 0
    for face in parts:
        planes = pl.ds(z, face.shape[1])
        reach = face[1 - away] + VOXEL
        if away:
            reach = reach + VOXEL
        buf[planes, :] = jnp.minimum(edges[planes, :], reach)
        z += face.shape[1]
    if corner is not None:
        for end, z in enumerate((0, buf.shape[0] - 1)):
            offer = jnp.where(missing[end], FAR, corner[pl.ds(end, 1), :])
            line = pl.ds(z, 1)
            buf[line, :] = jnp.minimum(buf[line, :], offer + VOXEL + VOXEL)


def sides(rows):
    return (((0, 0), (1, 1)), ((rows - 1, 3), (rows - 2, 2)))


def patch_far_kernel(edges, far, _, out, buf, sem):
    odd = lax.axis_index("gy") & 1
    for side, places in enumerate(sides(out.shape[1])):

        @pl.when(odd == 1 - side)
        def _():
            copies = []
            for away, (row, edge) in enumerate(places):
                merge_rows(away, edges.at[edge], (far,), None, None, buf.at[away])
                cp = pltpu.make_async_copy(buf.at[away], out.at[:, row, :], sem.at[away])
                cp.start()
                copies.append(cp)
            for cp in copies:
                cp.wait()


def patch_near_kernel(
    scale, slabs, edges, near0, near1, far, clow, chigh, counts, _, out, share, buf, lines, sem
):
    depth, rows, _ = out.shape
    odd = lax.axis_index("gy") & 1
    slab = lax.axis_index("gz")
    missing = (slab == 0, slab == slabs - 1)
    corners = (clow, chigh)
    for side, places in enumerate(sides(rows)):

        @pl.when(odd == side)
        def _():
            copies = []
            for away, (row, edge) in enumerate(places):
                corner = None if away else corners[side]
                merge_rows(away, edges.at[edge], (near0, near1), corner, missing, buf.at[away])
                cp = pltpu.make_async_copy(buf.at[away], out.at[:, row, :], sem.at[away])
                cp.start()
                copies.append(cp)
            row, edge = sides(rows)[1 - side][0]
            for end, z in enumerate((0, depth - 1)):
                line = pl.ds(z, 1)
                reach = jnp.minimum(edges[edge, line, :], far[1, line, :] + VOXEL)
                offer = jnp.where(missing[end], FAR, corners[1 - side][pl.ds(end, 1), :])
                lines[end] = jnp.minimum(reach, offer + VOXEL + VOXEL)
                cp = pltpu.make_async_copy(
                    lines.at[end], out.at[line, row, :], sem.at[2 + end]
                )
                cp.start()
                copies.append(cp)
            for cp in copies:
                cp.wait()

    x = pl.ds(0, LANES)
    both = (counts[:, x] + clow[:, x]).astype(jnp.int32)
    row = lax.broadcasted_iota(jnp.int32, both.shape, 0)
    both = jnp.where(row == 2, both, jnp.where(row == 3, both << COUNT_BITS, 0))
    count = jnp.sum(both, axis=0, keepdims=True)
    share[...] = count[:, :1].astype(jnp.float32) * jnp.float32(scale)


def patch_far(edges, far, out):
    depth, _, cols = out.shape
    return pl.pallas_call(
        patch_far_kernel,
        name="patch_far",
        out_shape=jax.ShapeDtypeStruct(out.shape, out.dtype),
        in_specs=[VMEM] * 2 + [HBM],
        out_specs=HBM,
        input_output_aliases={2: 0},
        scratch_shapes=[pltpu.VMEM((2, depth, cols), jnp.float32), pltpu.SemaphoreType.DMA((2,))],
        compiler_params=params(4),
        cost_estimate=cost(1),
    )(edges, far, out)


def patch_near(scale, edges, near0, near1, far, clow, chigh, counts, out):
    depth, _, cols = out.shape
    return pl.pallas_call(
        functools.partial(patch_near_kernel, scale, lax.axis_size("gz")),
        name="patch_near",
        out_shape=(
            jax.ShapeDtypeStruct(out.shape, out.dtype),
            jax.ShapeDtypeStruct((1, 1), jnp.float32),
        ),
        in_specs=[VMEM] * 7 + [HBM],
        out_specs=(HBM, VMEM),
        input_output_aliases={7: 0},
        scratch_shapes=[
            pltpu.VMEM((2, depth, cols), jnp.float32),
            pltpu.VMEM((2, 1, cols), jnp.float32),
            pltpu.SemaphoreType.DMA((4,)),
        ],
        compiler_params=params(4),
        cost_estimate=cost(1),
    )(edges, near0, near1, far, clow, chigh, counts, out)


def swapped(value, axis, partner):
    count = lax.axis_size(axis)
    return lax.ppermute(value, axis, [(i, partner(i) % count) for i in range(count)])


def after_odd(i):
    return i - 1 + 2 * (i % 2)


def shifted(value, axis, by):
    return swapped(value, axis, lambda i: i + by)


def on_device(distance, parent, removed, occupied):
    depth, rows, cols = distance.shape
    half = depth // 2
    most = depth // 4 * 3
    slabs, columns = lax.axis_size("gz"), lax.axis_size("gy")
    tied = lax.optimization_barrier
    distance, parent, flags, occupied = (
        pltpu.with_memory_space_constraint(a, pltpu.HBM)
        for a in (distance, parent, removed.reshape(-1, LANES), occupied)
    )
    field, first, second = raise_all(distance, parent, flags, occupied)
    face0, face1 = faces(field, rows, cols, 1, (most, depth - most))
    near0 = swapped(face0, "gy", after_odd)
    got_first = swapped(first, "gz", after_odd)
    (face,) = faces(field, rows, cols, 0, (depth,))
    once0 = sweep_once(field, 0, half, rows, cols)
    face, once0 = tied((face, once0))
    far = swapped(face, "gy", lambda i: i ^ 1)
    got_first, once0 = tied((got_first, once0))
    second = second.at[2 * rows :].add(got_first[2 * rows :])
    got_second = swapped(second, "gz", lambda i: i ^ 1)
    once1 = sweep_once(field, half, half, rows, cols)
    got_second, once1 = tied((got_second, once1))
    counts = second[2 * rows :] + got_second[2 * rows :]
    tiles, half0 = sweep_again_low(once0, rows, cols)
    lowered, half1 = sweep_again_high(once1, tiles)

    more = jnp.zeros_like(counts)
    mask = columns // 2
    while mask > 1:
        counts = counts + more
        more = swapped(counts, "gy", lambda i: i ^ mask)
        if mask == 4:
            more, half0 = tied((more, half0))
        if mask == 2:
            more, half1, face1 = tied((more, half1, face1))
        mask //= 2
    near1 = swapped(face1, "gy", after_odd)
    clow, chigh, counts = corners(got_first, got_second, counts, more)
    from_low = shifted(chigh, "gy", 1)
    from_high = shifted(clow, "gy", -1)
    lowered, edges = patch_z(got_first, got_second, half0, half1, lowered)
    total = distance.size * slabs * columns
    lowered = patch_far(edges, far, lowered)
    lowered, share = patch_near(
        100.0 / total, edges, near0, near1, far, from_low, from_high, counts, lowered
    )
    return (lowered, share[0, 0])


def solution(mesh):
    slabs, columns = mesh.shape["gz"], mesh.shape["gy"]
    if slabs != 4 or columns < 8 or columns & (columns - 1):
        raise ValueError("unsupported mesh")
    placed = (P("gz", "gy", None), P("gz", "gy", None), P(), P("gz", "gy", None))
    return jax.shard_map(
        on_device, mesh=mesh, in_specs=placed, out_specs=(P("gz", "gy", None), P()), check_vma=False
    )
```

```python
import functools

import jax
import jax.numpy as jnp
from jax import lax
from jax.experimental import pallas as pl
from jax.experimental.pallas import tpu as pltpu
from jax.sharding import PartitionSpec as P


FAR = 1000000.0
VOXEL = 0.1
TRUNC = 2.0
LANES = 128
SUBLANES = 8
CHUNK = 8
READ = 8
AHEAD = 3
RAISE_UNROLL = 8
SWEEP_UNROLL = 8
MIB = 2**20

HBM = pl.BlockSpec(memory_space=pltpu.HBM)
VMEM = pl.BlockSpec(memory_space=pltpu.VMEM)

COUNT_BITS = 12


def params(mib):
    return pltpu.CompilerParams(vmem_limit_bytes=mib * MIB)


def cost(mib):
    return pl.CostEstimate(flops=0, bytes_accessed=mib * MIB, transcendentals=0)


def packed_table(flags_ref):
    bits = (flags_ref[...] == 1).astype(jnp.int32)
    bits = bits << lax.broadcasted_iota(jnp.int32, bits.shape, 0)
    words = jnp.sum(bits, axis=0, keepdims=True)
    return jnp.broadcast_to(words, (SUBLANES, LANES))


PICK = lax.GatherDimensionNumbers(
    offset_dims=(),
    collapsed_slice_dims=(1,),
    start_index_map=(1,),
    operand_batching_dims=(0,),
    start_indices_batching_dims=(0,),
)


def raise_tile(words, dist, par, occ):
    lane = par & (LANES - 1)
    word = lax.gather(words, lane[..., None], PICK, (1, 1), mode="promise_in_bounds")
    cleared = (word >> (par >> 7)) & (occ ^ 1)
    raised = jnp.where(occ == 1, 0.0, jnp.where(cleared == 1, TRUNC, dist))
    return raised, cleared


def swept_tiles(centers, others):
    lane = lax.broadcasted_iota(jnp.int32, (SUBLANES, LANES), 1)
    last = len(centers) - 1
    after = [pltpu.roll(c, 1, 1) for c in centers]
    before = [pltpu.roll(c, LANES - 1, 1) for c in centers]
    swept = []
    for i, center in enumerate(centers):
        left = jnp.where(lane == 0, after[i - 1] if i else FAR, after[i])
        right = jnp.where(lane == LANES - 1, before[i + 1] if i < last else FAR, before[i])
        nearest = jnp.minimum(left, right)
        for other in others[i]:
            nearest = jnp.minimum(nearest, other)
        swept.append(jnp.minimum(center, nearest + VOXEL))
    return swept


def padded_rows(rows, cols):
    return cols // LANES * (rows + SUBLANES) + SUBLANES


def row_of(column, row, rows):
    return column * (rows + SUBLANES) + SUBLANES + row


def fill_pads(ref, at, rows, cols):
    for column in range(cols // LANES + 1):
        first = row_of(column, -SUBLANES, rows)
        ref[(*at, pl.ds(first, SUBLANES), slice(None))] = jnp.full((SUBLANES, LANES), FAR)


def swept_plane(read, rows, cols, y, beside=(-1, 1)):
    firsts = [row_of(c, y, rows) for c in range(cols // LANES)]
    centers = [read(0, f) for f in firsts]
    others = [[read(dz, f) for dz in beside] + [read(0, f - 1), read(0, f + 1)] for f in firsts]
    return swept_tiles(centers, others)


def face_tiles(field, rows, cols, row, inward, z):
    planes, height, _ = field.shape
    lines = field.reshape(planes * height, LANES)
    columns = range(cols // LANES)

    def read(column, y, dz=0):
        first = (z + 1 + dz) * height + row_of(column, y, rows)
        return lines[pl.ds(first, SUBLANES, stride=height), :]

    ends = [read(c, row) for c in columns]
    others = [(read(c, row, -1), read(c, row, 1), read(c, inward)) for c in columns]
    return ends, swept_tiles(ends, others)


def write_faces(field, rows, cols, top, start, out):
    def body(group, _):
        at = pl.ds(pl.multiple_of(group * SUBLANES, SUBLANES), SUBLANES)

        def write(row, inward):
            ends, swept = face_tiles(field, rows, cols, row, inward, start + group * SUBLANES)
            for column, (end, tile) in enumerate(zip(ends, swept)):
                x = pl.ds(column * LANES, LANES)
                out[0, at, x] = end
                out[1, at, x] = tile

        pl.when(top)(lambda: write(rows - 1, rows - 2))
        pl.when(jnp.logical_not(top))(lambda: write(0, 1))
        return 0

    lax.fori_loop(0, out.shape[1] // SUBLANES, body, 0)


def faces_kernel(rows, cols, toward_odd, field, out):
    odd = lax.axis_index("gy") & 1
    write_faces(field, rows, cols, odd == toward_odd, 0, out)


def faces(field, rows, cols, toward_odd):
    return pl.pallas_call(
        functools.partial(faces_kernel, rows, cols, toward_odd),
        out_shape=jax.ShapeDtypeStruct((2, field.shape[0] - 2, cols), jnp.float32),
        in_specs=[VMEM],
        out_specs=VMEM,
        compiler_params=params(4),
        cost_estimate=cost(2),
    )(field)


def raise_planes(start, count, dist, par, flags_at, occ, field, flags, buf, fsem, sem):
    _, rows, cols = dist.shape
    columns = range(cols // LANES)
    chunks = count // READ

    def reads(chunk):
        source, target = pl.ds(start + chunk * READ, READ), pl.ds(chunk * READ, READ)
        return [
            pltpu.make_async_copy(src.at[source], dst.at[target], sem.at[which, chunk])
            for which, (src, dst) in enumerate(zip((dist, par, occ), buf))
        ]

    table_in = pltpu.make_async_copy(flags_at, flags, fsem)
    table_in.start()
    for chunk in range(min(AHEAD, chunks)):
        for cp in reads(chunk):
            cp.start()
    for z in (0, field.shape[0] - 1):
        if start < z <= start + count + 1 or z == start == 0:
            field[z] = jnp.full(field.shape[1:], FAR)
    table_in.wait()
    table = packed_table(flags)

    def body(chunk, acc):
        @pl.when(chunk + AHEAD < chunks)
        def _():
            for cp in reads(chunk + AHEAD):
                cp.start()

        for cp in reads(chunk):
            cp.wait()

        def planes(group, acc):
            for part in range(RAISE_UNROLL):
                z = chunk * READ + group * RAISE_UNROLL + part
                fill_pads(field, (start + z + 1,), rows, cols)
                for y in range(0, rows, SUBLANES):
                    for column in columns:
                        at = (z, pl.ds(y, SUBLANES), pl.ds(column * LANES, LANES))
                        tile, cleared = raise_tile(table, *(b[at] for b in buf))
                        to = pl.ds(row_of(column, y, rows), SUBLANES)
                        field[start + z + 1, to, :] = tile
                        acc[part] = acc[part] + cleared
            return acc

        return lax.fori_loop(0, READ // RAISE_UNROLL, planes, acc)

    zeros = jnp.zeros((SUBLANES, LANES), jnp.int32)
    parts = lax.fori_loop(0, chunks, body, [zeros] * RAISE_UNROLL)
    return sum(parts[1:], parts[0])


def keep_end(field, z, inward, rows, cols, out):
    def read(dz, at):
        return field[z + 1 + dz, pl.ds(at, SUBLANES), :]

    for y in range(0, rows, SUBLANES):
        swept = swept_plane(read, rows, cols, y, (inward,))
        for column in range(cols // LANES):
            x = pl.ds(column * LANES, LANES)
            out[pl.ds(y, SUBLANES), x] = read(0, row_of(column, y, rows))
            out[pl.ds(rows + y, SUBLANES), x] = swept[column]


def raise_kernel(dist, par, flags_at, occ, field, first, second, flags, buf, ends, fsem, sem):
    depth, rows, cols = dist.shape
    total = raise_planes(0, depth, dist, par, flags_at, occ, field, flags, buf, fsem, sem)
    keep_end(field, 0, 1, rows, cols, ends.at[0])
    keep_end(field, depth - 1, -1, rows, cols, ends.at[1])
    count = jnp.sum(total)
    row = lax.broadcasted_iota(jnp.int32, (SUBLANES, cols), 0)
    small = (count & (2**COUNT_BITS - 1)).astype(jnp.float32)
    large = (count >> COUNT_BITS).astype(jnp.float32)
    counts = jnp.where(row == 2, small, jnp.where(row == 3, large, 0.0))
    odd = lax.axis_index("gz") & 1
    for out, side in ((first, odd), (second, 1 - odd)):
        out[pl.ds(0, 2 * rows), :] = ends[side]
        out[pl.ds(2 * rows, SUBLANES), :] = counts


def raise_scratch(count, dist, par, flags, occ):
    return [
        pltpu.VMEM(flags.shape, jnp.int32),
        [pltpu.VMEM((count, *a.shape[1:]), a.dtype) for a in (dist, par, occ)],
        pltpu.SemaphoreType.DMA,
        pltpu.SemaphoreType.DMA((3, count // READ)),
    ]


def raise_all(dist, par, flags, occ):
    depth, rows, cols = dist.shape
    message = jax.ShapeDtypeStruct((2 * rows + SUBLANES, cols), jnp.float32)
    scratch = raise_scratch(depth, dist, par, flags, occ)
    return pl.pallas_call(
        raise_kernel,
        name="raise_all",
        out_shape=(
            jax.ShapeDtypeStruct((depth + 2, padded_rows(rows, cols), LANES), jnp.float32),
            message,
            message,
        ),
        in_specs=[HBM] * 4,
        out_specs=(VMEM,) * 3,
        scratch_shapes=scratch[:2] + [pltpu.VMEM((2, 2 * rows, cols), jnp.float32)] + scratch[2:],
        compiler_params=params(20),
        cost_estimate=cost(12),
    )(dist, par, flags, occ)


def sweep_once_kernel(start, count, rows, cols, field, once):
    depth = field.shape[0] - 2

    def sweep(z):
        def read(dz, at):
            return field[z + 1 + dz, pl.ds(at, SUBLANES), :]

        fill_pads(once, (z - start + 1,), rows, cols)
        for y in range(0, rows, SUBLANES):
            for column, tile in enumerate(swept_plane(read, rows, cols, y)):
                once[z - start + 1, pl.ds(row_of(column, y, rows), SUBLANES), :] = tile

    def body(group, _):
        for part in range(SWEEP_UNROLL):
            sweep(start + group * SWEEP_UNROLL + part)
        return 0

    for z in (start - 1, start + count):
        if 0 <= z < depth:
            sweep(z)
        else:
            once[z - start + 1] = jnp.full(once.shape[1:], FAR)
    lax.fori_loop(0, count // SWEEP_UNROLL, body, 0)


def sweep_once(field, start, count, rows, cols):
    return pl.pallas_call(
        functools.partial(sweep_once_kernel, start, count, rows, cols),
        out_shape=jax.ShapeDtypeStruct((count + 2, *field.shape[1:]), jnp.float32),
        in_specs=[VMEM],
        out_specs=VMEM,
        compiler_params=params(8),
        cost_estimate=cost(8),
    )(field)


def sweep_again_planes(once, first, count, tiles, slab):
    _, rows, cols = tiles.shape
    columns = range(cols // LANES)

    def body(group, _):
        for part in range(SWEEP_UNROLL):
            plane = first + group * SWEEP_UNROLL + part

            def read(dz, at):
                return once[plane + 1 + dz, pl.ds(at, SUBLANES), :]

            for y in range(0, rows, SUBLANES):
                for column, tile in enumerate(swept_plane(read, rows, cols, y)):
                    tiles[plane, pl.ds(y, SUBLANES), pl.ds(column * LANES, LANES)] = tile
                    at = plane * (rows * len(columns)) + column * rows + y
                    slab[pl.ds(pl.multiple_of(at, SUBLANES), SUBLANES), :] = tile
        return 0

    lax.fori_loop(0, count // SWEEP_UNROLL, body, 0)


def sweep_again_low_kernel(once, tiles, slab):
    sweep_again_planes(once, 0, tiles.shape[0], tiles, slab)


def sweep_again_high_kernel(once, low, out, slab, tiles, sem):
    half = low.shape[0]
    copies = [pltpu.make_async_copy(low, out.at[pl.ds(0, half)], sem.at[0])]
    copies[0].start()
    for step, first in enumerate(range(0, tiles.shape[0], CHUNK)):
        sweep_again_planes(once, first, CHUNK, tiles, slab)
        at = pl.ds(first, CHUNK)
        to = out.at[pl.ds(half + first, CHUNK)]
        cp = pltpu.make_async_copy(tiles.at[at], to, sem.at[step + 1])
        cp.start()
        copies.append(cp)
    for cp in copies:
        cp.wait()


def sweep_again_low(once, rows, cols):
    count = once.shape[0] - 2
    return pl.pallas_call(
        sweep_again_low_kernel,
        name="sweep_again_low",
        out_shape=(
            jax.ShapeDtypeStruct((count, rows, cols), jnp.float32),
            jax.ShapeDtypeStruct((count * rows * cols // LANES, LANES), jnp.float32),
        ),
        in_specs=[VMEM],
        out_specs=(VMEM, VMEM),
        compiler_params=params(4),
        cost_estimate=cost(8),
    )(once)


def sweep_again_high(once, low):
    count = once.shape[0] - 2
    _, rows, cols = low.shape
    return pl.pallas_call(
        sweep_again_high_kernel,
        name="sweep_again_high",
        out_shape=(
            jax.ShapeDtypeStruct((low.shape[0] + count, rows, cols), jnp.float32),
            jax.ShapeDtypeStruct((count * rows * cols // LANES, LANES), jnp.float32),
        ),
        in_specs=[VMEM, VMEM],
        out_specs=(HBM, VMEM),
        scratch_shapes=[
            pltpu.VMEM((count, rows, cols), jnp.float32),
            pltpu.SemaphoreType.DMA((count // CHUNK + 1,)),
        ],
        compiler_params=params(8),
        cost_estimate=cost(8),
    )(once, low)


def corners_kernel(first, second, counts, more, low, high, total):
    rows = (first.shape[0] - SUBLANES) // 2
    odd = lax.axis_index("gz") & 1
    total[...] = counts[...] + more[...]
    low[...] = total[...]
    high[...] = total[...]
    for side in range(2):
        for out, row in ((low, 0), (high, rows - 1)):
            line = jnp.where(odd == side, first[pl.ds(row, 1), :], second[pl.ds(row, 1), :])
            out[pl.ds(side, 1), :] = line


def corners(first, second, counts, more):
    shape = jax.ShapeDtypeStruct(counts.shape, jnp.float32)
    return pl.pallas_call(
        corners_kernel,
        name="corners",
        out_shape=(shape,) * 3,
        in_specs=[VMEM] * 4,
        out_specs=(VMEM,) * 3,
        compiler_params=params(2),
        cost_estimate=cost(1),
    )(first, second, counts, more)


def patch_z_kernel(slabs, first, second, slab_low, slab_high, _, out, edges, planes, sem):
    depth, rows, cols = out.shape
    columns = range(cols // LANES)
    slab = lax.axis_index("gz")
    odd = slab & 1
    size = rows * len(columns)
    stores = []
    for side, own in enumerate((slab_low, slab_high)):
        missing = slab == (0, slabs - 1)[side]
        base = (0, own.shape[0] - 2 * size)[side]
        for away in range(2):
            plane = (away, 1 - away)[side]
            offered = (rows, 0)[away]
            for y in range(0, rows, SUBLANES):
                for column in columns:
                    x = pl.ds(column * LANES, LANES)
                    at = (pl.ds(offered + y, SUBLANES), x)
                    got = jnp.where(odd == side, first[at], second[at])
                    got = jnp.where(missing, FAR, got) + VOXEL
                    if away:
                        got = got + VOXEL
                    tile = own[pl.ds(base + plane * size + column * rows + y, SUBLANES), :]
                    planes[side, plane, pl.ds(y, SUBLANES), x] = jnp.minimum(tile, got)
        to = out.at[pl.ds((0, depth - 2)[side], 2)]
        cp = pltpu.make_async_copy(planes.at[side], to, sem.at[side])
        cp.start()
        stores.append(cp)
    for edge, row in enumerate((0, 1, rows - 2, rows - 1)):
        z = 0
        for own in (slab_low, slab_high):
            for base in range(0, own.shape[0], SUBLANES * size):
                for column in columns:
                    tile = own[pl.ds(base + column * rows + row, SUBLANES, stride=size), :]
                    edges[edge, pl.ds(z, SUBLANES), pl.ds(column * LANES, LANES)] = tile
                z += SUBLANES
        for side in range(2):
            for plane in range(2):
                at = pl.ds((0, depth - 2)[side] + plane, 1)
                edges[edge, at, :] = planes[side, plane, pl.ds(row, 1), :]
    for cp in stores:
        cp.wait()


def patch_z(first, second, slab_low, slab_high, out):
    depth, rows, cols = out.shape
    return pl.pallas_call(
        functools.partial(patch_z_kernel, lax.axis_size("gz")),
        name="patch_z",
        out_shape=(
            jax.ShapeDtypeStruct(out.shape, out.dtype),
            jax.ShapeDtypeStruct((4, depth, cols), jnp.float32),
        ),
        in_specs=[VMEM] * 4 + [HBM],
        out_specs=(HBM, VMEM),
        input_output_aliases={4: 0},
        scratch_shapes=[
            pltpu.VMEM((2, 2, rows, cols), jnp.float32),
            pltpu.SemaphoreType.DMA((2,)),
        ],
        compiler_params=params(4),
        cost_estimate=cost(1),
    )(first, second, slab_low, slab_high, out)


def merge_rows(away, edges, face, corner, missing, buf):
    reach = face[1 - away] + VOXEL
    if away:
        reach = reach + VOXEL
    buf[...] = jnp.minimum(edges[...], reach)
    if corner is not None:
        for end, z in enumerate((0, buf.shape[0] - 1)):
            offer = jnp.where(missing[end], FAR, corner[pl.ds(end, 1), :])
            line = pl.ds(z, 1)
            buf[line, :] = jnp.minimum(buf[line, :], offer + VOXEL + VOXEL)


def sides(rows):
    return (((0, 0), (1, 1)), ((rows - 1, 3), (rows - 2, 2)))


def patch_near_kernel(edges, near, _, out, buf, sem):
    odd = lax.axis_index("gy") & 1
    for side, places in enumerate(sides(out.shape[1])):

        @pl.when(odd == 1 - side)
        def _():
            copies = []
            for away, (row, edge) in enumerate(places):
                merge_rows(away, edges.at[edge], near, None, None, buf.at[away])
                cp = pltpu.make_async_copy(buf.at[away], out.at[:, row, :], sem.at[away])
                cp.start()
                copies.append(cp)
            for cp in copies:
                cp.wait()


def patch_far_kernel(
    scale, slabs, edges, near, far, clow, chigh, counts, _, out, share, buf, lines, sem
):
    depth, rows, _ = out.shape
    odd = lax.axis_index("gy") & 1
    slab = lax.axis_index("gz")
    missing = (slab == 0, slab == slabs - 1)
    corners = (clow, chigh)
    for side, places in enumerate(sides(rows)):

        @pl.when(odd == side)
        def _():
            copies = []
            for away, (row, edge) in enumerate(places):
                corner = None if away else corners[side]
                merge_rows(away, edges.at[edge], far, corner, missing, buf.at[away])
                cp = pltpu.make_async_copy(buf.at[away], out.at[:, row, :], sem.at[away])
                cp.start()
                copies.append(cp)
            row, edge = sides(rows)[1 - side][0]
            for end, z in enumerate((0, depth - 1)):
                line = pl.ds(z, 1)
                reach = jnp.minimum(edges[edge, line, :], near[1, line, :] + VOXEL)
                offer = jnp.where(missing[end], FAR, corners[1 - side][pl.ds(end, 1), :])
                lines[end] = jnp.minimum(reach, offer + VOXEL + VOXEL)
                cp = pltpu.make_async_copy(
                    lines.at[end], out.at[line, row, :], sem.at[2 + end]
                )
                cp.start()
                copies.append(cp)
            for cp in copies:
                cp.wait()

    x = pl.ds(0, LANES)
    both = (counts[:, x] + clow[:, x]).astype(jnp.int32)
    row = lax.broadcasted_iota(jnp.int32, both.shape, 0)
    both = jnp.where(row == 2, both, jnp.where(row == 3, both << COUNT_BITS, 0))
    count = jnp.sum(both, axis=0, keepdims=True)
    share[...] = count[:, :1].astype(jnp.float32) * jnp.float32(scale)


def patch_near(edges, near, out):
    depth, _, cols = out.shape
    return pl.pallas_call(
        patch_near_kernel,
        name="patch_near",
        out_shape=jax.ShapeDtypeStruct(out.shape, out.dtype),
        in_specs=[VMEM] * 2 + [HBM],
        out_specs=HBM,
        input_output_aliases={2: 0},
        scratch_shapes=[pltpu.VMEM((2, depth, cols), jnp.float32), pltpu.SemaphoreType.DMA((2,))],
        compiler_params=params(4),
        cost_estimate=cost(1),
    )(edges, near, out)


def patch_far(scale, edges, near, far, clow, chigh, counts, out):
    depth, _, cols = out.shape
    return pl.pallas_call(
        functools.partial(patch_far_kernel, scale, lax.axis_size("gz")),
        name="patch_far",
        out_shape=(
            jax.ShapeDtypeStruct(out.shape, out.dtype),
            jax.ShapeDtypeStruct((1, 1), jnp.float32),
        ),
        in_specs=[VMEM] * 6 + [HBM],
        out_specs=(HBM, VMEM),
        input_output_aliases={6: 0},
        scratch_shapes=[
            pltpu.VMEM((2, depth, cols), jnp.float32),
            pltpu.VMEM((2, 1, cols), jnp.float32),
            pltpu.SemaphoreType.DMA((4,)),
        ],
        compiler_params=params(4),
        cost_estimate=cost(1),
    )(edges, near, far, clow, chigh, counts, out)


def swapped(value, axis, partner):
    count = lax.axis_size(axis)
    return lax.ppermute(value, axis, [(i, partner(i) % count) for i in range(count)])


def after_odd(i):
    return i - 1 + 2 * (i % 2)


def shifted(value, axis, by):
    return swapped(value, axis, lambda i: i + by)


def on_device(distance, parent, removed, occupied):
    depth, rows, cols = distance.shape
    half = depth // 2
    slabs, columns = lax.axis_size("gz"), lax.axis_size("gy")
    tied = lax.optimization_barrier
    distance, parent, flags, occupied = (
        pltpu.with_memory_space_constraint(a, pltpu.HBM)
        for a in (distance, parent, removed.reshape(-1, LANES), occupied)
    )
    field, first, second = raise_all(distance, parent, flags, occupied)
    face0 = faces(field, rows, cols, 0)
    near = swapped(face0, "gy", lambda i: i ^ 1)
    face1 = faces(field, rows, cols, 1)
    once0 = sweep_once(field, 0, half, rows, cols)

    counts = first[2 * rows :]
    mask = columns // 2
    while mask > 1:
        more = swapped(counts, "gy", lambda i: i ^ mask)
        if mask == 4:
            more, face1 = tied((more, face1))
        if mask == 2:
            more, once0 = tied((more, once0))
        counts = counts + more
        mask //= 2
    face1, counts = tied((face1, counts))
    far = swapped(face1, "gy", after_odd)

    first = first.at[2 * rows :].set(counts)
    got_first = swapped(first, "gz", after_odd)
    once1 = sweep_once(field, half, half, rows, cols)
    tiles, half0 = sweep_again_low(once0, rows, cols)
    got_first, tiles = tied((got_first, tiles))
    counts = counts + got_first[2 * rows :]
    second = second.at[2 * rows :].set(counts)
    got_second = swapped(second, "gz", lambda i: i ^ 1)
    lowered, half1 = sweep_again_high(once1, tiles)
    got_second, half1 = tied((got_second, half1))
    more = got_second[2 * rows :]
    clow, chigh, counts = corners(got_first, got_second, counts, more)
    from_low = shifted(chigh, "gy", 1)
    from_high = shifted(clow, "gy", -1)
    lowered, edges = patch_z(got_first, got_second, half0, half1, lowered)
    total = distance.size * slabs * columns
    lowered = patch_near(edges, near, lowered)
    lowered, share = patch_far(
        100.0 / total, edges, near, far, from_low, from_high, counts, lowered
    )
    return (lowered, share[0, 0])


def solution(mesh):
    slabs, columns = mesh.shape["gz"], mesh.shape["gy"]
    if slabs != 4 or columns < 8 or columns & (columns - 1):
        raise ValueError("unsupported mesh")
    placed = (P("gz", "gy", None), P("gz", "gy", None), P(), P("gz", "gy", None))
    return jax.shard_map(
        on_device, mesh=mesh, in_specs=placed, out_specs=(P("gz", "gy", None), P()), check_vma=False
    )
```

```python
import functools

import jax
import jax.numpy as jnp
from jax import lax
from jax.experimental import pallas as pl
from jax.experimental.pallas import tpu as pltpu
from jax.sharding import PartitionSpec as P


FAR = 1000000.0
VOXEL = 0.1
TRUNC = 2.0
LANES = 128
SUBLANES = 8
CHUNK = 8
READ = 8
AHEAD = 3
RAISE_UNROLL = 8
SWEEP_UNROLL = 8
MIB = 2**20

HBM = pl.BlockSpec(memory_space=pltpu.HBM)
VMEM = pl.BlockSpec(memory_space=pltpu.VMEM)

COUNT_BITS = 12


def params(mib):
    return pltpu.CompilerParams(vmem_limit_bytes=mib * MIB)


def cost(mib):
    return pl.CostEstimate(flops=0, bytes_accessed=mib * MIB, transcendentals=0)


def packed_table(flags_ref):
    bits = (flags_ref[...] == 1).astype(jnp.int32)
    bits = bits << lax.broadcasted_iota(jnp.int32, bits.shape, 0)
    words = jnp.sum(bits, axis=0, keepdims=True)
    return jnp.broadcast_to(words, (SUBLANES, LANES))


PICK = lax.GatherDimensionNumbers(
    offset_dims=(),
    collapsed_slice_dims=(1,),
    start_index_map=(1,),
    operand_batching_dims=(0,),
    start_indices_batching_dims=(0,),
)


def raise_tile(words, dist, par, occ):
    lane = par & (LANES - 1)
    word = lax.gather(words, lane[..., None], PICK, (1, 1), mode="promise_in_bounds")
    cleared = (word >> (par >> 7)) & (occ ^ 1)
    raised = jnp.where(occ == 1, 0.0, jnp.where(cleared == 1, TRUNC, dist))
    return raised, cleared


def swept_tiles(centers, others):
    lane = lax.broadcasted_iota(jnp.int32, (SUBLANES, LANES), 1)
    last = len(centers) - 1
    after = [pltpu.roll(c, 1, 1) for c in centers]
    before = [pltpu.roll(c, LANES - 1, 1) for c in centers]
    swept = []
    for i, center in enumerate(centers):
        left = jnp.where(lane == 0, after[i - 1] if i else FAR, after[i])
        right = jnp.where(lane == LANES - 1, before[i + 1] if i < last else FAR, before[i])
        nearest = jnp.minimum(left, right)
        for other in others[i]:
            nearest = jnp.minimum(nearest, other)
        swept.append(jnp.minimum(center, nearest + VOXEL))
    return swept


def padded_rows(rows, cols):
    return cols // LANES * (rows + SUBLANES) + SUBLANES


def row_of(column, row, rows):
    return column * (rows + SUBLANES) + SUBLANES + row


def fill_pads(ref, at, rows, cols):
    for column in range(cols // LANES + 1):
        first = row_of(column, -SUBLANES, rows)
        ref[(*at, pl.ds(first, SUBLANES), slice(None))] = jnp.full((SUBLANES, LANES), FAR)


def swept_plane(read, rows, cols, y, beside=(-1, 1)):
    firsts = [row_of(c, y, rows) for c in range(cols // LANES)]
    centers = [read(0, f) for f in firsts]
    others = [[read(dz, f) for dz in beside] + [read(0, f - 1), read(0, f + 1)] for f in firsts]
    return swept_tiles(centers, others)


def face_tiles(field, rows, cols, row, inward, z):
    planes, height, _ = field.shape
    lines = field.reshape(planes * height, LANES)
    columns = range(cols // LANES)

    def read(column, y, dz=0):
        first = (z + 1 + dz) * height + row_of(column, y, rows)
        return lines[pl.ds(first, SUBLANES, stride=height), :]

    ends = [read(c, row) for c in columns]
    others = [(read(c, row, -1), read(c, row, 1), read(c, inward)) for c in columns]
    return ends, swept_tiles(ends, others)


def write_faces(field, rows, cols, top, start, out):
    def body(group, _):
        at = pl.ds(pl.multiple_of(group * SUBLANES, SUBLANES), SUBLANES)

        def write(row, inward):
            ends, swept = face_tiles(field, rows, cols, row, inward, start + group * SUBLANES)
            for column, (end, tile) in enumerate(zip(ends, swept)):
                x = pl.ds(column * LANES, LANES)
                out[0, at, x] = end
                out[1, at, x] = tile

        pl.when(top)(lambda: write(rows - 1, rows - 2))
        pl.when(jnp.logical_not(top))(lambda: write(0, 1))
        return 0

    lax.fori_loop(0, out.shape[1] // SUBLANES, body, 0)


def faces_kernel(rows, cols, toward_odd, field, out):
    odd = lax.axis_index("gy") & 1
    write_faces(field, rows, cols, odd == toward_odd, 0, out)


def faces(field, rows, cols, toward_odd):
    return pl.pallas_call(
        functools.partial(faces_kernel, rows, cols, toward_odd),
        out_shape=jax.ShapeDtypeStruct((2, field.shape[0] - 2, cols), jnp.float32),
        in_specs=[VMEM],
        out_specs=VMEM,
        compiler_params=params(4),
        cost_estimate=cost(2),
    )(field)


def raise_planes(start, count, dist, par, flags_at, occ, field, flags, buf, fsem, sem):
    _, rows, cols = dist.shape
    columns = range(cols // LANES)
    chunks = count // READ

    def reads(chunk):
        source, target = pl.ds(start + chunk * READ, READ), pl.ds(chunk * READ, READ)
        return [
            pltpu.make_async_copy(src.at[source], dst.at[target], sem.at[which, chunk])
            for which, (src, dst) in enumerate(zip((dist, par, occ), buf))
        ]

    table_in = pltpu.make_async_copy(flags_at, flags, fsem)
    table_in.start()
    for chunk in range(min(AHEAD, chunks)):
        for cp in reads(chunk):
            cp.start()
    for z in (0, field.shape[0] - 1):
        if start < z <= start + count + 1 or z == start == 0:
            field[z] = jnp.full(field.shape[1:], FAR)
    table_in.wait()
    table = packed_table(flags)

    def body(chunk, acc):
        @pl.when(chunk + AHEAD < chunks)
        def _():
            for cp in reads(chunk + AHEAD):
                cp.start()

        for cp in reads(chunk):
            cp.wait()

        def planes(group, acc):
            for part in range(RAISE_UNROLL):
                z = chunk * READ + group * RAISE_UNROLL + part
                fill_pads(field, (start + z + 1,), rows, cols)
                for y in range(0, rows, SUBLANES):
                    for column in columns:
                        at = (z, pl.ds(y, SUBLANES), pl.ds(column * LANES, LANES))
                        tile, cleared = raise_tile(table, *(b[at] for b in buf))
                        to = pl.ds(row_of(column, y, rows), SUBLANES)
                        field[start + z + 1, to, :] = tile
                        acc[part] = acc[part] + cleared
            return acc

        return lax.fori_loop(0, READ // RAISE_UNROLL, planes, acc)

    zeros = jnp.zeros((SUBLANES, LANES), jnp.int32)
    parts = lax.fori_loop(0, chunks, body, [zeros] * RAISE_UNROLL)
    return sum(parts[1:], parts[0])


def keep_end(field, z, inward, rows, cols, out):
    def read(dz, at):
        return field[z + 1 + dz, pl.ds(at, SUBLANES), :]

    for y in range(0, rows, SUBLANES):
        swept = swept_plane(read, rows, cols, y, (inward,))
        for column in range(cols // LANES):
            x = pl.ds(column * LANES, LANES)
            out[pl.ds(y, SUBLANES), x] = read(0, row_of(column, y, rows))
            out[pl.ds(rows + y, SUBLANES), x] = swept[column]


def raise_kernel(dist, par, flags_at, occ, field, first, second, counts, flags, buf, ends, fsem, sem):
    depth, rows, cols = dist.shape
    total = raise_planes(0, depth, dist, par, flags_at, occ, field, flags, buf, fsem, sem)
    keep_end(field, 0, 1, rows, cols, ends.at[0])
    keep_end(field, depth - 1, -1, rows, cols, ends.at[1])
    count = jnp.sum(total)
    row = lax.broadcasted_iota(jnp.int32, (SUBLANES, cols), 0)
    small = (count & (2**COUNT_BITS - 1)).astype(jnp.float32)
    large = (count >> COUNT_BITS).astype(jnp.float32)
    counts[...] = jnp.where(row == 2, small, jnp.where(row == 3, large, 0.0))
    odd = lax.axis_index("gz") & 1
    for out, side in ((first, odd), (second, 1 - odd)):
        out[...] = ends[side]


def raise_scratch(count, dist, par, flags, occ):
    return [
        pltpu.VMEM(flags.shape, jnp.int32),
        [pltpu.VMEM((count, *a.shape[1:]), a.dtype) for a in (dist, par, occ)],
        pltpu.SemaphoreType.DMA,
        pltpu.SemaphoreType.DMA((3, count // READ)),
    ]


def raise_all(dist, par, flags, occ):
    depth, rows, cols = dist.shape
    message = jax.ShapeDtypeStruct((2 * rows, cols), jnp.float32)
    scratch = raise_scratch(depth, dist, par, flags, occ)
    return pl.pallas_call(
        raise_kernel,
        name="raise_all",
        out_shape=(
            jax.ShapeDtypeStruct((depth + 2, padded_rows(rows, cols), LANES), jnp.float32),
            message,
            message,
            jax.ShapeDtypeStruct((SUBLANES, cols), jnp.float32),
        ),
        in_specs=[HBM] * 4,
        out_specs=(VMEM,) * 4,
        scratch_shapes=scratch[:2] + [pltpu.VMEM((2, 2 * rows, cols), jnp.float32)] + scratch[2:],
        compiler_params=params(20),
        cost_estimate=cost(12),
    )(dist, par, flags, occ)


def sweep_once_kernel(start, count, rows, cols, field, once):
    depth = field.shape[0] - 2

    def sweep(z):
        def read(dz, at):
            return field[z + 1 + dz, pl.ds(at, SUBLANES), :]

        fill_pads(once, (z - start + 1,), rows, cols)
        for y in range(0, rows, SUBLANES):
            for column, tile in enumerate(swept_plane(read, rows, cols, y)):
                once[z - start + 1, pl.ds(row_of(column, y, rows), SUBLANES), :] = tile

    def body(group, _):
        for part in range(SWEEP_UNROLL):
            sweep(start + group * SWEEP_UNROLL + part)
        return 0

    for z in (start - 1, start + count):
        if 0 <= z < depth:
            sweep(z)
        else:
            once[z - start + 1] = jnp.full(once.shape[1:], FAR)
    lax.fori_loop(0, count // SWEEP_UNROLL, body, 0)


def sweep_once(field, start, count, rows, cols):
    return pl.pallas_call(
        functools.partial(sweep_once_kernel, start, count, rows, cols),
        out_shape=jax.ShapeDtypeStruct((count + 2, *field.shape[1:]), jnp.float32),
        in_specs=[VMEM],
        out_specs=VMEM,
        compiler_params=params(8),
        cost_estimate=cost(8),
    )(field)


def sweep_again_planes(once, first, count, tiles, slab):
    _, rows, cols = tiles.shape
    columns = range(cols // LANES)

    def body(group, _):
        for part in range(SWEEP_UNROLL):
            plane = first + group * SWEEP_UNROLL + part

            def read(dz, at):
                return once[plane + 1 + dz, pl.ds(at, SUBLANES), :]

            for y in range(0, rows, SUBLANES):
                for column, tile in enumerate(swept_plane(read, rows, cols, y)):
                    tiles[plane, pl.ds(y, SUBLANES), pl.ds(column * LANES, LANES)] = tile
                    at = plane * (rows * len(columns)) + column * rows + y
                    slab[pl.ds(pl.multiple_of(at, SUBLANES), SUBLANES), :] = tile
        return 0

    lax.fori_loop(0, count // SWEEP_UNROLL, body, 0)


def sweep_again_low_kernel(once, tiles, slab):
    sweep_again_planes(once, 0, tiles.shape[0], tiles, slab)


def sweep_again_high_kernel(once, low, out, slab, tiles, sem):
    half = low.shape[0]
    copies = [pltpu.make_async_copy(low, out.at[pl.ds(0, half)], sem.at[0])]
    copies[0].start()
    for step, first in enumerate(range(0, tiles.shape[0], CHUNK)):
        sweep_again_planes(once, first, CHUNK, tiles, slab)
        at = pl.ds(first, CHUNK)
        to = out.at[pl.ds(half + first, CHUNK)]
        cp = pltpu.make_async_copy(tiles.at[at], to, sem.at[step + 1])
        cp.start()
        copies.append(cp)
    for cp in copies:
        cp.wait()


def sweep_again_low(once, rows, cols):
    count = once.shape[0] - 2
    return pl.pallas_call(
        sweep_again_low_kernel,
        name="sweep_again_low",
        out_shape=(
            jax.ShapeDtypeStruct((count, rows, cols), jnp.float32),
            jax.ShapeDtypeStruct((count * rows * cols // LANES, LANES), jnp.float32),
        ),
        in_specs=[VMEM],
        out_specs=(VMEM, VMEM),
        compiler_params=params(4),
        cost_estimate=cost(8),
    )(once)


def sweep_again_high(once, low):
    count = once.shape[0] - 2
    _, rows, cols = low.shape
    return pl.pallas_call(
        sweep_again_high_kernel,
        name="sweep_again_high",
        out_shape=(
            jax.ShapeDtypeStruct((low.shape[0] + count, rows, cols), jnp.float32),
            jax.ShapeDtypeStruct((count * rows * cols // LANES, LANES), jnp.float32),
        ),
        in_specs=[VMEM, VMEM],
        out_specs=(HBM, VMEM),
        scratch_shapes=[
            pltpu.VMEM((count, rows, cols), jnp.float32),
            pltpu.SemaphoreType.DMA((count // CHUNK + 1,)),
        ],
        compiler_params=params(8),
        cost_estimate=cost(8),
    )(once, low)


def corners_kernel(first, second, counts, more, low, high, total):
    rows = first.shape[0] // 2
    odd = lax.axis_index("gz") & 1
    total[...] = counts[...] + more[...]
    low[...] = total[...]
    high[...] = total[...]
    for side in range(2):
        for out, row in ((low, 0), (high, rows - 1)):
            line = jnp.where(odd == side, first[pl.ds(row, 1), :], second[pl.ds(row, 1), :])
            out[pl.ds(side, 1), :] = line


def corners(first, second, counts, more):
    shape = jax.ShapeDtypeStruct(counts.shape, jnp.float32)
    return pl.pallas_call(
        corners_kernel,
        name="corners",
        out_shape=(shape,) * 3,
        in_specs=[VMEM] * 4,
        out_specs=(VMEM,) * 3,
        compiler_params=params(2),
        cost_estimate=cost(1),
    )(first, second, counts, more)


def patch_z_kernel(slabs, first, second, slab_low, slab_high, _, out, edges, planes, sem):
    depth, rows, cols = out.shape
    columns = range(cols // LANES)
    slab = lax.axis_index("gz")
    odd = slab & 1
    size = rows * len(columns)
    stores = []
    for side, own in enumerate((slab_low, slab_high)):
        missing = slab == (0, slabs - 1)[side]
        base = (0, own.shape[0] - 2 * size)[side]
        for away in range(2):
            plane = (away, 1 - away)[side]
            offered = (rows, 0)[away]
            for y in range(0, rows, SUBLANES):
                for column in columns:
                    x = pl.ds(column * LANES, LANES)
                    at = (pl.ds(offered + y, SUBLANES), x)
                    got = jnp.where(odd == side, first[at], second[at])
                    got = jnp.where(missing, FAR, got) + VOXEL
                    if away:
                        got = got + VOXEL
                    tile = own[pl.ds(base + plane * size + column * rows + y, SUBLANES), :]
                    planes[side, plane, pl.ds(y, SUBLANES), x] = jnp.minimum(tile, got)
        to = out.at[pl.ds((0, depth - 2)[side], 2)]
        cp = pltpu.make_async_copy(planes.at[side], to, sem.at[side])
        cp.start()
        stores.append(cp)
    for edge, row in enumerate((0, 1, rows - 2, rows - 1)):
        z = 0
        for own in (slab_low, slab_high):
            for base in range(0, own.shape[0], SUBLANES * size):
                for column in columns:
                    tile = own[pl.ds(base + column * rows + row, SUBLANES, stride=size), :]
                    edges[edge, pl.ds(z, SUBLANES), pl.ds(column * LANES, LANES)] = tile
                z += SUBLANES
        for side in range(2):
            for plane in range(2):
                at = pl.ds((0, depth - 2)[side] + plane, 1)
                edges[edge, at, :] = planes[side, plane, pl.ds(row, 1), :]
    for cp in stores:
        cp.wait()


def patch_z(first, second, slab_low, slab_high, out):
    depth, rows, cols = out.shape
    return pl.pallas_call(
        functools.partial(patch_z_kernel, lax.axis_size("gz")),
        name="patch_z",
        out_shape=(
            jax.ShapeDtypeStruct(out.shape, out.dtype),
            jax.ShapeDtypeStruct((4, depth, cols), jnp.float32),
        ),
        in_specs=[VMEM] * 4 + [HBM],
        out_specs=(HBM, VMEM),
        input_output_aliases={4: 0},
        scratch_shapes=[
            pltpu.VMEM((2, 2, rows, cols), jnp.float32),
            pltpu.SemaphoreType.DMA((2,)),
        ],
        compiler_params=params(4),
        cost_estimate=cost(1),
    )(first, second, slab_low, slab_high, out)


def merge_rows(away, edges, face, corner, missing, buf):
    reach = face[1 - away] + VOXEL
    if away:
        reach = reach + VOXEL
    buf[...] = jnp.minimum(edges[...], reach)
    if corner is not None:
        for end, z in enumerate((0, buf.shape[0] - 1)):
            offer = jnp.where(missing[end], FAR, corner[pl.ds(end, 1), :])
            line = pl.ds(z, 1)
            buf[line, :] = jnp.minimum(buf[line, :], offer + VOXEL + VOXEL)


def sides(rows):
    return (((0, 0), (1, 1)), ((rows - 1, 3), (rows - 2, 2)))


def patch_near_kernel(edges, near, _, out, buf, sem):
    odd = lax.axis_index("gy") & 1
    for side, places in enumerate(sides(out.shape[1])):

        @pl.when(odd == 1 - side)
        def _():
            copies = []
            for away, (row, edge) in enumerate(places):
                merge_rows(away, edges.at[edge], near, None, None, buf.at[away])
                cp = pltpu.make_async_copy(buf.at[away], out.at[:, row, :], sem.at[away])
                cp.start()
                copies.append(cp)
            for cp in copies:
                cp.wait()


def patch_far_kernel(
    scale, slabs, edges, near, far, clow, chigh, counts, _, out, share, buf, lines, sem
):
    depth, rows, _ = out.shape
    odd = lax.axis_index("gy") & 1
    slab = lax.axis_index("gz")
    missing = (slab == 0, slab == slabs - 1)
    corners = (clow, chigh)
    for side, places in enumerate(sides(rows)):

        @pl.when(odd == side)
        def _():
            copies = []
            for away, (row, edge) in enumerate(places):
                corner = None if away else corners[side]
                merge_rows(away, edges.at[edge], far, corner, missing, buf.at[away])
                cp = pltpu.make_async_copy(buf.at[away], out.at[:, row, :], sem.at[away])
                cp.start()
                copies.append(cp)
            row, edge = sides(rows)[1 - side][0]
            for end, z in enumerate((0, depth - 1)):
                line = pl.ds(z, 1)
                reach = jnp.minimum(edges[edge, line, :], near[1, line, :] + VOXEL)
                offer = jnp.where(missing[end], FAR, corners[1 - side][pl.ds(end, 1), :])
                lines[end] = jnp.minimum(reach, offer + VOXEL + VOXEL)
                cp = pltpu.make_async_copy(
                    lines.at[end], out.at[line, row, :], sem.at[2 + end]
                )
                cp.start()
                copies.append(cp)
            for cp in copies:
                cp.wait()

    x = pl.ds(0, LANES)
    both = (counts[:, x] + clow[:, x]).astype(jnp.int32)
    row = lax.broadcasted_iota(jnp.int32, both.shape, 0)
    both = jnp.where(row == 2, both, jnp.where(row == 3, both << COUNT_BITS, 0))
    count = jnp.sum(both, axis=0, keepdims=True)
    share[...] = count[:, :1].astype(jnp.float32) * jnp.float32(scale)


def patch_near(edges, near, out):
    depth, _, cols = out.shape
    return pl.pallas_call(
        patch_near_kernel,
        name="patch_near",
        out_shape=jax.ShapeDtypeStruct(out.shape, out.dtype),
        in_specs=[VMEM] * 2 + [HBM],
        out_specs=HBM,
        input_output_aliases={2: 0},
        scratch_shapes=[pltpu.VMEM((2, depth, cols), jnp.float32), pltpu.SemaphoreType.DMA((2,))],
        compiler_params=params(4),
        cost_estimate=cost(1),
    )(edges, near, out)


def patch_far(scale, edges, near, far, clow, chigh, counts, out):
    depth, _, cols = out.shape
    return pl.pallas_call(
        functools.partial(patch_far_kernel, scale, lax.axis_size("gz")),
        name="patch_far",
        out_shape=(
            jax.ShapeDtypeStruct(out.shape, out.dtype),
            jax.ShapeDtypeStruct((1, 1), jnp.float32),
        ),
        in_specs=[VMEM] * 6 + [HBM],
        out_specs=(HBM, VMEM),
        input_output_aliases={6: 0},
        scratch_shapes=[
            pltpu.VMEM((2, depth, cols), jnp.float32),
            pltpu.VMEM((2, 1, cols), jnp.float32),
            pltpu.SemaphoreType.DMA((4,)),
        ],
        compiler_params=params(4),
        cost_estimate=cost(1),
    )(edges, near, far, clow, chigh, counts, out)


def swapped(value, axis, partner):
    count = lax.axis_size(axis)
    return lax.ppermute(value, axis, [(i, partner(i) % count) for i in range(count)])


def after_odd(i):
    return i - 1 + 2 * (i % 2)


def shifted(value, axis, by):
    return swapped(value, axis, lambda i: i + by)


def on_device(distance, parent, removed, occupied):
    depth, rows, cols = distance.shape
    half = depth // 2
    slabs, columns = lax.axis_size("gz"), lax.axis_size("gy")
    tied = lax.optimization_barrier
    distance, parent, flags, occupied = (
        pltpu.with_memory_space_constraint(a, pltpu.HBM)
        for a in (distance, parent, removed.reshape(-1, LANES), occupied)
    )
    field, first, second, counts = raise_all(distance, parent, flags, occupied)
    face0 = faces(field, rows, cols, 0)
    near = swapped(face0, "gy", lambda i: i ^ 1)
    got_first = swapped(first, "gz", after_odd)
    got_second = swapped(second, "gz", lambda i: i ^ 1)
    face1 = faces(field, rows, cols, 1)
    once0 = sweep_once(field, 0, half, rows, cols)

    mask = columns // 2
    while mask > 1:
        more = swapped(counts, "gy", lambda i: i ^ mask)
        if mask == 4:
            more, face1 = tied((more, face1))
        if mask == 2:
            more, once0 = tied((more, once0))
        counts = counts + more
        mask //= 2
    face1, counts = tied((face1, counts))
    far = swapped(face1, "gy", after_odd)

    more = swapped(counts, "gz", after_odd)
    once1 = sweep_once(field, half, half, rows, cols)
    tiles, half0 = sweep_again_low(once0, rows, cols)
    more, tiles = tied((more, tiles))
    counts = counts + more
    more = swapped(counts, "gz", lambda i: i ^ 1)
    lowered, half1 = sweep_again_high(once1, tiles)
    more, half1 = tied((more, half1))
    clow, chigh, counts = corners(got_first, got_second, counts, more)
    from_low = shifted(chigh, "gy", 1)
    from_high = shifted(clow, "gy", -1)
    lowered, edges = patch_z(got_first, got_second, half0, half1, lowered)
    total = distance.size * slabs * columns
    lowered = patch_near(edges, near, lowered)
    lowered, share = patch_far(
        100.0 / total, edges, near, far, from_low, from_high, counts, lowered
    )
    return (lowered, share[0, 0])


def solution(mesh):
    slabs, columns = mesh.shape["gz"], mesh.shape["gy"]
    if slabs != 4 or columns < 8 or columns & (columns - 1):
        raise ValueError("unsupported mesh")
    placed = (P("gz", "gy", None), P("gz", "gy", None), P(), P("gz", "gy", None))
    return jax.shard_map(
        on_device, mesh=mesh, in_specs=placed, out_specs=(P("gz", "gy", None), P()), check_vma=False
    )
```

```python
import functools

import jax
import jax.numpy as jnp
from jax import lax
from jax.experimental import pallas as pl
from jax.experimental.pallas import tpu as pltpu
from jax.sharding import PartitionSpec as P


FAR = 1000000.0
VOXEL = 0.1
TRUNC = 2.0
LANES = 128
SUBLANES = 8
CHUNK = 8
READ = 8
AHEAD = 3
RAISE_UNROLL = 8
SWEEP_UNROLL = 8
MIB = 2**20

HBM = pl.BlockSpec(memory_space=pltpu.HBM)
VMEM = pl.BlockSpec(memory_space=pltpu.VMEM)

COUNT_BITS = 12


def params(mib):
    return pltpu.CompilerParams(vmem_limit_bytes=mib * MIB)


def cost(mib):
    return pl.CostEstimate(flops=0, bytes_accessed=mib * MIB, transcendentals=0)


def packed_table(flags_ref):
    bits = (flags_ref[...] == 1).astype(jnp.int32)
    bits = bits << lax.broadcasted_iota(jnp.int32, bits.shape, 0)
    words = jnp.sum(bits, axis=0, keepdims=True)
    return jnp.broadcast_to(words, (SUBLANES, LANES))


PICK = lax.GatherDimensionNumbers(
    offset_dims=(),
    collapsed_slice_dims=(1,),
    start_index_map=(1,),
    operand_batching_dims=(0,),
    start_indices_batching_dims=(0,),
)


def raise_tile(words, dist, par, occ):
    lane = par & (LANES - 1)
    word = lax.gather(words, lane[..., None], PICK, (1, 1), mode="promise_in_bounds")
    cleared = (word >> (par >> 7)) & (occ ^ 1)
    raised = jnp.where(occ == 1, 0.0, jnp.where(cleared == 1, TRUNC, dist))
    return raised, cleared


def swept_tiles(centers, others):
    lane = lax.broadcasted_iota(jnp.int32, (SUBLANES, LANES), 1)
    last = len(centers) - 1
    after = [pltpu.roll(c, 1, 1) for c in centers]
    before = [pltpu.roll(c, LANES - 1, 1) for c in centers]
    swept = []
    for i, center in enumerate(centers):
        left = jnp.where(lane == 0, after[i - 1] if i else FAR, after[i])
        right = jnp.where(lane == LANES - 1, before[i + 1] if i < last else FAR, before[i])
        nearest = jnp.minimum(left, right)
        for other in others[i]:
            nearest = jnp.minimum(nearest, other)
        swept.append(jnp.minimum(center, nearest + VOXEL))
    return swept


def padded_rows(rows, cols):
    return cols // LANES * (rows + SUBLANES) + SUBLANES


def row_of(column, row, rows):
    return column * (rows + SUBLANES) + SUBLANES + row


def fill_pads(ref, at, rows, cols):
    for column in range(cols // LANES + 1):
        first = row_of(column, -SUBLANES, rows)
        ref[(*at, pl.ds(first, SUBLANES), slice(None))] = jnp.full((SUBLANES, LANES), FAR)


def swept_plane(read, rows, cols, y, beside=(-1, 1)):
    firsts = [row_of(c, y, rows) for c in range(cols // LANES)]
    centers = [read(0, f) for f in firsts]
    others = [[read(dz, f) for dz in beside] + [read(0, f - 1), read(0, f + 1)] for f in firsts]
    return swept_tiles(centers, others)


def face_tiles(field, rows, cols, row, inward, z):
    planes, height, _ = field.shape
    lines = field.reshape(planes * height, LANES)
    columns = range(cols // LANES)

    def read(column, y, dz=0):
        first = (z + 1 + dz) * height + row_of(column, y, rows)
        return lines[pl.ds(first, SUBLANES, stride=height), :]

    ends = [read(c, row) for c in columns]
    others = [(read(c, row, -1), read(c, row, 1), read(c, inward)) for c in columns]
    return ends, swept_tiles(ends, others)


def write_faces(field, rows, cols, top, start, out):
    def body(group, _):
        at = pl.ds(pl.multiple_of(group * SUBLANES, SUBLANES), SUBLANES)

        def write(row, inward):
            ends, swept = face_tiles(field, rows, cols, row, inward, start + group * SUBLANES)
            for column, (end, tile) in enumerate(zip(ends, swept)):
                x = pl.ds(column * LANES, LANES)
                out[0, at, x] = end
                out[1, at, x] = tile

        pl.when(top)(lambda: write(rows - 1, rows - 2))
        pl.when(jnp.logical_not(top))(lambda: write(0, 1))
        return 0

    lax.fori_loop(0, out.shape[1] // SUBLANES, body, 0)


def faces_kernel(rows, cols, toward_odd, field, out):
    odd = lax.axis_index("gy") & 1
    write_faces(field, rows, cols, odd == toward_odd, 0, out)


def faces(field, rows, cols, toward_odd):
    return pl.pallas_call(
        functools.partial(faces_kernel, rows, cols, toward_odd),
        out_shape=jax.ShapeDtypeStruct((2, field.shape[0] - 2, cols), jnp.float32),
        in_specs=[VMEM],
        out_specs=VMEM,
        compiler_params=params(4),
        cost_estimate=cost(2),
    )(field)


def raise_planes(start, count, dist, par, flags_at, occ, field, flags, buf, fsem, sem):
    _, rows, cols = dist.shape
    columns = range(cols // LANES)
    chunks = count // READ

    def reads(chunk):
        source, target = pl.ds(start + chunk * READ, READ), pl.ds(chunk * READ, READ)
        return [
            pltpu.make_async_copy(src.at[source], dst.at[target], sem.at[which, chunk])
            for which, (src, dst) in enumerate(zip((dist, par, occ), buf))
        ]

    table_in = pltpu.make_async_copy(flags_at, flags, fsem)
    table_in.start()
    for chunk in range(min(AHEAD, chunks)):
        for cp in reads(chunk):
            cp.start()
    for z in (0, field.shape[0] - 1):
        if start < z <= start + count + 1 or z == start == 0:
            field[z] = jnp.full(field.shape[1:], FAR)
    table_in.wait()
    table = packed_table(flags)

    def body(chunk, acc):
        @pl.when(chunk + AHEAD < chunks)
        def _():
            for cp in reads(chunk + AHEAD):
                cp.start()

        for cp in reads(chunk):
            cp.wait()

        def planes(group, acc):
            for part in range(RAISE_UNROLL):
                z = chunk * READ + group * RAISE_UNROLL + part
                fill_pads(field, (start + z + 1,), rows, cols)
                for y in range(0, rows, SUBLANES):
                    for column in columns:
                        at = (z, pl.ds(y, SUBLANES), pl.ds(column * LANES, LANES))
                        tile, cleared = raise_tile(table, *(b[at] for b in buf))
                        to = pl.ds(row_of(column, y, rows), SUBLANES)
                        field[start + z + 1, to, :] = tile
                        acc[part] = acc[part] + cleared
            return acc

        return lax.fori_loop(0, READ // RAISE_UNROLL, planes, acc)

    zeros = jnp.zeros((SUBLANES, LANES), jnp.int32)
    parts = lax.fori_loop(0, chunks, body, [zeros] * RAISE_UNROLL)
    return sum(parts[1:], parts[0])


def keep_end(field, z, inward, rows, cols, out):
    def read(dz, at):
        return field[z + 1 + dz, pl.ds(at, SUBLANES), :]

    for y in range(0, rows, SUBLANES):
        swept = swept_plane(read, rows, cols, y, (inward,))
        for column in range(cols // LANES):
            x = pl.ds(column * LANES, LANES)
            out[pl.ds(y, SUBLANES), x] = read(0, row_of(column, y, rows))
            out[pl.ds(rows + y, SUBLANES), x] = swept[column]


def raise_kernel(dist, par, flags_at, occ, field, first, second, counts, flags, buf, ends, fsem, sem):
    depth, rows, cols = dist.shape
    total = raise_planes(0, depth, dist, par, flags_at, occ, field, flags, buf, fsem, sem)
    keep_end(field, 0, 1, rows, cols, ends.at[0])
    keep_end(field, depth - 1, -1, rows, cols, ends.at[1])
    count = jnp.sum(total)
    row = lax.broadcasted_iota(jnp.int32, (SUBLANES, cols), 0)
    small = (count & (2**COUNT_BITS - 1)).astype(jnp.float32)
    large = (count >> COUNT_BITS).astype(jnp.float32)
    counts[...] = jnp.where(row == 2, small, jnp.where(row == 3, large, 0.0))
    odd = lax.axis_index("gz") & 1
    for out, side in ((first, odd), (second, 1 - odd)):
        out[...] = ends[side]


def raise_scratch(count, dist, par, flags, occ):
    return [
        pltpu.VMEM(flags.shape, jnp.int32),
        [pltpu.VMEM((count, *a.shape[1:]), a.dtype) for a in (dist, par, occ)],
        pltpu.SemaphoreType.DMA,
        pltpu.SemaphoreType.DMA((3, count // READ)),
    ]


def raise_all(dist, par, flags, occ):
    depth, rows, cols = dist.shape
    message = jax.ShapeDtypeStruct((2 * rows, cols), jnp.float32)
    scratch = raise_scratch(depth, dist, par, flags, occ)
    return pl.pallas_call(
        raise_kernel,
        name="raise_all",
        out_shape=(
            jax.ShapeDtypeStruct((depth + 2, padded_rows(rows, cols), LANES), jnp.float32),
            message,
            message,
            jax.ShapeDtypeStruct((SUBLANES, cols), jnp.float32),
        ),
        in_specs=[HBM] * 4,
        out_specs=(VMEM,) * 4,
        scratch_shapes=scratch[:2] + [pltpu.VMEM((2, 2 * rows, cols), jnp.float32)] + scratch[2:],
        compiler_params=params(20),
        cost_estimate=cost(12),
    )(dist, par, flags, occ)


def sweep_once_kernel(start, count, rows, cols, field, once):
    depth = field.shape[0] - 2

    def sweep(z):
        def read(dz, at):
            return field[z + 1 + dz, pl.ds(at, SUBLANES), :]

        fill_pads(once, (z - start + 1,), rows, cols)
        for y in range(0, rows, SUBLANES):
            for column, tile in enumerate(swept_plane(read, rows, cols, y)):
                once[z - start + 1, pl.ds(row_of(column, y, rows), SUBLANES), :] = tile

    def body(group, _):
        for part in range(SWEEP_UNROLL):
            sweep(start + group * SWEEP_UNROLL + part)
        return 0

    for z in (start - 1, start + count):
        if 0 <= z < depth:
            sweep(z)
        else:
            once[z - start + 1] = jnp.full(once.shape[1:], FAR)
    lax.fori_loop(0, count // SWEEP_UNROLL, body, 0)


def sweep_once(field, start, count, rows, cols):
    return pl.pallas_call(
        functools.partial(sweep_once_kernel, start, count, rows, cols),
        out_shape=jax.ShapeDtypeStruct((count + 2, *field.shape[1:]), jnp.float32),
        in_specs=[VMEM],
        out_specs=VMEM,
        compiler_params=params(8),
        cost_estimate=cost(8),
    )(field)


def sweep_again_planes(once, first, count, tiles, slab):
    _, rows, cols = tiles.shape
    columns = range(cols // LANES)

    def body(group, _):
        for part in range(SWEEP_UNROLL):
            plane = first + group * SWEEP_UNROLL + part

            def read(dz, at):
                return once[plane + 1 + dz, pl.ds(at, SUBLANES), :]

            for y in range(0, rows, SUBLANES):
                for column, tile in enumerate(swept_plane(read, rows, cols, y)):
                    tiles[plane, pl.ds(y, SUBLANES), pl.ds(column * LANES, LANES)] = tile
                    at = plane * (rows * len(columns)) + column * rows + y
                    slab[pl.ds(pl.multiple_of(at, SUBLANES), SUBLANES), :] = tile
        return 0

    lax.fori_loop(0, count // SWEEP_UNROLL, body, 0)


def sweep_again_low_kernel(once, tiles, slab):
    sweep_again_planes(once, 0, tiles.shape[0], tiles, slab)


def sweep_again_high_kernel(once, low, out, slab, tiles, sem):
    half = low.shape[0]
    copies = [pltpu.make_async_copy(low, out.at[pl.ds(0, half)], sem.at[0])]
    copies[0].start()
    for step, first in enumerate(range(0, tiles.shape[0], CHUNK)):
        sweep_again_planes(once, first, CHUNK, tiles, slab)
        at = pl.ds(first, CHUNK)
        to = out.at[pl.ds(half + first, CHUNK)]
        cp = pltpu.make_async_copy(tiles.at[at], to, sem.at[step + 1])
        cp.start()
        copies.append(cp)
    for cp in copies:
        cp.wait()


def sweep_again_low(once, rows, cols):
    count = once.shape[0] - 2
    return pl.pallas_call(
        sweep_again_low_kernel,
        name="sweep_again_low",
        out_shape=(
            jax.ShapeDtypeStruct((count, rows, cols), jnp.float32),
            jax.ShapeDtypeStruct((count * rows * cols // LANES, LANES), jnp.float32),
        ),
        in_specs=[VMEM],
        out_specs=(VMEM, VMEM),
        compiler_params=params(4),
        cost_estimate=cost(8),
    )(once)


def sweep_again_high(once, low):
    count = once.shape[0] - 2
    _, rows, cols = low.shape
    return pl.pallas_call(
        sweep_again_high_kernel,
        name="sweep_again_high",
        out_shape=(
            jax.ShapeDtypeStruct((low.shape[0] + count, rows, cols), jnp.float32),
            jax.ShapeDtypeStruct((count * rows * cols // LANES, LANES), jnp.float32),
        ),
        in_specs=[VMEM, VMEM],
        out_specs=(HBM, VMEM),
        scratch_shapes=[
            pltpu.VMEM((count, rows, cols), jnp.float32),
            pltpu.SemaphoreType.DMA((count // CHUNK + 1,)),
        ],
        compiler_params=params(8),
        cost_estimate=cost(8),
    )(once, low)


def corners_kernel(first, second, counts, more, low, high, total):
    rows = first.shape[0] // 2
    odd = lax.axis_index("gz") & 1
    total[...] = counts[...] + more[...]
    low[...] = total[...]
    high[...] = total[...]
    for side in range(2):
        for out, row in ((low, 0), (high, rows - 1)):
            line = jnp.where(odd == side, first[pl.ds(row, 1), :], second[pl.ds(row, 1), :])
            out[pl.ds(side, 1), :] = line


def corners(first, second, counts, more):
    shape = jax.ShapeDtypeStruct(counts.shape, jnp.float32)
    return pl.pallas_call(
        corners_kernel,
        name="corners",
        out_shape=(shape,) * 3,
        in_specs=[VMEM] * 4,
        out_specs=(VMEM,) * 3,
        compiler_params=params(2),
        cost_estimate=cost(1),
    )(first, second, counts, more)


def patch_z_kernel(slabs, first, second, slab_low, slab_high, _, out, edges, planes, sem):
    depth, rows, cols = out.shape
    columns = range(cols // LANES)
    slab = lax.axis_index("gz")
    odd = slab & 1
    size = rows * len(columns)
    stores = []
    for side, own in enumerate((slab_low, slab_high)):
        missing = slab == (0, slabs - 1)[side]
        base = (0, own.shape[0] - 2 * size)[side]
        for away in range(2):
            plane = (away, 1 - away)[side]
            offered = (rows, 0)[away]
            for y in range(0, rows, SUBLANES):
                for column in columns:
                    x = pl.ds(column * LANES, LANES)
                    at = (pl.ds(offered + y, SUBLANES), x)
                    got = jnp.where(odd == side, first[at], second[at])
                    got = jnp.where(missing, FAR, got) + VOXEL
                    if away:
                        got = got + VOXEL
                    tile = own[pl.ds(base + plane * size + column * rows + y, SUBLANES), :]
                    planes[side, plane, pl.ds(y, SUBLANES), x] = jnp.minimum(tile, got)
        to = out.at[pl.ds((0, depth - 2)[side], 2)]
        cp = pltpu.make_async_copy(planes.at[side], to, sem.at[side])
        cp.start()
        stores.append(cp)
    for edge, row in enumerate((0, 1, rows - 2, rows - 1)):
        z = 0
        for own in (slab_low, slab_high):
            for base in range(0, own.shape[0], SUBLANES * size):
                for column in columns:
                    tile = own[pl.ds(base + column * rows + row, SUBLANES, stride=size), :]
                    edges[edge, pl.ds(z, SUBLANES), pl.ds(column * LANES, LANES)] = tile
                z += SUBLANES
        for side in range(2):
            for plane in range(2):
                at = pl.ds((0, depth - 2)[side] + plane, 1)
                edges[edge, at, :] = planes[side, plane, pl.ds(row, 1), :]
    for cp in stores:
        cp.wait()


def patch_z(first, second, slab_low, slab_high, out):
    depth, rows, cols = out.shape
    return pl.pallas_call(
        functools.partial(patch_z_kernel, lax.axis_size("gz")),
        name="patch_z",
        out_shape=(
            jax.ShapeDtypeStruct(out.shape, out.dtype),
            jax.ShapeDtypeStruct((4, depth, cols), jnp.float32),
        ),
        in_specs=[VMEM] * 4 + [HBM],
        out_specs=(HBM, VMEM),
        input_output_aliases={4: 0},
        scratch_shapes=[
            pltpu.VMEM((2, 2, rows, cols), jnp.float32),
            pltpu.SemaphoreType.DMA((2,)),
        ],
        compiler_params=params(4),
        cost_estimate=cost(1),
    )(first, second, slab_low, slab_high, out)


def merge_rows(away, edges, face, corner, missing, buf):
    reach = face[1 - away] + VOXEL
    if away:
        reach = reach + VOXEL
    buf[...] = jnp.minimum(edges[...], reach)
    if corner is not None:
        for end, z in enumerate((0, buf.shape[0] - 1)):
            offer = jnp.where(missing[end], FAR, corner[pl.ds(end, 1), :])
            line = pl.ds(z, 1)
            buf[line, :] = jnp.minimum(buf[line, :], offer + VOXEL + VOXEL)


def sides(rows):
    return (((0, 0), (1, 1)), ((rows - 1, 3), (rows - 2, 2)))


def patch_far_kernel(
    scale, slabs, edges, near, far, clow, chigh, counts, _, out, share, buf, sem
):
    _, rows, _ = out.shape
    odd = lax.axis_index("gy") & 1
    slab = lax.axis_index("gz")
    missing = (slab == 0, slab == slabs - 1)
    corners = (clow, chigh)
    for side in range(2):

        @pl.when(odd == side)
        def _():
            copies = []
            for face, end in ((near, 1 - side), (far, side)):
                for away, (row, edge) in enumerate(sides(rows)[end]):
                    corner = None if away else corners[end]
                    at = len(copies)
                    merge_rows(away, edges.at[edge], face, corner, missing, buf.at[at])
                    cp = pltpu.make_async_copy(buf.at[at], out.at[:, row, :], sem.at[at])
                    cp.start()
                    copies.append(cp)
            for cp in copies:
                cp.wait()

    x = pl.ds(0, LANES)
    both = (counts[:, x] + clow[:, x]).astype(jnp.int32)
    row = lax.broadcasted_iota(jnp.int32, both.shape, 0)
    both = jnp.where(row == 2, both, jnp.where(row == 3, both << COUNT_BITS, 0))
    count = jnp.sum(both, axis=0, keepdims=True)
    share[...] = count[:, :1].astype(jnp.float32) * jnp.float32(scale)


def patch_far(scale, edges, near, far, clow, chigh, counts, out):
    depth, _, cols = out.shape
    return pl.pallas_call(
        functools.partial(patch_far_kernel, scale, lax.axis_size("gz")),
        name="patch_far",
        out_shape=(
            jax.ShapeDtypeStruct(out.shape, out.dtype),
            jax.ShapeDtypeStruct((1, 1), jnp.float32),
        ),
        in_specs=[VMEM] * 6 + [HBM],
        out_specs=(HBM, VMEM),
        input_output_aliases={6: 0},
        scratch_shapes=[
            pltpu.VMEM((4, depth, cols), jnp.float32),
            pltpu.SemaphoreType.DMA((4,)),
        ],
        compiler_params=params(4),
        cost_estimate=cost(1),
    )(edges, near, far, clow, chigh, counts, out)


def swapped(value, axis, partner):
    count = lax.axis_size(axis)
    return lax.ppermute(value, axis, [(i, partner(i) % count) for i in range(count)])


def after_odd(i):
    return i - 1 + 2 * (i % 2)


def shifted(value, axis, by):
    return swapped(value, axis, lambda i: i + by)


def on_device(distance, parent, removed, occupied):
    depth, rows, cols = distance.shape
    half = depth // 2
    slabs, columns = lax.axis_size("gz"), lax.axis_size("gy")
    tied = lax.optimization_barrier
    distance, parent, flags, occupied = (
        pltpu.with_memory_space_constraint(a, pltpu.HBM)
        for a in (distance, parent, removed.reshape(-1, LANES), occupied)
    )
    field, first, second, counts = raise_all(distance, parent, flags, occupied)
    face0 = faces(field, rows, cols, 0)
    near = swapped(face0, "gy", lambda i: i ^ 1)
    got_first = swapped(first, "gz", after_odd)
    got_second = swapped(second, "gz", lambda i: i ^ 1)
    face1 = faces(field, rows, cols, 1)
    once0 = sweep_once(field, 0, half, rows, cols)

    mask = columns // 2
    while mask > 1:
        more = swapped(counts, "gy", lambda i: i ^ mask)
        if mask == 4:
            more, face1 = tied((more, face1))
        if mask == 2:
            more, once0 = tied((more, once0))
        counts = counts + more
        mask //= 2
    face1, counts = tied((face1, counts))
    far = swapped(face1, "gy", after_odd)

    more = swapped(counts, "gz", after_odd)
    once1 = sweep_once(field, half, half, rows, cols)
    tiles, half0 = sweep_again_low(once0, rows, cols)
    more, tiles = tied((more, tiles))
    counts = counts + more
    more = swapped(counts, "gz", lambda i: i ^ 1)
    lowered, half1 = sweep_again_high(once1, tiles)
    more, half1 = tied((more, half1))
    clow, chigh, counts = corners(got_first, got_second, counts, more)
    from_low = shifted(chigh, "gy", 1)
    from_high = shifted(clow, "gy", -1)
    lowered, edges = patch_z(got_first, got_second, half0, half1, lowered)
    total = distance.size * slabs * columns
    lowered, share = patch_far(
        100.0 / total, edges, near, far, from_low, from_high, counts, lowered
    )
    return (lowered, share[0, 0])


def solution(mesh):
    slabs, columns = mesh.shape["gz"], mesh.shape["gy"]
    if slabs != 4 or columns < 8 or columns & (columns - 1):
        raise ValueError("unsupported mesh")
    placed = (P("gz", "gy", None), P("gz", "gy", None), P(), P("gz", "gy", None))
    return jax.shard_map(
        on_device, mesh=mesh, in_specs=placed, out_specs=(P("gz", "gy", None), P()), check_vma=False
    )
```
